512 devices in a mesh: seq: 128 (over x, z, core), head: 4 (over y).
Axes of the slice: x: 4, y: 4, z: 16, core: 2. Of those that a mesh axis runs over, the one named last changes fastest.
Arguments:
- queries: bfloat16 [16384, 2048], P('seq', 'head'), may hold values from -5 to 5
- key_rows: bfloat16 [16384, 2048], P('seq', 'head'), may hold values from -5 to 5
- value_rows: bfloat16 [16384, 2048], P('seq', 'head'), may hold values from -6 to 6
- out_weight: bfloat16 [2048, 2048], P('head'), may hold values from -0.125 to 0.125
- grad_out: bfloat16 [16384, 2048], P('seq', 'head'), may hold values from -6 to 6
- pair_offsets: int32 [16], replicated, may hold values from 0 to 1
- far_head_offsets: int32 [16], replicated, may hold values from 0 to 31
Outputs:
- layer_out: bfloat16 [16384, 2048], P('seq')
- grad_queries: bfloat16 [16384, 2048], P('seq', 'head')
- grad_keys: bfloat16 [16384, 2048], P('seq', 'head')
- grad_values: bfloat16 [16384, 2048], P('seq', 'head')
The draws below stay inside these ranges and needn't reach their ends.
All inputs are finite; a program needn't handle non-finite values.
Results may differ from the reference program's by a relative error of at most 0.009.
Values may be sent and summed in bfloat16 or wider, within the bound.
A program may use at most 64 MiB of HBM per device.

```python
import jax
import jax.numpy as jnp
from jax import lax

D = 2048
ATTENTION_HEADS = 16
HEAD_DIM = 128
TOKENS = 16384
SELECTED = 512
FAR_DILATION = 32
N_HEAD = 4


def drawn_draws(key):
    base_key = jax.random.fold_in(key, 7101)
    query_key, keys_key = jax.random.split(base_key, 2)
    queries = jax.random.truncated_normal(query_key, -4.5, 4.5, (TOKENS, D), jnp.float32)
    key_rows = jax.random.truncated_normal(keys_key, -4.5, 4.5, (TOKENS, D), jnp.float32)
    return (queries, key_rows)


def draw_queries(key, part):
    return drawn_draws(key)[0].astype(jnp.bfloat16)


def draw_key_rows(key, part):
    return drawn_draws(key)[1].astype(jnp.bfloat16)


def plant(values, own_key, smallest, high):
    index_at = [jax.random.randint(jax.random.fold_in(own_key, axis), (), 0, length) for axis, length in enumerate(values.shape)]
    longest = values.shape.index(max(values.shape))
    next_to = index_at[:longest] + [(index_at[longest] + 1) % values.shape[longest]] + index_at[longest + 1:]
    return values.at[tuple(index_at)].set(smallest).at[tuple(next_to)].set(high)


def level_of(own_key, dims, pieces, smallest, top_value):
    loudness = 1.0
    for dim, shards_of in pieces:
        steps = jax.random.uniform(jax.random.fold_in(jax.random.fold_in(own_key, 6), dim), (shards_of,), jnp.float32, smallest / len(pieces), top_value / len(pieces))
        loudness = loudness * jnp.repeat(jnp.exp(steps), dims[dim] // shards_of).reshape((-1,) + (1,) * (len(dims) - 1 - dim))
    return loudness


def noise(key, extent, width, limit, shards=(), dtype=jnp.bfloat16):
    values = jax.random.normal(key, extent, jnp.float32) * width
    if len(shards) > 0:
        values = level_of(key, extent, shards, -0.22, 0.18) * values
    return jnp.clip(values, min=-limit, max=limit).astype(dtype)


def setup_inputs(seed: int = 0) -> dict:
    splits = jax.random.split(jax.random.key(seed), 8)
    queries = draw_queries(jax.random.fold_in(splits[7], 71), 0)
    key_rows = draw_key_rows(jax.random.fold_in(splits[7], 71), 0)
    value_rows = noise(splits[2], (TOKENS, D), 1.0, 6.0, ((0, 128), (1, 4)))
    out_weight = noise(splits[3], (D, D), D ** -0.5, 0.125, ((0, 4),))
    grad_out = noise(splits[4], (TOKENS, D), 1.0, 6.0, ((0, 128), (1, 4)))
    pair_offsets = plant(jax.random.randint(splits[5], (ATTENTION_HEADS,), 0, 2), jax.random.fold_in(splits[5], 1), 0, 1).astype(jnp.int32)
    far_head_offsets = plant(jax.random.randint(splits[6], (ATTENTION_HEADS,), 0, FAR_DILATION), jax.random.fold_in(splits[6], 1), 0, FAR_DILATION - 1).astype(jnp.int32)
    return dict(queries=queries, key_rows=key_rows, value_rows=value_rows, out_weight=out_weight, grad_out=grad_out, pair_offsets=pair_offsets, far_head_offsets=far_head_offsets)


masked_score = -1.0e30


def to_float(tensor):
    return tensor.astype(jnp.float32)


def round_trip(tensor):
    return lax.optimization_barrier(tensor.astype(jnp.bfloat16)).astype(jnp.float32)


def select(tensor, token_stride, start_offset):
    layout = (tensor.shape[0] // (SELECTED * token_stride), SELECTED, token_stride) + tensor.shape[1:]
    return lax.dynamic_index_in_dim(tensor.reshape(layout), start_offset, axis=2, keepdims=False)


def spread(entries, token_stride, start_offset, filler):
    layout = entries.shape[:2] + (token_stride,) + entries.shape[2:]
    lane_ids = lax.broadcasted_iota(jnp.int32, layout, 2)
    placed = jnp.where(lane_ids == start_offset, jnp.expand_dims(entries, 2), filler)
    return placed.reshape((layout[0] * layout[1] * token_stride,) + entries.shape[2:])


def causal_scores(query_part, key_part):
    number = query_part.shape[1]
    scores = jnp.einsum("sid,sjd->sij", to_float(query_part), to_float(key_part)) * (HEAD_DIM ** -0.5)
    row_ids = lax.broadcasted_iota(jnp.int32, (number, number), 0)
    col_ids = lax.broadcasted_iota(jnp.int32, (number, number), 1)
    return jnp.where(row_ids >= col_ids, scores, masked_score)


def head_forward(operands):
    head_query, head_key, head_value, pair_branch_shift, far_branch_shift = operands
    branches = []
    for token_stride, start_offset in ((1, 0), (2, pair_branch_shift), (FAR_DILATION, far_branch_shift)):
        scores = causal_scores(select(head_query, token_stride, start_offset), select(head_key, token_stride, start_offset))
        branch_max = jnp.max(scores, axis=-1)
        weights = jnp.exp(scores - branch_max[..., None])
        branch_sum = jnp.sum(weights, axis=-1)
        numerator = jnp.einsum("sij,sjd->sid", round_trip(weights), to_float(select(head_value, token_stride, start_offset)))
        branches.append((spread(branch_max, token_stride, start_offset, masked_score), spread(branch_sum, token_stride, start_offset, 0.0), spread(numerator, token_stride, start_offset, 0.0)))
    row_max = jnp.maximum(jnp.maximum(branches[0][0], branches[1][0]), branches[2][0])
    row_sum = jnp.zeros_like(row_max)
    numerator = jnp.zeros_like(branches[0][2])
    for branch in branches:
        rescale = jnp.exp(branch[0] - row_max)
        row_sum = row_sum + branch[1] * rescale
        numerator = numerator + branch[2] * rescale[:, None]
    return numerator / row_sum[:, None], row_max, row_sum


def head_backward(operands):
    head_query, head_key, head_value, head_grad, head_out, row_max, row_sum, pair_branch_shift, far_branch_shift = operands
    factor = HEAD_DIM ** -0.5
    row_delta = jnp.sum(to_float(head_grad) * head_out, axis=-1)
    query_grad = jnp.zeros_like(head_out)
    key_grad = jnp.zeros_like(head_out)
    value_grad = jnp.zeros_like(head_out)
    for token_stride, start_offset in ((1, 0), (2, pair_branch_shift), (FAR_DILATION, far_branch_shift)):
        query_part = select(head_query, token_stride, start_offset)
        key_part = select(head_key, token_stride, start_offset)
        value_part = select(head_value, token_stride, start_offset)
        grad_part = select(head_grad, token_stride, start_offset)
        scores = causal_scores(query_part, key_part)
        probability = jnp.exp(scores - select(row_max, token_stride, start_offset)[..., None]) / select(row_sum, token_stride, start_offset)[..., None]
        branch_dv = jnp.einsum("sij,sid->sjd", round_trip(probability), to_float(grad_part))
        prob_grad = jnp.einsum("sid,sjd->sij", to_float(grad_part), to_float(value_part))
        score_grad = round_trip(probability * (prob_grad - select(row_delta, token_stride, start_offset)[..., None]))
        branch_dq = jnp.einsum("sij,sjd->sid", score_grad, to_float(key_part)) * factor
        branch_dk = jnp.einsum("sij,sid->sjd", score_grad, to_float(query_part)) * factor
        query_grad = query_grad + spread(branch_dq, token_stride, start_offset, 0.0)
        key_grad = key_grad + spread(branch_dk, token_stride, start_offset, 0.0)
        value_grad = value_grad + spread(branch_dv, token_stride, start_offset, 0.0)
    return query_grad, key_grad, value_grad


def by_head(tensor):
    return tensor.reshape(TOKENS, ATTENTION_HEADS, HEAD_DIM).transpose(1, 0, 2)


def by_token(tensor):
    return tensor.transpose(1, 0, 2).reshape(TOKENS, ATTENTION_HEADS * HEAD_DIM)


def reference(queries, key_rows, value_rows, out_weight, grad_out, pair_offsets, far_head_offsets):
    head_queries = by_head(queries)
    head_keys = by_head(key_rows)
    head_values = by_head(value_rows)
    head_out, row_max, row_sum = lax.map(head_forward, (head_queries, head_keys, head_values, pair_offsets, far_head_offsets))
    attended = by_token(head_out).astype(jnp.bfloat16)
    slab_width = D // N_HEAD
    layer_sum = jnp.zeros((TOKENS, D), jnp.float32)
    for part_index in range(N_HEAD):
        lower = part_index * slab_width
        partial_out = jnp.dot(attended[:, lower:lower + slab_width], out_weight[lower:lower + slab_width], preferred_element_type=jnp.float32)
        layer_sum = layer_sum + round_trip(partial_out)
    layer_out = layer_sum.astype(jnp.bfloat16)
    grad_attended = jnp.dot(grad_out, out_weight.T, preferred_element_type=jnp.float32).astype(jnp.bfloat16)
    query_grad, key_grad, value_grad = lax.map(head_backward, (head_queries, head_keys, head_values, by_head(grad_attended), head_out, row_max, row_sum, pair_offsets, far_head_offsets))
    return (layer_out, by_token(query_grad).astype(jnp.bfloat16), by_token(key_grad).astype(jnp.bfloat16), by_token(value_grad).astype(jnp.bfloat16))
```

```python
import jax
import jax.numpy as jnp
from jax import lax
from jax.experimental import pallas as pl
from jax.experimental.pallas import tpu as pltpu
from jax.sharding import PartitionSpec as P

MESH = pl.DeviceIdType.MESH
NEG = -1.0e30
F32 = jnp.float32
BF = jnp.bfloat16
FACTOR = 128 ** (-0.5)
ROWS = 128
BOTH = 256
ZC = 16
FAR = 32

PQKV, PGRAD, POUT, PDQ = 0, 3, 4, 5
LOC, PAIR, YG, RS, AG = 6, 10, 18, 21, 24
STL, STP = 27, 28
R1, R2 = 30, 32
FA, FB = 34, 36
NSEM = 38


def nt(a, b):
    return lax.dot_general(a, b, (((1,), (1,)), ((), ())), preferred_element_type=F32)


def nn(a, b):
    return jnp.dot(a, b, preferred_element_type=F32)


def exact(a, b):
    return lax.dot_general(
        a, b, (((1,), (0,)), ((), ())), precision=lax.Precision.HIGHEST, preferred_element_type=F32
    )


def iota(shape, dim):
    return lax.broadcasted_iota(jnp.int32, shape, dim)


def pick_far(x, off):
    rows = iota(x.shape, 0)
    kept = jnp.where((rows & (FAR - 1)) == off, x, 0.0)
    return jnp.sum(kept.reshape(BOTH // FAR, FAR, 128), axis=1)


def repeat_far(x):
    return jnp.broadcast_to(x[:, None, :], (BOTH // FAR, FAR, 128)).reshape(BOTH, 128)


def kernel(
    q, k, v, w, go, po, fo,
    lo, dq, dk, dv,
    QC, KC, VC, GC, LB, PB, PSND, GOA, GOUT,
    MR, LR, ACC, DQ, DK, DV, STR, STPS, LSR, PSR,
    FS, FS2, FG, FG2, R1S, R2S, FR1, FR2,
    OB, ORC, RSS, RSR, AGS, AGR, DSND, DRCV,
    ss, rs,
):
    t = lax.axis_index("seq")
    y = lax.axis_index("head")
    c = t % 2
    chip = t // 2
    odd = chip % 2
    g = chip % 4
    upper = g // 2
    mate = t + 1 - 2 * c
    near = chip + 1 - 2 * odd
    other = chip - g + 2 - 2 * upper
    nchip = lax.axis_size("seq") // 2
    hub_turn = (chip // ZC) % 2
    is_hub = jnp.logical_and(chip % ZC == 8, (chip // ZC) // 2 == c)

    def hub_chip(i):
        return ZC * (2 * c + i) + 8

    def rc(src, dst, i, j, dev):
        return pltpu.make_async_remote_copy(
            src_ref=src, dst_ref=dst, send_sem=ss.at[i], recv_sem=rs.at[j],
            device_id=dev, device_id_type=MESH,
        )

    bar = pltpu.get_barrier_semaphore()

    def sig(dev):
        pl.semaphore_signal(bar, inc=1, device_id=dev, device_id_type=MESH)

    for i in range(2):
        @pl.when(chip != hub_chip(i))
        def _(i=i):
            sig((2 * hub_chip(i) + c, y))

    @pl.when(is_hub)
    def _():
        @pl.loop(0, nchip)
        def _(n):
            @pl.when(n != chip)
            def _():
                sig((2 * n + c, y))

    for d in range(1, 4):
        sig((t, (y + d) % 4))
    sig((mate, y))
    for s in range(2):
        sig((2 * near + s, y))
        for d in range(2):
            sig((2 * (other + d) + s, y))

    off_p = [po[4 * y + 2 * c + i] for i in range(2)]
    off_f = [fo[4 * y + 2 * c + i] for i in range(2)]
    lane = pl.ds(pl.multiple_of(256 * c, 256), 256)
    mine = pl.ds(pl.multiple_of(ROWS * c, ROWS), ROWS)
    theirs = pl.ds(pl.multiple_of(ROWS * (1 - c), ROWS), ROWS)
    mate_lane = pl.ds(pl.multiple_of(256 * (1 - c), 256), 256)

    def one_hot(off):
        return jnp.where(
            iota((64, ROWS), 1) == 2 * iota((64, ROWS), 0) + off, 1.0, 0.0
        ).astype(BF)

    def pair_rows(src, slot):
        for h in range(4):
            e = one_hot(po[4 * y + h])
            cols = slice(128 * h, 128 * h + 128)
            PSND[slot, :, cols] = nn(e, src[:, cols]).astype(BF)

    @pl.when(upper == 0)
    def _():
        pair_rows(k, 0)
        pair_rows(v, 1)

    @pl.when(upper == 1)
    def _():
        pair_rows(q, 0)

    for src, dst in ((q, QC), (k, KC), (v, VC)):
        dst[mine, :] = jnp.where(c == 0, src[:, 0:256], src[:, 256:512])

    count = 3 + 1 + 2 + 4
    for i in range(2):
        count = count + jnp.where(chip != hub_chip(i), 1, 0)
    count = count + jnp.where(is_hub, nchip - 1, 0)
    pl.semaphore_wait(bar, count)

    mate_copies = [
        rc(src.at[:, mate_lane], dst.at[mine, :], PQKV + n, PQKV + n, (mate, y))
        for n, (src, dst) in enumerate(((q, QC), (k, KC), (v, VC)))
    ]
    for x in mate_copies:
        x.start()

    def y_copy(d):
        return rc(go, GOA.at[y], YG + d - 1, YG + d - 1, (t, (y + d) % 4))

    for d in (2, 1, 3):
        y_copy(d).start()

    def local_copy(src, n, s):
        return rc(
            src.at[:, 256 * s : 256 * s + 256], LB.at[n, mine, :],
            LOC + 2 * n + s, LOC + 2 * n + c, (2 * near + s, y),
        )

    def pair_copy(n, d, s):
        at = pl.ds(pl.multiple_of(128 * odd + 64 * c, 64), 64)
        return rc(
            PSND.at[n, :, 256 * s : 256 * s + 256], PB.at[n, at, :],
            PAIR + 4 * n + 2 * d + s, PAIR + 4 * n + 2 * odd + c, (2 * (other + d) + s, y),
        )

    for s in range(2):
        @pl.when(odd == 0)
        def _(s=s):
            local_copy(k, 0, s).start()
            local_copy(v, 1, s).start()

        @pl.when(odd == 1)
        def _(s=s):
            local_copy(q, 0, s).start()

    for d in range(2):
        for s in range(2):
            pair_copy(0, d, s).start()

            @pl.when(upper == 0)
            def _(d=d, s=s):
                pair_copy(1, d, s).start()

    for x in mate_copies:
        x.wait_recv()

    far_at = pl.ds(pl.multiple_of(8 * chip, 8), 8)
    for i in range(2):
        cols = slice(128 * i, 128 * i + 128)
        for n, src in enumerate((QC, KC, VC)):
            FS[i, n] = pick_far(src[:, cols].astype(F32), off_f[i])

    def far_copy(i):
        return rc(FS.at[i], FG.at[:, far_at, :], FA + i, FA, (2 * hub_chip(i) + c, y))

    def far_copy2(i):
        return rc(FS2.at[i], FG2.at[:, far_at, :], FB + i, FB, (2 * hub_chip(i) + c, y))

    for i in range(2):
        @pl.when(chip != hub_chip(i))
        def _(i=i):
            far_copy(i).start()

        @pl.when(chip == hub_chip(i))
        def _(i=i):
            FG[:, far_at, :] = FS[i]

    grad = nt(go[...], w[:, pl.ds(pl.multiple_of(512 * y, 512), 512)])
    for d in (1, 3, 2):
        src = (y + 4 - d) % 4
        rc(go, GOA.at[src], YG + d - 1, YG + d - 1, (t, src)).wait_recv()
        grad = grad + nt(GOA[src], w[:, pl.ds(pl.multiple_of(512 * src, 512), 512)])
    GOUT[...] = grad.astype(BF)
    GC[mine, :] = jnp.where(c == 0, GOUT[:, 0:256], GOUT[:, 256:512])

    @pl.when(upper == 1)
    def _():
        pair_rows(GOUT, 1)

    grad_mate = rc(GOUT.at[:, mate_lane], GC.at[mine, :], PGRAD, PGRAD, (mate, y))
    grad_mate.start()

    @pl.when(odd == 1)
    def _():
        for s in range(2):
            local_copy(GOUT, 1, s).start()

    @pl.when(upper == 1)
    def _():
        for d in range(2):
            for s in range(2):
                pair_copy(1, d, s).start()

    ri = iota((BOTH, BOTH), 0)
    ci = iota((BOTH, BOTH), 1)

    def own_count(i):
        both = jnp.logical_and((ri & 1) == off_p[i], (ci & 1) == off_p[i])
        return jnp.where(both, 2.0, 1.0)

    def fwd(i, kk, vv, cnt, first=False):
        cols = slice(128 * i, 128 * i + 128)
        s = nt(QC[:, cols], kk) * FACTOR
        s = jnp.where(cnt > 0.0, s, NEG)
        top = jnp.max(s, axis=1, keepdims=True)
        if first:
            m = top
        else:
            m_old = MR[i][:, 0:1]
            m = jnp.maximum(m_old, top)
        p = cnt * jnp.exp(s - m)
        total = jnp.sum(p, axis=1, keepdims=True)
        num = nn(p.astype(BF), vv)
        if not first:
            a = jnp.exp(m_old - m)
            total = total + a * LR[i][:, 0:1]
            num = num + a * ACC[i]
        MR[i] = jnp.broadcast_to(m, (BOTH, 128))
        LR[i] = jnp.broadcast_to(total, (BOTH, 128))
        ACC[i] = num

    for i in range(2):
        cols = slice(128 * i, 128 * i + 128)
        fwd(i, KC[:, cols], VC[:, cols], jnp.where(ri >= ci, own_count(i), 0.0), True)

    @pl.when(is_hub)
    def _():
        rest = FG.at[:, pl.ds(0, 8 * (nchip - 1)), :]
        rc(rest, rest, FA, FA, (t, y)).wait_recv()
        s = nt(FG[0].astype(BF), FG[1].astype(BF)) * FACTOR
        n = s.shape[0]
        s = jnp.where(iota((n, n), 0) >= iota((n, n), 1), s, NEG)
        m = jnp.max(s, axis=1, keepdims=True)
        p = jnp.exp(s - m)
        total = jnp.sum(p, axis=1, keepdims=True)
        R1S[0] = nn(p.astype(BF), FG[2].astype(BF))
        lanes = iota((n, 128), 1)
        R1S[1] = jnp.where(lanes == 0, m, total)

        @pl.loop(0, nchip)
        def _(u):
            at = pl.ds(pl.multiple_of(8 * u, 8), 8)

            @pl.when(u != chip)
            def _():
                rc(R1S.at[:, at, :], FR1.at[hub_turn], R1, R1 + hub_turn, (2 * u + c, y)).start()

        FR1[hub_turn] = R1S[:, far_at, :]

    @pl.when(odd == 1)
    def _():
        for n in range(2):
            for s in range(2):
                rc(
                    k.at[:, 0:256], LB.at[n, pl.ds(128 * s, 128), :],
                    LOC + 2 * n, LOC + 2 * n + s, (2 * near + s, y),
                ).wait_recv()
        for i in range(2):
            cols = slice(128 * i, 128 * i + 128)
            fwd(i, LB[0, :, cols], LB[1, :, cols], own_count(i))

    def pair_wait(n, d, s):
        rc(
            PSND.at[n, :, 0:256], PB.at[n, pl.ds(128 * d + 64 * s, 64), :],
            PAIR, PAIR + 4 * n + 2 * d + s, (2 * (other + d) + s, y),
        ).wait_recv()

    def pair_key_count(i, x):
        return jnp.where((x & 1) == off_p[i], 1.0, 0.0)

    @pl.when(upper == 1)
    def _():
        for n in range(2):
            for d in range(2):
                for s in range(2):
                    pair_wait(n, d, s)
        for i in range(2):
            cols = slice(128 * i, 128 * i + 128)
            fwd(i, PB[0, :, cols], PB[1, :, cols], pair_key_count(i, ri))

    grad_mate.wait_recv()
    l128 = iota((BOTH, 128), 1)
    for i in range(2):
        cols = slice(128 * i, 128 * i + 128)
        gf = GC[:, cols].astype(F32)
        dn = jnp.sum(gf * ACC[i], axis=1, keepdims=True)
        st = jnp.where(l128 == 0, MR[i], jnp.where(l128 == 1, LR[i], dn))
        FS2[i, 0] = pick_far(gf, off_f[i])
        FS2[i, 1] = pick_far(st, off_f[i])

    for i in range(2):
        @pl.when(chip != hub_chip(i))
        def _(i=i):
            far_copy2(i).start()

        @pl.when(chip == hub_chip(i))
        def _(i=i):
            FG2[:, far_at, :] = FS2[i]

    stats = jnp.zeros((BOTH, 128), F32)
    for i in range(2):
        cols = slice(128 * i, 128 * i + 128)

        @pl.when(chip != hub_chip(i))
        def _(i=i):
            rc(R1S.at[:, 0:8, :], FR1.at[i], R1, R1 + i, (2 * hub_chip(i) + c, y)).wait_recv()

        is_far = (iota((BOTH, 1), 0) & (FAR - 1)) == off_f[i]
        num_f = repeat_far(FR1[i, 0])
        st_f = repeat_far(FR1[i, 1])
        m_f = jnp.where(is_far, st_f[:, 0:1], NEG)
        l_f = jnp.where(is_far, st_f[:, 1:2], 0.0)
        m_n = MR[i][:, 0:1]
        m = jnp.maximum(m_n, m_f)
        a = jnp.exp(m_n - m)
        b = jnp.where(is_far, jnp.exp(m_f - m), 0.0)
        total = a * LR[i][:, 0:1] + b * l_f
        out = (a * ACC[i] + b * num_f) / total
        OB[:, cols] = out.astype(BF)
        lse = m + jnp.log(total)
        delta = jnp.sum(GC[:, cols].astype(F32) * out, axis=1, keepdims=True)
        MR[i] = jnp.broadcast_to(lse, (BOTH, 128))
        LR[i] = jnp.broadcast_to(delta, (BOTH, 128))
        stats = jnp.where(l128 == 2 * i, lse, jnp.where(l128 == 2 * i + 1, delta, stats))

    out_mate = rc(OB.at[theirs, :], ORC, POUT, POUT, (mate, y))
    out_mate.start()
    STR[...] = jnp.transpose(stats)[0:8, :]

    @pl.when(upper == 1)
    def _():
        srow = iota((8, 128), 0)
        parts = []
        for i in range(2):
            e = jnp.where(iota((BOTH, 128), 0) == 2 * iota((BOTH, 128), 1) + off_p[i], 1.0, 0.0)
            parts.append(exact(STR[...], e))
        STPS[...] = jnp.where(srow < 2, parts[0], parts[1])

    def near_stats():
        return rc(STR, LSR, STL, STL, (2 * near + c, y))

    def pair_stats(d):
        at = pl.ds(pl.multiple_of(128 * odd, 128), 128)
        return rc(STPS, PSR.at[:, at], STP + d, STP + odd, (2 * (other + d) + c, y))

    @pl.when(odd == 1)
    def _():
        near_stats().start()

    @pl.when(upper == 1)
    def _():
        for d in range(2):
            pair_stats(d).start()

    @pl.when(is_hub)
    def _():
        rest = FG2.at[:, pl.ds(0, 8 * (nchip - 1)), :]
        rc(rest, rest, FB, FB, (t, y)).wait_recv()
        sent = R1S.at[:, pl.ds(0, 8 * (nchip - 1)), :]
        rc(sent, sent, R1, R1, (t, y)).wait_send()
        n = FG.shape[1]
        gf = FG2[0]
        m_f = R1S[1][:, 0:1]
        l_f = R1S[1][:, 1:2]
        m_n = FG2[1][:, 0:1]
        l_n = FG2[1][:, 1:2]
        d_n = FG2[1][:, 2:3]
        m = jnp.maximum(m_f, m_n)
        a = jnp.exp(m_n - m)
        b = jnp.exp(m_f - m)
        total = a * l_n + b * l_f
        lse = m + jnp.log(total)
        d_f = jnp.sum(gf * R1S[0], axis=1, keepdims=True)
        delta = (a * d_n + b * d_f) / total
        lanes = iota((n, 128), 1)
        rows = jnp.transpose(jnp.where(lanes == 0, lse, delta))
        lse_r = rows[0:1, :]
        delta_r = rows[1:2, :]
        qf = FG[0].astype(BF)
        kf = FG[1].astype(BF)
        vf = FG[2].astype(BF)
        gb = gf.astype(BF)
        lower = iota((n, n), 0) >= iota((n, n), 1)
        s = jnp.where(lower, nt(qf, kf) * FACTOR, NEG)
        p = jnp.exp(s - lse)
        ds = (p * (nt(gb, vf) - delta)).astype(BF)
        R2S[0] = nn(ds, kf) * FACTOR
        later = iota((n, n), 1) >= iota((n, n), 0)
        s = jnp.where(later, nt(kf, qf) * FACTOR, NEG)
        p = jnp.exp(s - lse_r)
        R2S[2] = nn(p.astype(BF), gb)
        ds = (p * (nt(vf, gb) - delta_r)).astype(BF)
        R2S[1] = nn(ds, qf) * FACTOR

        @pl.loop(0, nchip)
        def _(u):
            at = pl.ds(pl.multiple_of(8 * u, 8), 8)

            @pl.when(u != chip)
            def _():
                rc(R2S.at[:, at, :], FR2.at[hub_turn], R2, R2 + hub_turn, (2 * u + c, y)).start()

        FR2[hub_turn] = R2S[:, far_at, :]

    out_mate.wait_recv()
    attended = jnp.where(
        c == 0,
        jnp.concatenate([OB[mine, :], ORC[...]], axis=1),
        jnp.concatenate([ORC[...], OB[mine, :]], axis=1),
    )

    def rs_copy(d):
        to = (y + d) % 4
        return rc(RSS.at[to], RSR.at[d - 1], RS + d - 1, RS + d - 1, (t, to))

    for d in (2, 1, 3):
        to = (y + d) % 4
        RSS[to] = nn(attended, w[:, pl.ds(pl.multiple_of(512 * to, 512), 512)]).astype(BF)
        rs_copy(d).start()
    own_lanes = pl.ds(pl.multiple_of(512 * y, 512), 512)
    own_part = nn(attended, w[:, own_lanes]).astype(BF).astype(F32)

    def row_side(i, kk, vv, cnt, masked):
        cols = slice(128 * i, 128 * i + 128)
        s = nt(QC[:, cols], kk) * FACTOR
        if masked:
            s = jnp.where(cnt > 0.0, s, NEG)
        p = cnt * jnp.exp(s - MR[i][:, 0:1])
        ds = (p * (nt(GC[:, cols], vv) - LR[i][:, 0:1])).astype(BF)
        return nn(ds, kk)

    def col_side(i, qq, gg, st, cnt, masked):
        cols = slice(128 * i, 128 * i + 128)
        s = nt(KC[:, cols], qq) * FACTOR
        if masked:
            s = jnp.where(cnt > 0.0, s, NEG)
        p = cnt * jnp.exp(s - st[2 * i : 2 * i + 1, :])
        ds = (p * (nt(VC[:, cols], gg) - st[2 * i + 1 : 2 * i + 2, :])).astype(BF)
        return nn(ds, qq), nn(p.astype(BF), gg)

    for i in range(2):
        cols = slice(128 * i, 128 * i + 128)
        DQ[i] = row_side(i, KC[:, cols], VC[:, cols], jnp.where(ri >= ci, own_count(i), 0.0), True)
        DK[i], DV[i] = col_side(
            i, QC[:, cols], GC[:, cols], STR[...], jnp.where(ci >= ri, own_count(i), 0.0), True
        )

    acc = own_part
    for d in (1, 3, 2):
        rs_copy(d).wait_recv()
        acc = acc + RSR[d - 1].astype(F32)
    AGS[...] = acc.astype(BF)

    def ag_copy(d):
        return rc(AGS, AGR.at[d - 1], AG + d - 1, AG + d - 1, (t, (y + d) % 4))

    for d in (2, 1, 3):
        ag_copy(d).start()
    lo[:, own_lanes] = AGS[...]

    @pl.when(odd == 1)
    def _():
        for i in range(2):
            cols = slice(128 * i, 128 * i + 128)
            DQ[i] += row_side(i, LB[0, :, cols], LB[1, :, cols], own_count(i), False)

    @pl.when(odd == 0)
    def _():
        for n in range(2):
            for s in range(2):
                rc(
                    k.at[:, 0:256], LB.at[n, pl.ds(128 * s, 128), :],
                    LOC + 2 * n, LOC + 2 * n + s, (2 * near + s, y),
                ).wait_recv()
        near_stats().wait_recv()
        for i in range(2):
            cols = slice(128 * i, 128 * i + 128)
            a, b = col_side(i, LB[0, :, cols], LB[1, :, cols], LSR[...], own_count(i), False)
            DK[i] += a
            DV[i] += b

    @pl.when(upper == 1)
    def _():
        for i in range(2):
            cols = slice(128 * i, 128 * i + 128)
            DQ[i] += row_side(i, PB[0, :, cols], PB[1, :, cols], pair_key_count(i, ri), True)

    @pl.when(upper == 0)
    def _():
        for n in range(2):
            for d in range(2):
                for s in range(2):
                    pair_wait(n, d, s)
        for d in range(2):
            rc(
                STPS, PSR.at[:, 128 * d : 128 * d + 128], STP, STP + d, (2 * (other + d) + c, y)
            ).wait_recv()
        for i in range(2):
            cols = slice(128 * i, 128 * i + 128)
            a, b = col_side(
                i, PB[0, :, cols], PB[1, :, cols], PSR[...], pair_key_count(i, ri), True
            )
            DK[i] += a
            DV[i] += b

    for i in range(2):
        @pl.when(chip != hub_chip(i))
        def _(i=i):
            rc(R2S.at[:, 0:8, :], FR2.at[i], R2, R2 + i, (2 * hub_chip(i) + c, y)).wait_recv()

    is_far = [(iota((BOTH, 1), 0) & (FAR - 1)) == off_f[i] for i in range(2)]
    for n, (src, scale) in enumerate(((DQ, FACTOR), (DK, FACTOR), (DV, 1.0))):
        full = jnp.concatenate(
            [
                (src[i] * scale + jnp.where(is_far[i], repeat_far(FR2[i, n]), 0.0)).astype(BF)
                for i in range(2)
            ],
            axis=1,
        )
        DSND[n] = jnp.where(c == 0, full[ROWS:, :], full[:ROWS, :])
        (dq, dk, dv)[n][:, lane] = jnp.where(c == 0, full[:ROWS, :], full[ROWS:, :])
    back = rc(DSND, DRCV, PDQ, PDQ, (mate, y))
    back.start()

    for d in (1, 3, 2):
        ag_copy(d).wait_recv()
        src = (y + 4 - d) % 4
        lo[:, pl.ds(pl.multiple_of(512 * src, 512), 512)] = AGR[d - 1]
    back.wait_recv()
    for n, dst in enumerate((dq, dk, dv)):
        dst[:, mate_lane] = DRCV[n]

    for x in mate_copies:
        x.wait_send()
    for d in range(1, 4):
        y_copy(d).wait_send()
        rs_copy(d).wait_send()
        ag_copy(d).wait_send()
    for n in range(2):
        for s in range(2):
            local_copy(k, n, s).wait_send()
            for d in range(2):
                pair_copy(n, d, s).wait_send()
    grad_mate.wait_send()
    out_mate.wait_send()
    back.wait_send()
    for i in range(2):
        @pl.when(chip != hub_chip(i))
        def _(i=i):
            far_copy(i).wait_send()
            far_copy2(i).wait_send()

    @pl.when(odd == 1)
    def _():
        near_stats().wait_send()

    @pl.when(upper == 1)
    def _():
        for d in range(2):
            pair_stats(d).wait_send()

    @pl.when(is_hub)
    def _():
        sent = R2S.at[:, pl.ds(0, 8 * (nchip - 1)), :]
        rc(sent, sent, R2, R2, (t, y)).wait_send()


def local(queries, key_rows, value_rows, out_weight, grad_out, pair_offsets, far_head_offsets):
    vm = pl.BlockSpec(memory_space=pltpu.VMEM)
    sm = pl.BlockSpec(memory_space=pltpu.SMEM)
    rows = jax.ShapeDtypeStruct((ROWS, 512), BF)

    def b(*shape):
        return pltpu.VMEM(shape, BF)

    def f(*shape):
        return pltpu.VMEM(shape, F32)

    return pl.pallas_call(
        kernel,
        out_shape=(jax.ShapeDtypeStruct((ROWS, 2048), BF), rows, rows, rows),
        in_specs=[vm] * 5 + [sm] * 2,
        out_specs=(vm,) * 4,
        scratch_shapes=[
            b(256, 256), b(256, 256), b(256, 256), b(256, 256),
            b(2, 256, 256), b(2, 256, 256), b(2, 64, 512), b(4, 128, 512), b(128, 512),
            f(2, 256, 128), f(2, 256, 128), f(2, 256, 128),
            f(2, 256, 128), f(2, 256, 128), f(2, 256, 128),
            f(8, 256), f(8, 128), f(8, 256), f(8, 256),
            f(2, 3, 8, 128), f(2, 2, 8, 128), f(3, 512, 128), f(2, 512, 128),
            f(2, 512, 128), f(3, 512, 128), f(2, 2, 8, 128), f(2, 3, 8, 128),
            b(256, 256), b(128, 256), b(4, 128, 512), b(3, 128, 512),
            b(128, 512), b(3, 128, 512), b(3, 128, 256), b(3, 128, 256),
            pltpu.SemaphoreType.DMA((NSEM,)),
            pltpu.SemaphoreType.DMA((NSEM,)),
        ],
        compiler_params=pltpu.CompilerParams(collective_id=0, has_side_effects=True),
    )(queries, key_rows, value_rows, out_weight, grad_out, pair_offsets, far_head_offsets)


def solution(mesh):
    seq = P("seq", "head")
    return jax.shard_map(
        local,
        mesh=mesh,
        in_specs=(seq, seq, seq, P("head", None), seq, P(), P()),
        out_specs=(P("seq", None), seq, seq, seq),
        check_vma=False,
    )
```

```python
import jax
import jax.numpy as jnp
from jax import lax
from jax.experimental import pallas as pl
from jax.experimental.pallas import tpu as pltpu
from jax.sharding import PartitionSpec as P

MESH = pl.DeviceIdType.MESH
NEG = -1.0e30
F32 = jnp.float32
BF = jnp.bfloat16
FACTOR = 128 ** (-0.5)
ROWS = 128
BOTH = 256
ZC = 16
FAR = 32

PQKV, PGRAD, POUT, PDQ = 0, 3, 4, 5
LOC, PAIR, YG, RS, AG = 6, 10, 18, 21, 24
STL, STP = 27, 28
R1, R2 = 30, 32
FA, FB, FMATE = 34, 36, 38
NSEM = 39


def nt(a, b):
    return lax.dot_general(a, b, (((1,), (1,)), ((), ())), preferred_element_type=F32)


def nn(a, b):
    return jnp.dot(a, b, preferred_element_type=F32)


def exact(a, b):
    return lax.dot_general(
        a, b, (((1,), (0,)), ((), ())), precision=lax.Precision.HIGHEST, preferred_element_type=F32
    )


def iota(shape, dim):
    return lax.broadcasted_iota(jnp.int32, shape, dim)


def pick_far(x, off):
    rows = iota(x.shape, 0)
    kept = jnp.where((rows & (FAR - 1)) == off, x, 0.0)
    return jnp.sum(kept.reshape(BOTH // FAR, FAR, 128), axis=1)


def repeat_far(x):
    return jnp.broadcast_to(x[:, None, :], (BOTH // FAR, FAR, 128)).reshape(BOTH, 128)


def kernel(
    q_in, k_in, v_in, w_in, go_in, po, fo,
    lo, dq, dk, dv,
    q, k, v, w, go,
    QC, KC, VC, GC, LB, PB, PSND, GOA, GOUT,
    MR, LR, ACC, DQ, DK, DV, STR, STPS, LSR, PSR,
    FX, FY, FS, FS2, FG, FG2, R1S, R2S, FR1, FR2,
    OB, ORC, RSS, RSR, AGS, AGR, DSND, DRCV,
    ss, rs, ls,
):
    t = lax.axis_index("seq")
    y = lax.axis_index("head")
    c = t % 2
    chip = t // 2
    odd = chip % 2
    g = chip % 4
    upper = g // 2
    mate = t + 1 - 2 * c
    near = chip + 1 - 2 * odd
    other = chip - g + 2 - 2 * upper
    nchip = lax.axis_size("seq") // 2
    hub_turn = (chip // ZC) % 2
    is_hub = jnp.logical_and(chip % ZC == 0, (chip // ZC) // 2 == c)

    def hub_chip(i):
        return ZC * (2 * c + i)

    def rc(src, dst, i, j, dev):
        return pltpu.make_async_remote_copy(
            src_ref=src, dst_ref=dst, send_sem=ss.at[i], recv_sem=rs.at[j],
            device_id=dev, device_id_type=MESH,
        )

    loads = [
        pltpu.make_async_copy(a, b, ls.at[n])
        for n, (a, b) in enumerate(((k_in, k), (v_in, v), (q_in, q), (go_in, go), (w_in, w)))
    ]
    for x in loads:
        x.start()

    bar = pltpu.get_barrier_semaphore()

    def sig(dev):
        pl.semaphore_signal(bar, inc=1, device_id=dev, device_id_type=MESH)

    def from_far(n):
        turn = n // 4
        step = (turn + 1) // 2
        return ZC * (n % 4) + (8 + jnp.where(turn % 2 == 1, ZC - step, step)) % ZC

    @pl.when(is_hub)
    def _():
        @pl.loop(0, nchip)
        def _(n):
            u = from_far(n)

            @pl.when(u != chip)
            def _():
                sig((2 * u + c, y))

    for d in range(1, 4):
        sig((t, (y + d) % 4))
    sig((mate, y))
    for s in range(2):
        sig((2 * near + s, y))
        for d in range(2):
            sig((2 * (other + d) + s, y))

    off_p = [po[4 * y + 2 * c + i] for i in range(2)]
    off_f = [fo[4 * y + 2 * c + i] for i in range(2)]
    lane = pl.ds(pl.multiple_of(256 * c, 256), 256)
    mine = pl.ds(pl.multiple_of(ROWS * c, ROWS), ROWS)
    theirs = pl.ds(pl.multiple_of(ROWS * (1 - c), ROWS), ROWS)
    mate_lane = pl.ds(pl.multiple_of(256 * (1 - c), 256), 256)

    def one_hot(off):
        return jnp.where(
            iota((64, ROWS), 1) == 2 * iota((64, ROWS), 0) + off, 1.0, 0.0
        ).astype(BF)

    def pair_rows(src, slot):
        for h in range(4):
            e = one_hot(po[4 * y + h])
            cols = slice(128 * h, 128 * h + 128)
            PSND[slot, :, cols] = nn(e, src[:, cols]).astype(BF)

    for x in loads[:3]:
        x.wait()
    own_rows = (iota((8, 128), 0) // 4) == c
    for h in range(4):
        for n, src in enumerate((q, k, v)):
            x = src[:, 128 * h : 128 * h + 128].astype(F32)
            x = jnp.where((iota((ROWS, 128), 0) & (FAR - 1)) == fo[4 * y + h], x, 0.0)
            x = jnp.sum(x.reshape(4, FAR, 128), axis=1)
            x = jnp.where(own_rows, jnp.concatenate([x, x], axis=0), 0.0)
            FX[h // 2, h % 2, n] = x

    @pl.when(upper == 0)
    def _():
        pair_rows(k, 0)
        pair_rows(v, 1)

    @pl.when(upper == 1)
    def _():
        pair_rows(q, 0)

    for src, dst in ((q, QC), (k, KC), (v, VC)):
        dst[mine, :] = jnp.where(c == 0, src[:, 0:256], src[:, 256:512])

    count = 3 + 1 + 2 + 4
    for i in range(2):
        count = count + jnp.where(chip != hub_chip(i), 1, 0)
    pl.semaphore_wait(bar, count)

    def far_mate():
        return rc(FX.at[1 - c], FY, FMATE, FMATE, (mate, y))

    far_mate().start()
    def y_copy(d):
        return rc(go, GOA.at[y], YG + d - 1, YG + d - 1, (t, (y + d) % 4))

    loads[3].wait()
    for d in (2, 1, 3):
        y_copy(d).start()

    def local_copy(src, n, s):
        return rc(
            src.at[:, 256 * s : 256 * s + 256], LB.at[n, mine, :],
            LOC + 2 * n + s, LOC + 2 * n + c, (2 * near + s, y),
        )

    def pair_copy(n, d, s):
        at = pl.ds(pl.multiple_of(128 * odd + 64 * c, 64), 64)
        return rc(
            PSND.at[n, :, 256 * s : 256 * s + 256], PB.at[n, at, :],
            PAIR + 4 * n + 2 * d + s, PAIR + 4 * n + 2 * odd + c, (2 * (other + d) + s, y),
        )

    far_at = pl.ds(pl.multiple_of(8 * chip, 8), 8)
    far_mate().wait_recv()
    for i in range(2):
        FS[i] = FX[c, i] + FY[i]

    def far_copy(i):
        return rc(FS.at[i], FG.at[:, far_at, :], FA + i, FA, (2 * hub_chip(i) + c, y))

    def far_copy2(i):
        return rc(FS2.at[i], FG2.at[:, far_at, :], FB + i, FB, (2 * hub_chip(i) + c, y))

    for i in range(2):
        @pl.when(chip != hub_chip(i))
        def _(i=i):
            far_copy(i).start()

        @pl.when(chip == hub_chip(i))
        def _(i=i):
            FG[:, far_at, :] = FS[i]

    mate_copies = [
        rc(src.at[:, mate_lane], dst.at[mine, :], PQKV + n, PQKV + n, (mate, y))
        for n, (src, dst) in enumerate(((q, QC), (k, KC), (v, VC)))
    ]
    for x in mate_copies:
        x.start()

    for s in range(2):
        @pl.when(odd == 0)
        def _(s=s):
            local_copy(k, 0, s).start()
            local_copy(v, 1, s).start()

        @pl.when(odd == 1)
        def _(s=s):
            local_copy(q, 0, s).start()

    for d in range(2):
        for s in range(2):
            pair_copy(0, d, s).start()

            @pl.when(upper == 0)
            def _(d=d, s=s):
                pair_copy(1, d, s).start()

    loads[4].wait()
    grad = nt(go[...], w[:, pl.ds(pl.multiple_of(512 * y, 512), 512)])
    for d in (1, 3, 2):
        src = (y + 4 - d) % 4
        rc(go, GOA.at[src], YG + d - 1, YG + d - 1, (t, src)).wait_recv()
        grad = grad + nt(GOA[src], w[:, pl.ds(pl.multiple_of(512 * src, 512), 512)])
    GOUT[...] = grad.astype(BF)
    GC[mine, :] = jnp.where(c == 0, GOUT[:, 0:256], GOUT[:, 256:512])

    @pl.when(upper == 1)
    def _():
        pair_rows(GOUT, 1)

    grad_mate = rc(GOUT.at[:, mate_lane], GC.at[mine, :], PGRAD, PGRAD, (mate, y))
    grad_mate.start()

    @pl.when(odd == 1)
    def _():
        for s in range(2):
            local_copy(GOUT, 1, s).start()

    @pl.when(upper == 1)
    def _():
        for d in range(2):
            for s in range(2):
                pair_copy(1, d, s).start()

    for x in mate_copies:
        x.wait_recv()

    ri = iota((BOTH, BOTH), 0)
    ci = iota((BOTH, BOTH), 1)

    def own_count(i):
        both = jnp.logical_and((ri & 1) == off_p[i], (ci & 1) == off_p[i])
        return jnp.where(both, 2.0, 1.0)

    def fwd(i, kk, vv, cnt, first=False):
        cols = slice(128 * i, 128 * i + 128)
        s = nt(QC[:, cols], kk) * FACTOR
        s = jnp.where(cnt > 0.0, s, NEG)
        top = jnp.max(s, axis=1, keepdims=True)
        if first:
            m = top
        else:
            m_old = MR[i][:, 0:1]
            m = jnp.maximum(m_old, top)
        p = cnt * jnp.exp(s - m)
        total = jnp.sum(p, axis=1, keepdims=True)
        num = nn(p.astype(BF), vv)
        if not first:
            a = jnp.exp(m_old - m)
            total = total + a * LR[i][:, 0:1]
            num = num + a * ACC[i]
        MR[i] = jnp.broadcast_to(m, (BOTH, 128))
        LR[i] = jnp.broadcast_to(total, (BOTH, 128))
        ACC[i] = num

    for i in range(2):
        cols = slice(128 * i, 128 * i + 128)
        fwd(i, KC[:, cols], VC[:, cols], jnp.where(ri >= ci, own_count(i), 0.0), True)

    @pl.when(odd == 1)
    def _():
        for n in range(2):
            for s in range(2):
                rc(
                    k.at[:, 0:256], LB.at[n, pl.ds(128 * s, 128), :],
                    LOC + 2 * n, LOC + 2 * n + s, (2 * near + s, y),
                ).wait_recv()
        for i in range(2):
            cols = slice(128 * i, 128 * i + 128)
            fwd(i, LB[0, :, cols], LB[1, :, cols], own_count(i))

    def pair_wait(n, d, s):
        rc(
            PSND.at[n, :, 0:256], PB.at[n, pl.ds(128 * d + 64 * s, 64), :],
            PAIR, PAIR + 4 * n + 2 * d + s, (2 * (other + d) + s, y),
        ).wait_recv()

    def pair_key_count(i, x):
        return jnp.where((x & 1) == off_p[i], 1.0, 0.0)

    @pl.when(upper == 1)
    def _():
        for n in range(2):
            for d in range(2):
                for s in range(2):
                    pair_wait(n, d, s)
        for i in range(2):
            cols = slice(128 * i, 128 * i + 128)
            fwd(i, PB[0, :, cols], PB[1, :, cols], pair_key_count(i, ri))

    grad_mate.wait_recv()
    l128 = iota((BOTH, 128), 1)
    for i in range(2):
        cols = slice(128 * i, 128 * i + 128)
        gf = GC[:, cols].astype(F32)
        dn = jnp.sum(gf * ACC[i], axis=1, keepdims=True)
        st = jnp.where(l128 == 0, MR[i], jnp.where(l128 == 1, LR[i], dn))
        FS2[i, 0] = pick_far(gf, off_f[i])
        FS2[i, 1] = pick_far(st, off_f[i])

    for i in range(2):
        @pl.when(chip != hub_chip(i))
        def _(i=i):
            far_copy2(i).start()

        @pl.when(chip == hub_chip(i))
        def _(i=i):
            FG2[:, far_at, :] = FS2[i]

    @pl.when(is_hub)
    def _():
        rest = FG.at[:, pl.ds(0, 8 * (nchip - 1)), :]
        rc(rest, rest, FA, FA, (t, y)).wait_recv()
        s = nt(FG[0].astype(BF), FG[1].astype(BF)) * FACTOR
        n = s.shape[0]
        s = jnp.where(iota((n, n), 0) >= iota((n, n), 1), s, NEG)
        m = jnp.max(s, axis=1, keepdims=True)
        p = jnp.exp(s - m)
        total = jnp.sum(p, axis=1, keepdims=True)
        R1S[0] = nn(p.astype(BF), FG[2].astype(BF))
        lanes = iota((n, 128), 1)
        R1S[1] = jnp.where(lanes == 0, m, total)

        @pl.loop(0, nchip)
        def _(n):
            u = from_far(n)
            at = pl.ds(pl.multiple_of(8 * u, 8), 8)

            @pl.when(u != chip)
            def _():
                rc(R1S.at[:, at, :], FR1.at[hub_turn], R1, R1 + hub_turn, (2 * u + c, y)).start()

        FR1[hub_turn] = R1S[:, far_at, :]

    stats = jnp.zeros((BOTH, 128), F32)
    for i in range(2):
        cols = slice(128 * i, 128 * i + 128)

        @pl.when(chip != hub_chip(i))
        def _(i=i):
            rc(R1S.at[:, 0:8, :], FR1.at[i], R1, R1 + i, (2 * hub_chip(i) + c, y)).wait_recv()

        is_far = (iota((BOTH, 1), 0) & (FAR - 1)) == off_f[i]
        num_f = repeat_far(FR1[i, 0])
        st_f = repeat_far(FR1[i, 1])
        m_f = jnp.where(is_far, st_f[:, 0:1], NEG)
        l_f = jnp.where(is_far, st_f[:, 1:2], 0.0)
        m_n = MR[i][:, 0:1]
        m = jnp.maximum(m_n, m_f)
        a = jnp.exp(m_n - m)
        b = jnp.where(is_far, jnp.exp(m_f - m), 0.0)
        total = a * LR[i][:, 0:1] + b * l_f
        out = (a * ACC[i] + b * num_f) / total
        OB[:, cols] = out.astype(BF)
        lse = m + jnp.log(total)
        delta = jnp.sum(GC[:, cols].astype(F32) * out, axis=1, keepdims=True)
        MR[i] = jnp.broadcast_to(lse, (BOTH, 128))
        LR[i] = jnp.broadcast_to(delta, (BOTH, 128))
        stats = jnp.where(l128 == 2 * i, lse, jnp.where(l128 == 2 * i + 1, delta, stats))

    out_mate = rc(OB.at[theirs, :], ORC, POUT, POUT, (mate, y))
    out_mate.start()
    STR[...] = jnp.transpose(stats)[0:8, :]

    @pl.when(upper == 1)
    def _():
        srow = iota((8, 128), 0)
        parts = []
        for i in range(2):
            e = jnp.where(iota((BOTH, 128), 0) == 2 * iota((BOTH, 128), 1) + off_p[i], 1.0, 0.0)
            parts.append(exact(STR[...], e))
        STPS[...] = jnp.where(srow < 2, parts[0], parts[1])

    def near_stats():
        return rc(STR, LSR, STL, STL, (2 * near + c, y))

    def pair_stats(d):
        at = pl.ds(pl.multiple_of(128 * odd, 128), 128)
        return rc(STPS, PSR.at[:, at], STP + d, STP + odd, (2 * (other + d) + c, y))

    @pl.when(odd == 1)
    def _():
        near_stats().start()

    @pl.when(upper == 1)
    def _():
        for d in range(2):
            pair_stats(d).start()

    @pl.when(is_hub)
    def _():
        rest = FG2.at[:, pl.ds(0, 8 * (nchip - 1)), :]
        rc(rest, rest, FB, FB, (t, y)).wait_recv()
        sent = R1S.at[:, pl.ds(0, 8 * (nchip - 1)), :]
        rc(sent, sent, R1, R1, (t, y)).wait_send()
        n = FG.shape[1]
        gf = FG2[0]
        m_f = R1S[1][:, 0:1]
        l_f = R1S[1][:, 1:2]
        m_n = FG2[1][:, 0:1]
        l_n = FG2[1][:, 1:2]
        d_n = FG2[1][:, 2:3]
        m = jnp.maximum(m_f, m_n)
        a = jnp.exp(m_n - m)
        b = jnp.exp(m_f - m)
        total = a * l_n + b * l_f
        lse = m + jnp.log(total)
        d_f = jnp.sum(gf * R1S[0], axis=1, keepdims=True)
        delta = (a * d_n + b * d_f) / total
        lanes = iota((n, 128), 1)
        rows = jnp.transpose(jnp.where(lanes == 0, lse, delta))
        lse_r = rows[0:1, :]
        delta_r = rows[1:2, :]
        qf = FG[0].astype(BF)
        kf = FG[1].astype(BF)
        vf = FG[2].astype(BF)
        gb = gf.astype(BF)
        lower = iota((n, n), 0) >= iota((n, n), 1)
        s = jnp.where(lower, nt(qf, kf) * FACTOR, NEG)
        p = jnp.exp(s - lse)
        ds = (p * (nt(gb, vf) - delta)).astype(BF)
        R2S[0] = nn(ds, kf) * FACTOR
        later = iota((n, n), 1) >= iota((n, n), 0)
        s = jnp.where(later, nt(kf, qf) * FACTOR, NEG)
        p = jnp.exp(s - lse_r)
        R2S[2] = nn(p.astype(BF), gb)
        ds = (p * (nt(vf, gb) - delta_r)).astype(BF)
        R2S[1] = nn(ds, qf) * FACTOR

        @pl.loop(0, nchip)
        def _(n):
            u = from_far(n)
            at = pl.ds(pl.multiple_of(8 * u, 8), 8)

            @pl.when(u != chip)
            def _():
                rc(R2S.at[:, at, :], FR2.at[hub_turn], R2, R2 + hub_turn, (2 * u + c, y)).start()

        FR2[hub_turn] = R2S[:, far_at, :]

    out_mate.wait_recv()
    attended = jnp.where(
        c == 0,
        jnp.concatenate([OB[mine, :], ORC[...]], axis=1),
        jnp.concatenate([ORC[...], OB[mine, :]], axis=1),
    )

    def rs_copy(d):
        to = (y + d) % 4
        return rc(RSS.at[to], RSR.at[d - 1], RS + d - 1, RS + d - 1, (t, to))

    for d in (2, 1, 3):
        to = (y + d) % 4
        RSS[to] = nn(attended, w[:, pl.ds(pl.multiple_of(512 * to, 512), 512)]).astype(BF)
        rs_copy(d).start()
    own_lanes = pl.ds(pl.multiple_of(512 * y, 512), 512)
    own_part = nn(attended, w[:, own_lanes]).astype(BF).astype(F32)

    def row_side(i, kk, vv, cnt, masked):
        cols = slice(128 * i, 128 * i + 128)
        s = nt(QC[:, cols], kk) * FACTOR
        if masked:
            s = jnp.where(cnt > 0.0, s, NEG)
        p = cnt * jnp.exp(s - MR[i][:, 0:1])
        ds = (p * (nt(GC[:, cols], vv) - LR[i][:, 0:1])).astype(BF)
        return nn(ds, kk)

    def col_side(i, qq, gg, st, cnt, masked):
        cols = slice(128 * i, 128 * i + 128)
        s = nt(KC[:, cols], qq) * FACTOR
        if masked:
            s = jnp.where(cnt > 0.0, s, NEG)
        p = cnt * jnp.exp(s - st[2 * i : 2 * i + 1, :])
        ds = (p * (nt(VC[:, cols], gg) - st[2 * i + 1 : 2 * i + 2, :])).astype(BF)
        return nn(ds, qq), nn(p.astype(BF), gg)

    for i in range(2):
        cols = slice(128 * i, 128 * i + 128)
        DQ[i] = row_side(i, KC[:, cols], VC[:, cols], jnp.where(ri >= ci, own_count(i), 0.0), True)
        DK[i], DV[i] = col_side(
            i, QC[:, cols], GC[:, cols], STR[...], jnp.where(ci >= ri, own_count(i), 0.0), True
        )

    acc = own_part
    for d in (1, 3, 2):
        rs_copy(d).wait_recv()
        acc = acc + RSR[d - 1].astype(F32)
    AGS[...] = acc.astype(BF)

    def ag_copy(d):
        return rc(AGS, AGR.at[d - 1], AG + d - 1, AG + d - 1, (t, (y + d) % 4))

    for d in (2, 1, 3):
        ag_copy(d).start()
    lo[:, own_lanes] = AGS[...]

    @pl.when(odd == 1)
    def _():
        for i in range(2):
            cols = slice(128 * i, 128 * i + 128)
            DQ[i] += row_side(i, LB[0, :, cols], LB[1, :, cols], own_count(i), False)

    @pl.when(odd == 0)
    def _():
        for n in range(2):
            for s in range(2):
                rc(
                    k.at[:, 0:256], LB.at[n, pl.ds(128 * s, 128), :],
                    LOC + 2 * n, LOC + 2 * n + s, (2 * near + s, y),
                ).wait_recv()
        near_stats().wait_recv()
        for i in range(2):
            cols = slice(128 * i, 128 * i + 128)
            a, b = col_side(i, LB[0, :, cols], LB[1, :, cols], LSR[...], own_count(i), False)
            DK[i] += a
            DV[i] += b

    @pl.when(upper == 1)
    def _():
        for i in range(2):
            cols = slice(128 * i, 128 * i + 128)
            DQ[i] += row_side(i, PB[0, :, cols], PB[1, :, cols], pair_key_count(i, ri), True)

    @pl.when(upper == 0)
    def _():
        for n in range(2):
            for d in range(2):
                for s in range(2):
                    pair_wait(n, d, s)
        for d in range(2):
            rc(
                STPS, PSR.at[:, 128 * d : 128 * d + 128], STP, STP + d, (2 * (other + d) + c, y)
            ).wait_recv()
        for i in range(2):
            cols = slice(128 * i, 128 * i + 128)
            a, b = col_side(
                i, PB[0, :, cols], PB[1, :, cols], PSR[...], pair_key_count(i, ri), True
            )
            DK[i] += a
            DV[i] += b

    for i in range(2):
        @pl.when(chip != hub_chip(i))
        def _(i=i):
            rc(R2S.at[:, 0:8, :], FR2.at[i], R2, R2 + i, (2 * hub_chip(i) + c, y)).wait_recv()

    is_far = [(iota((BOTH, 1), 0) & (FAR - 1)) == off_f[i] for i in range(2)]
    for n, (src, scale) in enumerate(((DQ, FACTOR), (DK, FACTOR), (DV, 1.0))):
        full = jnp.concatenate(
            [
                (src[i] * scale + jnp.where(is_far[i], repeat_far(FR2[i, n]), 0.0)).astype(BF)
                for i in range(2)
            ],
            axis=1,
        )
        DSND[n] = jnp.where(c == 0, full[ROWS:, :], full[:ROWS, :])
        (dq, dk, dv)[n][:, lane] = jnp.where(c == 0, full[:ROWS, :], full[ROWS:, :])
    back = rc(DSND, DRCV, PDQ, PDQ, (mate, y))
    back.start()

    for d in (1, 3, 2):
        ag_copy(d).wait_recv()
        src = (y + 4 - d) % 4
        lo[:, pl.ds(pl.multiple_of(512 * src, 512), 512)] = AGR[d - 1]
    back.wait_recv()
    for n, dst in enumerate((dq, dk, dv)):
        dst[:, mate_lane] = DRCV[n]

    far_mate().wait_send()
    for x in mate_copies:
        x.wait_send()
    for d in range(1, 4):
        y_copy(d).wait_send()
        rs_copy(d).wait_send()
        ag_copy(d).wait_send()
    for n in range(2):
        for s in range(2):
            local_copy(k, n, s).wait_send()
            for d in range(2):
                pair_copy(n, d, s).wait_send()
    grad_mate.wait_send()
    out_mate.wait_send()
    back.wait_send()
    for i in range(2):
        @pl.when(chip != hub_chip(i))
        def _(i=i):
            far_copy(i).wait_send()
            far_copy2(i).wait_send()

    @pl.when(odd == 1)
    def _():
        near_stats().wait_send()

    @pl.when(upper == 1)
    def _():
        for d in range(2):
            pair_stats(d).wait_send()

    @pl.when(is_hub)
    def _():
        sent = R2S.at[:, pl.ds(0, 8 * (nchip - 1)), :]
        rc(sent, sent, R2, R2, (t, y)).wait_send()


def store(*refs):
    copies = [
        pltpu.make_async_copy(a, b, refs[8].at[n]) for n, (a, b) in enumerate(zip(refs[:4], refs[4:8]))
    ]
    for x in copies:
        x.start()
    for x in copies:
        x.wait()


def local(queries, key_rows, value_rows, out_weight, grad_out, pair_offsets, far_head_offsets):
    vm = pl.BlockSpec(memory_space=pltpu.VMEM)
    sm = pl.BlockSpec(memory_space=pltpu.SMEM)
    rows = jax.ShapeDtypeStruct((ROWS, 512), BF)

    def b(*shape):
        return pltpu.VMEM(shape, BF)

    def f(*shape):
        return pltpu.VMEM(shape, F32)

    outs = pl.pallas_call(
        kernel,
        out_shape=(pltpu.VMEM((ROWS, 2048), BF),) + (pltpu.VMEM((ROWS, 512), BF),) * 3,
        in_specs=[pl.BlockSpec(memory_space=pl.ANY)] * 5 + [sm] * 2,
        out_specs=(vm,) * 4,
        scratch_shapes=[
            b(128, 512), b(128, 512), b(128, 512), b(512, 2048), b(128, 512),
            b(256, 256), b(256, 256), b(256, 256), b(256, 256),
            b(2, 256, 256), b(2, 256, 256), b(2, 64, 512), b(4, 128, 512), b(128, 512),
            f(2, 256, 128), f(2, 256, 128), f(2, 256, 128),
            f(2, 256, 128), f(2, 256, 128), f(2, 256, 128),
            f(8, 256), f(8, 128), f(8, 256), f(8, 256),
            f(2, 2, 3, 8, 128), f(2, 3, 8, 128),
            f(2, 3, 8, 128), f(2, 2, 8, 128), f(3, 512, 128), f(2, 512, 128),
            f(2, 512, 128), f(3, 512, 128), f(2, 2, 8, 128), f(2, 3, 8, 128),
            b(256, 256), b(128, 256), b(4, 128, 512), b(3, 128, 512),
            b(128, 512), b(3, 128, 512), b(3, 128, 256), b(3, 128, 256),
            pltpu.SemaphoreType.DMA((NSEM,)),
            pltpu.SemaphoreType.DMA((NSEM,)),
            pltpu.SemaphoreType.DMA((5,)),
        ],
        compiler_params=pltpu.CompilerParams(collective_id=0, has_side_effects=True),
    )(queries, key_rows, value_rows, out_weight, grad_out, pair_offsets, far_head_offsets)
    return pl.pallas_call(
        store,
        out_shape=(jax.ShapeDtypeStruct((ROWS, 2048), BF), rows, rows, rows),
        in_specs=[vm] * 4,
        out_specs=(pl.BlockSpec(memory_space=pl.ANY),) * 4,
        scratch_shapes=[pltpu.SemaphoreType.DMA((4,))],
    )(*[pltpu.with_memory_space_constraint(x, pltpu.VMEM) for x in outs])


def solution(mesh):
    seq = P("seq", "head")
    return jax.shard_map(
        local,
        mesh=mesh,
        in_specs=(seq, seq, seq, P("head", None), seq, P(), P()),
        out_specs=(P("seq", None), seq, seq, seq),
        check_vma=False,
    )
```

```python
import jax
import jax.numpy as jnp
from jax import lax
from jax.experimental import pallas as pl
from jax.experimental.pallas import tpu as pltpu
from jax.sharding import PartitionSpec as P

MESH = pl.DeviceIdType.MESH
NEG = -1.0e30
F32 = jnp.float32
BF = jnp.bfloat16
FACTOR = 128 ** (-0.5)
ROWS = 128
BOTH = 256
ZC = 16
FAR = 32

PQKV, PGRAD, POUT, PDQ = 0, 3, 4, 5
LOC, PAIR, YG, RS, AG = 6, 10, 18, 21, 54
STL, STP = 27, 28
R1, R2 = 30, 32
FA, FB, FMATE = 34, 36, 38
FQN, FQP, FRN, FRP, FIX, FBK = 39, 40, 42, 43, 45, 53
NSEM = 60


def nt(a, b):
    return lax.dot_general(a, b, (((1,), (1,)), ((), ())), preferred_element_type=F32)


def nn(a, b):
    return jnp.dot(a, b, preferred_element_type=F32)


def exact(a, b):
    return lax.dot_general(
        a, b, (((1,), (0,)), ((), ())), precision=lax.Precision.HIGHEST, preferred_element_type=F32
    )


def iota(shape, dim):
    return lax.broadcasted_iota(jnp.int32, shape, dim)


def pick_far(x, off):
    rows = iota(x.shape, 0)
    kept = jnp.where((rows & (FAR - 1)) == off, x, 0.0)
    return jnp.sum(kept.reshape(BOTH // FAR, FAR, 128), axis=1)


def repeat_far(x):
    return jnp.broadcast_to(x[:, None, :], (BOTH // FAR, FAR, 128)).reshape(BOTH, 128)


def kernel(
    q_in, k_in, v_in, w_in, go_in, po, fo,
    lo, dq, dk, dv,
    q, k, v, w, go,
    QC, KC, VC, GC, LB, PB, PSND, GOA, GOUT,
    MR, LR, ACC, DQ, DK, DV, STR, STPS, LSR, PSR,
    FX, FY, FS, FS2, FG, FG2, R1S, R2S, FR1, FR2,
    FQNB, FQPB, FRNB, FRPB, FOUT, FM, FL, FACC, FST, CS, CB,
    OB, ORC, RSS, RSR, AGS, AGR, DSND, DRCV, GR, FRM,
    ss, rs, ls,
):
    t = lax.axis_index("seq")
    y = lax.axis_index("head")
    c = t % 2
    chip = t // 2
    odd = chip % 2
    g = chip % 4
    upper = g // 2
    mate = t + 1 - 2 * c
    near = chip + 1 - 2 * odd
    other = chip - g + 2 - 2 * upper
    nchip = lax.axis_size("seq") // 2
    hub_turn = (chip // ZC) % 2
    hub_z = 0
    is_hub = jnp.logical_and(chip % ZC == hub_z, (chip // ZC) // 2 == c)

    def hub_chip(i):
        return ZC * (2 * c + i)

    def rc(src, dst, i, j, dev):
        return pltpu.make_async_remote_copy(
            src_ref=src, dst_ref=dst, send_sem=ss.at[i], recv_sem=rs.at[j],
            device_id=dev, device_id_type=MESH,
        )

    loads = [
        pltpu.make_async_copy(a, b, ls.at[n])
        for n, (a, b) in enumerate(((k_in, k), (v_in, v), (q_in, q), (go_in, go), (w_in, w)))
    ]
    for x in loads:
        x.start()

    bar = pltpu.get_barrier_semaphore()

    def sig(dev):
        pl.semaphore_signal(bar, inc=1, device_id=dev, device_id_type=MESH)

    def from_near(b, n):
        step = (n + 1) // 2
        return ZC * b + (hub_z + jnp.where(n % 2 == 1, ZC - step, step)) % ZC

    @pl.when(is_hub)
    def _():
        @pl.loop(0, nchip)
        def _(n):
            u = from_near(n // ZC, n % ZC)

            @pl.when(u != chip)
            def _():
                sig((2 * u + c, y))

    for d in range(1, 4):
        sig((t, (y + d) % 4))
    sig((mate, y))
    for s in range(2):
        sig((2 * near + s, y))
        for d in range(2):
            sig((2 * (other + d) + s, y))

    off_p = [po[4 * y + 2 * c + i] for i in range(2)]
    off_f = [fo[4 * y + 2 * c + i] for i in range(2)]
    lane = pl.ds(pl.multiple_of(256 * c, 256), 256)
    mine = pl.ds(pl.multiple_of(ROWS * c, ROWS), ROWS)
    theirs = pl.ds(pl.multiple_of(ROWS * (1 - c), ROWS), ROWS)
    mate_lane = pl.ds(pl.multiple_of(256 * (1 - c), 256), 256)

    def one_hot(off):
        return jnp.where(
            iota((64, ROWS), 1) == 2 * iota((64, ROWS), 0) + off, 1.0, 0.0
        ).astype(BF)

    def pair_rows(src, slot):
        for h in range(4):
            e = one_hot(po[4 * y + h])
            cols = slice(128 * h, 128 * h + 128)
            PSND[slot, :, cols] = nn(e, src[:, cols]).astype(BF)

    for x in loads[:3]:
        x.wait()
    own_rows = (iota((8, 128), 0) // 4) == c
    for h in range(4):
        for n, src in enumerate((q, k, v)):
            x = src[:, 128 * h : 128 * h + 128].astype(F32)
            x = jnp.where((iota((ROWS, 128), 0) & (FAR - 1)) == fo[4 * y + h], x, 0.0)
            x = jnp.sum(x.reshape(4, FAR, 128), axis=1)
            x = jnp.where(own_rows, jnp.concatenate([x, x], axis=0), 0.0)
            FX[h // 2, h % 2, n] = x.astype(BF)

    @pl.when(upper == 0)
    def _():
        pair_rows(k, 0)
        pair_rows(v, 1)

    @pl.when(upper == 1)
    def _():
        pair_rows(q, 0)

    for src, dst in ((q, QC), (k, KC), (v, VC)):
        dst[mine, :] = jnp.where(c == 0, src[:, 0:256], src[:, 256:512])

    count = 3 + 1 + 2 + 4
    for i in range(2):
        count = count + jnp.where(chip != hub_chip(i), 1, 0)
    pl.semaphore_wait(bar, count)

    def far_mate():
        return rc(FX.at[1 - c], FY, FMATE, FMATE, (mate, y))

    far_mate().start()
    def y_copy(d):
        return rc(go, GOA.at[y], YG + d - 1, YG + d - 1, (t, (y + d) % 4))

    loads[3].wait()
    for d in (2, 1, 3):
        y_copy(d).start()

    def local_copy(src, n, s):
        return rc(
            src.at[:, 256 * s : 256 * s + 256], LB.at[n, mine, :],
            LOC + 2 * n + s, LOC + 2 * n + c, (2 * near + s, y),
        )

    def pair_copy(n, d, s):
        at = pl.ds(pl.multiple_of(128 * odd + 64 * c, 64), 64)
        return rc(
            PSND.at[n, :, 256 * s : 256 * s + 256], PB.at[n, at, :],
            PAIR + 4 * n + 2 * d + s, PAIR + 4 * n + 2 * odd + c, (2 * (other + d) + s, y),
        )

    far_at = pl.ds(pl.multiple_of(8 * chip, 8), 8)
    far_mate().wait_recv()
    for i in range(2):
        FS[i] = FX[c, i] + FY[i]

    def far_copy(i):
        return rc(FS.at[i], FG.at[:, far_at, :], FA + i, FA, (2 * hub_chip(i) + c, y))

    def far_copy2(i):
        return rc(FS2.at[i], FG2.at[:, far_at, :], FB + i, FB, (2 * hub_chip(i) + c, y))

    for i in range(2):
        @pl.when(chip != hub_chip(i))
        def _(i=i):
            far_copy(i).start()

        @pl.when(chip == hub_chip(i))
        def _(i=i):
            FG[:, far_at, :] = FS[i]

    def ask_near():
        return rc(FS.at[:, 0], FQNB, FQN, FQN, (2 * near + c, y))

    def ask_pair(d):
        return rc(FS.at[:, 0], FQPB.at[odd], FQP + d, FQP + odd, (2 * (other + d) + c, y))

    def tell_near():
        return rc(FOUT.at[2], FRNB, FRN, FRN, (2 * near + c, y))

    def tell_pair(d):
        return rc(FOUT.at[d], FRPB.at[odd], FRP + d, FRP + odd, (2 * (other + d) + c, y))

    @pl.when(odd == 1)
    def _():
        ask_near().start()

    @pl.when(upper == 1)
    def _():
        for d in range(2):
            ask_pair(d).start()

    mate_copies = [
        rc(src.at[:, mate_lane], dst.at[mine, :], PQKV + n, PQKV + n, (mate, y))
        for n, (src, dst) in enumerate(((q, QC), (k, KC), (v, VC)))
    ]
    for x in mate_copies:
        x.start()

    for s in range(2):
        @pl.when(odd == 0)
        def _(s=s):
            local_copy(k, 0, s).start()

        @pl.when(odd == 1)
        def _(s=s):
            local_copy(q, 0, s).start()

    for d in range(2):
        for s in range(2):
            @pl.when(jnp.logical_or(upper == 1, odd == 1))
            def _(d=d, s=s):
                pair_copy(0, d, s).start()

    for x in mate_copies:
        x.wait_recv()

    def answer(slot, i, qq, near_row):
        cols = slice(128 * i, 128 * i + 128)
        match = jnp.logical_and((iota((8, BOTH), 1) & 1) == off_p[i], ((off_f[i] - off_p[i]) & 1) == 0)
        cnt = jnp.where(match, 1.0, 0.0) + near_row
        s = nt(qq, KC[:, cols]) * FACTOR
        s = jnp.where(cnt > 0.0, s, NEG)
        m = jnp.max(s, axis=1, keepdims=True)
        p = cnt * jnp.exp(s - m)
        FOUT[slot, i, 0] = nn(p.astype(BF), VC[:, cols])
        total = jnp.sum(p, axis=1, keepdims=True)
        FOUT[slot, i, 1] = jnp.where(iota((8, 128), 1) == 0, m, total)

    @pl.when(upper == 0)
    def _():
        for d in range(2):
            rc(FS.at[:, 0], FQPB.at[d], FQP, FQP + d, (2 * (other + d) + c, y)).wait_recv()
            for i in range(2):
                answer(d, i, FQPB[d, i], 0.0)
            tell_pair(d).start()

    @pl.when(odd == 0)
    def _():
        ask_near().wait_recv()
        for i in range(2):
            answer(2, i, FQNB[i], 1.0)
        tell_near().start()
        for s in range(2):
            local_copy(v, 1, s).start()

    @pl.when(upper == 0)
    def _():
        for d in range(2):
            for s in range(2):
                @pl.when(odd == 0)
                def _(d=d, s=s):
                    pair_copy(0, d, s).start()

                pair_copy(1, d, s).start()

    loads[4].wait()
    grad = nt(go[...], w[:, pl.ds(pl.multiple_of(512 * y, 512), 512)])
    for d in (1, 3, 2):
        src = (y + 4 - d) % 4
        rc(go, GOA.at[src], YG + d - 1, YG + d - 1, (t, src)).wait_recv()
        grad = grad + nt(GOA[src], w[:, pl.ds(pl.multiple_of(512 * src, 512), 512)])
    GOUT[...] = grad.astype(BF)
    GC[mine, :] = jnp.where(c == 0, GOUT[:, 0:256], GOUT[:, 256:512])

    @pl.when(upper == 1)
    def _():
        pair_rows(GOUT, 1)

    grad_mate = rc(GOUT.at[:, mate_lane], GC.at[mine, :], PGRAD, PGRAD, (mate, y))
    grad_mate.start()

    ri = iota((BOTH, BOTH), 0)
    ci = iota((BOTH, BOTH), 1)

    def own_count(i):
        both = jnp.logical_and((ri & 1) == off_p[i], (ci & 1) == off_p[i])
        return jnp.where(both, 2.0, 1.0)

    def fwd(i, kk, vv, cnt, first=False):
        cols = slice(128 * i, 128 * i + 128)
        s = nt(QC[:, cols], kk) * FACTOR
        s = jnp.where(cnt > 0.0, s, NEG)
        top = jnp.max(s, axis=1, keepdims=True)
        if first:
            m = top
        else:
            m_old = MR[i][:, 0:1]
            m = jnp.maximum(m_old, top)
        p = cnt * jnp.exp(s - m)
        total = jnp.sum(p, axis=1, keepdims=True)
        num = nn(p.astype(BF), vv)
        if not first:
            a = jnp.exp(m_old - m)
            total = total + a * LR[i][:, 0:1]
            num = num + a * ACC[i]
        MR[i] = jnp.broadcast_to(m, (BOTH, 128))
        LR[i] = jnp.broadcast_to(total, (BOTH, 128))
        ACC[i] = num

    for i in range(2):
        cols = slice(128 * i, 128 * i + 128)
        fwd(i, KC[:, cols], VC[:, cols], jnp.where(ri >= ci, own_count(i), 0.0), True)

    for i in range(2):
        FM[i] = pick_far(MR[i], off_f[i])
        FL[i] = pick_far(LR[i], off_f[i])
        FACC[i] = pick_far(ACC[i], off_f[i])

    def join(i, got):
        m_o = FM[i][:, 0:1]
        m_g = got[1][:, 0:1]
        m = jnp.maximum(m_o, m_g)
        a = jnp.exp(m_o - m)
        e = jnp.exp(m_g - m)
        FACC[i] = a * FACC[i] + e * got[0]
        FL[i] = jnp.broadcast_to(a * FL[i][:, 0:1] + e * got[1][:, 1:2], (8, 128))
        FM[i] = jnp.broadcast_to(m, (8, 128))

    @pl.when(odd == 1)
    def _():
        tell_near().wait_recv()
        for i in range(2):
            join(i, FRNB[i])

    @pl.when(upper == 1)
    def _():
        for d in range(2):
            rc(FOUT.at[d], FRPB.at[d], FRP, FRP + d, (2 * (other + d) + c, y)).wait_recv()
            for i in range(2):
                join(i, FRPB[d, i])

    grad_mate.wait_recv()
    l8 = iota((8, 128), 1)
    for i in range(2):
        gf = pick_far(GC[:, 128 * i : 128 * i + 128].astype(F32), off_f[i])
        dn = jnp.sum(gf * FACC[i], axis=1, keepdims=True)
        FS2[i, 0] = gf
        FS2[i, 1] = jnp.where(l8 == 0, FM[i], jnp.where(l8 == 1, FL[i], dn))

    for i in range(2):
        @pl.when(chip != hub_chip(i))
        def _(i=i):
            far_copy2(i).start()

        @pl.when(chip == hub_chip(i))
        def _(i=i):
            FG2[:, far_at, :] = FS2[i]

    @pl.when(odd == 1)
    def _():
        for s in range(2):
            local_copy(GOUT, 1, s).start()

    @pl.when(upper == 1)
    def _():
        for d in range(2):
            for s in range(2):
                pair_copy(1, d, s).start()

    @pl.when(odd == 1)
    def _():
        for n in range(2):
            for s in range(2):
                rc(
                    k.at[:, 0:256], LB.at[n, pl.ds(128 * s, 128), :],
                    LOC + 2 * n, LOC + 2 * n + s, (2 * near + s, y),
                ).wait_recv()
        for i in range(2):
            cols = slice(128 * i, 128 * i + 128)
            fwd(i, LB[0, :, cols], LB[1, :, cols], own_count(i))

    def pair_wait(n, d, s):
        rc(
            PSND.at[n, :, 0:256], PB.at[n, pl.ds(128 * d + 64 * s, 64), :],
            PAIR, PAIR + 4 * n + 2 * d + s, (2 * (other + d) + s, y),
        ).wait_recv()

    def pair_key_count(i, x):
        return jnp.where((x & 1) == off_p[i], 1.0, 0.0)

    @pl.when(upper == 1)
    def _():
        for n in range(2):
            for d in range(2):
                for s in range(2):
                    pair_wait(n, d, s)
        for i in range(2):
            cols = slice(128 * i, 128 * i + 128)
            fwd(i, PB[0, :, cols], PB[1, :, cols], pair_key_count(i, ri))

    for i in range(2):
        OB[:, 128 * i : 128 * i + 128] = (ACC[i] / LR[i]).astype(BF)
    out_mate = rc(OB.at[theirs, :], ORC, POUT, POUT, (mate, y))
    out_mate.start()
    out_mate.wait_recv()
    attended = jnp.where(
        c == 0,
        jnp.concatenate([OB[mine, :], ORC[...]], axis=1),
        jnp.concatenate([ORC[...], OB[mine, :]], axis=1),
    )

    def rs_copy(d, half):
        to = (y + d) % 4
        at = slice(256 * half, 256 * half + 256)
        n = RS + 3 * half + d - 1
        return rc(RSS.at[to, :, at], RSR.at[d - 1, :, at], n, n, (t, to))

    def lanes_of(to, half):
        return pl.ds(pl.multiple_of(512 * to + 256 * half, 256), 256)

    own_parts = []
    for half in range(2):
        for d in (2, 1, 3):
            to = (y + d) % 4
            RSS[to, :, 256 * half : 256 * half + 256] = nn(attended, w[:, lanes_of(to, half)]).astype(BF)
            rs_copy(d, half).start()
        own_parts.append(nn(attended, w[:, lanes_of(y, half)]).astype(BF).astype(F32))

    @pl.when(is_hub)
    def _():
        rest = FG.at[:, pl.ds(0, 8 * (nchip - 1)), :]
        rc(rest, rest, FA, FA, (t, y)).wait_recv()
        lanes = iota((128, 128), 1)
        for b in range(nchip // ZC):
            at, size = slice(128 * b, 128 * b + 128), 128 * b + 128
            s = nt(FG[0, at, :], FG[1, 0:size, :]) * FACTOR
            s = jnp.where(iota((128, size), 0) + 128 * b >= iota((128, size), 1), s, NEG)
            m = jnp.max(s, axis=1, keepdims=True)
            p = jnp.exp(s - m)
            total = jnp.sum(p, axis=1, keepdims=True)
            R1S[0, at, :] = nn(p.astype(BF), FG[2, 0:size, :])
            R1S[1, at, :] = jnp.where(lanes == 0, m, total)

            @pl.loop(0, ZC)
            def _(n, b=b):
                u = from_near(b, n)
                at = pl.ds(pl.multiple_of(8 * u, 8), 8)

                @pl.when(u != chip)
                def _():
                    rc(
                        R1S.at[:, at, :], FR1.at[hub_turn], R1, R1 + hub_turn, (2 * u + c, y)
                    ).start()

        FR1[hub_turn] = R1S[:, far_at, :]

    l128 = iota((BOTH, 128), 1)
    stats = jnp.zeros((BOTH, 128), F32)
    for i in range(2):
        cols = slice(128 * i, 128 * i + 128)

        @pl.when(chip != hub_chip(i))
        def _(i=i):
            rc(R1S.at[:, 0:8, :], FR1.at[i], R1, R1 + i, (2 * hub_chip(i) + c, y)).wait_recv()

        is_far = (iota((BOTH, 1), 0) & (FAR - 1)) == off_f[i]
        num_f = repeat_far(FR1[i, 0])
        st_f = repeat_far(FR1[i, 1])
        m_f = jnp.where(is_far, st_f[:, 0:1], NEG)
        l_f = jnp.where(is_far, st_f[:, 1:2], 0.0)
        m_n = MR[i][:, 0:1]
        m = jnp.maximum(m_n, m_f)
        a = jnp.exp(m_n - m)
        b = jnp.where(is_far, jnp.exp(m_f - m), 0.0)
        total = a * LR[i][:, 0:1] + b * l_f
        out = (a * ACC[i] + b * num_f) / total
        FST[i] = pick_far(out - OB[:, cols].astype(F32), off_f[i])
        lse = m + jnp.log(total)
        delta = jnp.sum(GC[:, cols].astype(F32) * out, axis=1, keepdims=True)
        MR[i] = jnp.broadcast_to(lse, (BOTH, 128))
        LR[i] = jnp.broadcast_to(delta, (BOTH, 128))
        stats = jnp.where(l128 == 2 * i, lse, jnp.where(l128 == 2 * i + 1, delta, stats))

    STR[...] = jnp.transpose(stats)[0:8, :]

    @pl.when(upper == 1)
    def _():
        srow = iota((8, 128), 0)
        parts = []
        for i in range(2):
            e = jnp.where(iota((BOTH, 128), 0) == 2 * iota((BOTH, 128), 1) + off_p[i], 1.0, 0.0)
            parts.append(exact(STR[...], e))
        STPS[...] = jnp.where(srow < 2, parts[0], parts[1])

    def near_stats():
        return rc(STR, LSR, STL, STL, (2 * near + c, y))

    def pair_stats(d):
        at = pl.ds(pl.multiple_of(128 * odd, 128), 128)
        return rc(STPS, PSR.at[:, at], STP + d, STP + odd, (2 * (other + d) + c, y))

    @pl.when(odd == 1)
    def _():
        near_stats().start()

    @pl.when(upper == 1)
    def _():
        for d in range(2):
            pair_stats(d).start()

    fixes = [
        nn(FST[i].astype(BF), w[pl.ds(pl.multiple_of(256 * c + 128 * i, 128), 128), :]) for i in range(2)
    ]
    fix_at = pl.ds(pl.multiple_of(8 * (2 * y + c), 8), 8)
    for s in range(2):
        CS[s] = jnp.concatenate([x[4 * s : 4 * s + 4, :] for x in fixes], axis=0).astype(BF)

    def fix_copy(d, s):
        return rc(
            CS.at[s], CB.at[fix_at, :], FIX + 2 * d + s, FIX + 2 * y + c,
            (2 * chip + s, (y + d) % 4),
        )

    for d in (2, 1, 3):
        for s in range(2):
            fix_copy(d, s).start()
    for s in range(2):
        @pl.when(c == s)
        def _(s=s):
            fix_copy(0, 1 - s).start()
            CB[fix_at, :] = CS[s]

    def ag_copy(d, half):
        at = slice(256 * half, 256 * half + 256)
        n = AG + 3 * half + d - 1
        return rc(AGS.at[:, at], AGR.at[d - 1, :, at], n, n, (t, (y + d) % 4))

    for half in range(2):
        at = slice(256 * half, 256 * half + 256)
        acc = own_parts[half]
        for d in (1, 3, 2):
            rs_copy(d, half).wait_recv()
            acc = acc + RSR[d - 1, :, at].astype(F32)
        AGS[:, at] = acc.astype(BF)
        for d in (2, 1, 3):
            ag_copy(d, half).start()

    def row_side(i, kk, vv, cnt, masked):
        cols = slice(128 * i, 128 * i + 128)
        s = nt(QC[:, cols], kk) * FACTOR
        if masked:
            s = jnp.where(cnt > 0.0, s, NEG)
        p = cnt * jnp.exp(s - MR[i][:, 0:1])
        ds = (p * (nt(GC[:, cols], vv) - LR[i][:, 0:1])).astype(BF)
        return nn(ds, kk)

    def col_side(i, qq, gg, st, cnt, masked):
        cols = slice(128 * i, 128 * i + 128)
        s = nt(KC[:, cols], qq) * FACTOR
        if masked:
            s = jnp.where(cnt > 0.0, s, NEG)
        p = cnt * jnp.exp(s - st[2 * i : 2 * i + 1, :])
        ds = (p * (nt(VC[:, cols], gg) - st[2 * i + 1 : 2 * i + 2, :])).astype(BF)
        return nn(ds, qq), nn(p.astype(BF), gg)

    for i in range(2):
        cols = slice(128 * i, 128 * i + 128)
        DQ[i] = row_side(i, KC[:, cols], VC[:, cols], jnp.where(ri >= ci, own_count(i), 0.0), True)
        DK[i], DV[i] = col_side(
            i, QC[:, cols], GC[:, cols], STR[...], jnp.where(ci >= ri, own_count(i), 0.0), True
        )

    @pl.when(odd == 1)
    def _():
        for i in range(2):
            cols = slice(128 * i, 128 * i + 128)
            DQ[i] += row_side(i, LB[0, :, cols], LB[1, :, cols], own_count(i), False)

    @pl.when(odd == 0)
    def _():
        for n in range(2):
            for s in range(2):
                rc(
                    k.at[:, 0:256], LB.at[n, pl.ds(128 * s, 128), :],
                    LOC + 2 * n, LOC + 2 * n + s, (2 * near + s, y),
                ).wait_recv()
        near_stats().wait_recv()
        for i in range(2):
            cols = slice(128 * i, 128 * i + 128)
            a, b = col_side(i, LB[0, :, cols], LB[1, :, cols], LSR[...], own_count(i), False)
            DK[i] += a
            DV[i] += b

    @pl.when(upper == 1)
    def _():
        for i in range(2):
            cols = slice(128 * i, 128 * i + 128)
            DQ[i] += row_side(i, PB[0, :, cols], PB[1, :, cols], pair_key_count(i, ri), True)

    @pl.when(upper == 0)
    def _():
        for n in range(2):
            for d in range(2):
                for s in range(2):
                    pair_wait(n, d, s)
        for d in range(2):
            rc(
                STPS, PSR.at[:, 128 * d : 128 * d + 128], STP, STP + d, (2 * (other + d) + c, y)
            ).wait_recv()
        for i in range(2):
            cols = slice(128 * i, 128 * i + 128)
            a, b = col_side(
                i, PB[0, :, cols], PB[1, :, cols], PSR[...], pair_key_count(i, ri), True
            )
            DK[i] += a
            DV[i] += b

    for n, (src, scale) in enumerate(((DQ, FACTOR), (DK, FACTOR), (DV, 1.0))):
        full = jnp.concatenate([src[i] * scale for i in range(2)], axis=1)
        DSND[n] = jnp.where(c == 0, full[ROWS:, :], full[:ROWS, :]).astype(BF)
        GR[n] = jnp.where(c == 0, full[:ROWS, :], full[ROWS:, :])
    back = rc(DSND, DRCV, PDQ, PDQ, (mate, y))
    back.start()

    @pl.when(is_hub)
    def _():
        rest = FG2.at[:, pl.ds(0, 8 * (nchip - 1)), :]
        rc(rest, rest, FB, FB, (t, y)).wait_recv()
        rows = []
        lanes = iota((128, 128), 1)
        for b in range(nchip // ZC):
            at = slice(128 * b, 128 * b + 128)
            m_f = R1S[1, at, 0:1]
            l_f = R1S[1, at, 1:2]
            m_n = FG2[1, at, 0:1]
            l_n = FG2[1, at, 1:2]
            d_n = FG2[1, at, 2:3]
            m = jnp.maximum(m_f, m_n)
            a = jnp.exp(m_n - m)
            e = jnp.exp(m_f - m)
            total = a * l_n + e * l_f
            lse = m + jnp.log(total)
            d_f = jnp.sum(FG2[0, at, :] * R1S[0, at, :], axis=1, keepdims=True)
            delta = (a * d_n + e * d_f) / total
            both = jnp.where(lanes == 0, lse, delta)
            FG2[1, at, :] = both
            rows.append(jnp.transpose(both))
        rows = jnp.concatenate([x[0:8, :] for x in rows], axis=1)
        size = FG.shape[1]
        for b in range(nchip // ZC):
            at, end = slice(128 * b, 128 * b + 128), 128 * b + 128
            past, ahead = slice(0, end), slice(128 * b, size)
            lse = FG2[1, at, 0:1]
            delta = FG2[1, at, 1:2]
            lower = iota((128, end), 0) + 128 * b >= iota((128, end), 1)
            s = jnp.where(lower, nt(FG[0, at, :], FG[1, past, :]) * FACTOR, NEG)
            p = jnp.exp(s - lse)
            ds = (p * (nt(FG2[0, at, :].astype(BF), FG[2, past, :]) - delta)).astype(BF)
            R2S[0, at, :] = (nn(ds, FG[1, past, :]) * FACTOR).astype(BF)
            later = iota((128, size - 128 * b), 1) >= iota((128, size - 128 * b), 0)
            s = jnp.where(later, nt(FG[1, at, :], FG[0, ahead, :]) * FACTOR, NEG)
            p = jnp.exp(s - rows[0:1, ahead])
            gb = FG2[0, ahead, :].astype(BF)
            R2S[2, at, :] = nn(p.astype(BF), gb).astype(BF)
            ds = (p * (nt(FG[2, at, :], gb) - rows[1:2, ahead])).astype(BF)
            R2S[1, at, :] = (nn(ds, FG[0, ahead, :]) * FACTOR).astype(BF)

        @pl.loop(0, nchip)
        def _(n):
            u = from_near(n % 4, n // 4)
            at = pl.ds(pl.multiple_of(8 * u, 8), 8)

            @pl.when(u != chip)
            def _():
                rc(R2S.at[:, at, :], FR2.at[hub_turn], R2, R2 + hub_turn, (2 * u + c, y)).start()

        FR2[hub_turn] = R2S[:, far_at, :]

    for i in range(2):
        @pl.when(chip != hub_chip(i))
        def _(i=i):
            rc(R2S.at[:, 0:8, :], FR2.at[i], R2, R2 + i, (2 * hub_chip(i) + c, y)).wait_recv()

    back_far = rc(FR2, FRM, FBK, FBK, (mate, y))
    back_far.start()

    for d in range(4):
        for s in range(2):
            @pl.when(jnp.logical_or(d > 0, s != c))
            def _(d=d, s=s):
                src = (y + 4 - d) % 4
                rc(
                    CS.at[0], CB.at[pl.ds(pl.multiple_of(8 * (2 * src + s), 8), 8), :],
                    FIX, FIX + 2 * src + s, (2 * chip + s, src),
                ).wait_recv()
    kk = iota((ROWS, 64), 1)
    place = jnp.zeros((ROWS, 64), jnp.int32)
    for h in range(16):
        place = jnp.where(kk // 4 == h, fo[h], place)
    place = jnp.where(iota((ROWS, 64), 0) == FAR * (kk & 3) + place, 1.0, 0.0).astype(BF)

    def whole(base, at):
        lo[:, at] = (base.astype(F32) + nn(place, CB[:, at])).astype(BF)

    whole(AGS[...], pl.ds(pl.multiple_of(512 * y, 512), 512))
    for d in (1, 3, 2):
        ag_copy(d, 0).wait_recv()
        ag_copy(d, 1).wait_recv()
        src = (y + 4 - d) % 4
        whole(AGR[d - 1], pl.ds(pl.multiple_of(512 * src, 512), 512))

    def far_rows(tiles, n, cc):
        parts = []
        for i in range(2):
            x = tiles[i, n].astype(F32)
            x = jnp.where(c == 0, x[0:4, :], x[4:8, :])
            x = jnp.broadcast_to(x[:, None, :], (4, FAR, 128)).reshape(ROWS, 128)
            hit = (iota((ROWS, 128), 0) & (FAR - 1)) == fo[4 * y + 2 * cc + i]
            parts.append(jnp.where(hit, x, 0.0))
        return jnp.concatenate(parts, axis=1)

    for n, dst in enumerate((dq, dk, dv)):
        dst[:, lane] = (GR[n] + far_rows(FR2, n, c)).astype(BF)
    back.wait_recv()
    back_far.wait_recv()
    for n, dst in enumerate((dq, dk, dv)):
        dst[:, mate_lane] = (DRCV[n].astype(F32) + far_rows(FRM, n, 1 - c)).astype(BF)

    far_mate().wait_send()
    for x in mate_copies:
        x.wait_send()
    for d in range(1, 4):
        y_copy(d).wait_send()
        for half in range(2):
            rs_copy(d, half).wait_send()
            ag_copy(d, half).wait_send()
    for n in range(2):
        for s in range(2):
            local_copy(k, n, s).wait_send()
            for d in range(2):
                pair_copy(n, d, s).wait_send()
    grad_mate.wait_send()
    out_mate.wait_send()
    back.wait_send()
    back_far.wait_send()
    for i in range(2):
        @pl.when(chip != hub_chip(i))
        def _(i=i):
            far_copy(i).wait_send()
            far_copy2(i).wait_send()

    @pl.when(odd == 1)
    def _():
        near_stats().wait_send()
        ask_near().wait_send()

    @pl.when(odd == 0)
    def _():
        tell_near().wait_send()

    @pl.when(upper == 0)
    def _():
        for d in range(2):
            tell_pair(d).wait_send()

    @pl.when(upper == 1)
    def _():
        for d in range(2):
            pair_stats(d).wait_send()
            ask_pair(d).wait_send()

    for d in range(1, 4):
        for s in range(2):
            fix_copy(d, s).wait_send()
    for s in range(2):
        @pl.when(c == s)
        def _(s=s):
            fix_copy(0, 1 - s).wait_send()

    @pl.when(is_hub)
    def _():
        for sent, n in ((R1S, R1), (R2S, R2)):
            sent = sent.at[:, pl.ds(0, 8 * (nchip - 1)), :]
            rc(sent, sent, n, n, (t, y)).wait_send()


def store(*refs):
    copies = [
        pltpu.make_async_copy(a, b, refs[8].at[n]) for n, (a, b) in enumerate(zip(refs[:4], refs[4:8]))
    ]
    for x in copies:
        x.start()
    for x in copies:
        x.wait()


def local(queries, key_rows, value_rows, out_weight, grad_out, pair_offsets, far_head_offsets):
    vm = pl.BlockSpec(memory_space=pltpu.VMEM)
    sm = pl.BlockSpec(memory_space=pltpu.SMEM)
    rows = jax.ShapeDtypeStruct((ROWS, 512), BF)

    def b(*shape):
        return pltpu.VMEM(shape, BF)

    def f(*shape):
        return pltpu.VMEM(shape, F32)

    outs = pl.pallas_call(
        kernel,
        out_shape=(pltpu.VMEM((ROWS, 2048), BF),) + (pltpu.VMEM((ROWS, 512), BF),) * 3,
        in_specs=[pl.BlockSpec(memory_space=pl.ANY)] * 5 + [sm] * 2,
        out_specs=(vm,) * 4,
        scratch_shapes=[
            b(128, 512), b(128, 512), b(128, 512), b(512, 2048), b(128, 512),
            b(256, 256), b(256, 256), b(256, 256), b(256, 256),
            b(2, 256, 256), b(2, 256, 256), b(2, 64, 512), b(4, 128, 512), b(128, 512),
            f(2, 256, 128), f(2, 256, 128), f(2, 256, 128),
            f(2, 256, 128), f(2, 256, 128), f(2, 256, 128),
            f(8, 256), f(8, 128), f(8, 256), f(8, 256),
            b(2, 2, 3, 8, 128), b(2, 3, 8, 128),
            b(2, 3, 8, 128), f(2, 2, 8, 128), b(3, 512, 128), f(2, 512, 128),
            f(2, 512, 128), b(3, 512, 128), f(2, 2, 8, 128), b(2, 3, 8, 128),
            b(2, 8, 128), b(2, 2, 8, 128), f(2, 2, 8, 128), f(2, 2, 2, 8, 128), f(3, 2, 2, 8, 128),
            f(2, 8, 128), f(2, 8, 128), f(2, 8, 128), f(2, 8, 128),
            b(2, 8, 2048), b(64, 2048),
            b(256, 256), b(128, 256), b(4, 128, 512), b(3, 128, 512),
            b(128, 512), b(3, 128, 512), b(3, 128, 256), b(3, 128, 256), f(3, 128, 256), b(2, 3, 8, 128),
            pltpu.SemaphoreType.DMA((NSEM,)),
            pltpu.SemaphoreType.DMA((NSEM,)),
            pltpu.SemaphoreType.DMA((5,)),
        ],
        compiler_params=pltpu.CompilerParams(collective_id=0, has_side_effects=True),
    )(queries, key_rows, value_rows, out_weight, grad_out, pair_offsets, far_head_offsets)
    return pl.pallas_call(
        store,
        out_shape=(jax.ShapeDtypeStruct((ROWS, 2048), BF), rows, rows, rows),
        in_specs=[vm] * 4,
        out_specs=(pl.BlockSpec(memory_space=pl.ANY),) * 4,
        scratch_shapes=[pltpu.SemaphoreType.DMA((4,))],
    )(*[pltpu.with_memory_space_constraint(x, pltpu.VMEM) for x in outs])


def solution(mesh):
    seq = P("seq", "head")
    return jax.shard_map(
        local,
        mesh=mesh,
        in_specs=(seq, seq, seq, P("head", None), seq, P(), P()),
        out_specs=(P("seq", None), seq, seq, seq),
        check_vma=False,
    )
```

```python
import jax
import jax.numpy as jnp
from jax import lax
from jax.experimental import pallas as pl
from jax.experimental.pallas import tpu as pltpu
from jax.sharding import PartitionSpec as P

MESH = pl.DeviceIdType.MESH
NEG = -1.0e30
F32 = jnp.float32
BF = jnp.bfloat16
FACTOR = 128 ** (-0.5)
ROWS = 128
BOTH = 256
ZC = 16
FAR = 32

PQKV, PGRAD, POUT, PDQ = 0, 3, 4, 5
LOC, PAIR, YG, RS, AG = 6, 10, 18, 21, 54
STL, STP = 27, 28
R1, R2 = 30, 32
FA, FB, FMATE = 34, 36, 38
FQN, FQP, FRN, FRP, FIX, FBK = 39, 40, 42, 43, 45, 53
YF, FGM = 60, 63
NSEM = 64


def nt(a, b):
    return lax.dot_general(a, b, (((1,), (1,)), ((), ())), preferred_element_type=F32)


def nn(a, b):
    return jnp.dot(a, b, preferred_element_type=F32)


def exact(a, b):
    return lax.dot_general(
        a, b, (((1,), (0,)), ((), ())), precision=lax.Precision.HIGHEST, preferred_element_type=F32
    )


def iota(shape, dim):
    return lax.broadcasted_iota(jnp.int32, shape, dim)


def pick_far(x, off):
    rows = iota(x.shape, 0)
    kept = jnp.where((rows & (FAR - 1)) == off, x, 0.0)
    return jnp.sum(kept.reshape(BOTH // FAR, FAR, 128), axis=1)


def repeat_far(x):
    return jnp.broadcast_to(x[:, None, :], (BOTH // FAR, FAR, 128)).reshape(BOTH, 128)


def kernel(
    q_in, k_in, v_in, w_in, go_in, po, fo,
    lo, dq, dk, dv,
    q, k, v, w, go,
    QC, KC, VC, GC, LB, PB, PSND, GOA, GOUT,
    MR, LR, ACC, DQ, DK, DV, STR, STPS, LSR, PSR,
    FX, FY, FS, FS2, FG, FG2, R1S, R2S, FR1, FR2,
    GFS, GFR, DX, DY, FQNB, FQPB, FRNB, FRPB, FOUT, FM, FL, FACC, FST, CS, CB,
    OB, ORC, RSS, RSR, AGS, AGR, DSND, DRCV, GR, FRM,
    ss, rs, ls,
):
    t = lax.axis_index("seq")
    y = lax.axis_index("head")
    c = t % 2
    chip = t // 2
    odd = chip % 2
    g = chip % 4
    zz = chip % ZC
    upper = g // 2
    mate = t + 1 - 2 * c
    near = chip + 1 - 2 * odd
    other = chip - g + 2 - 2 * upper
    nchip = lax.axis_size("seq") // 2
    hub_turn = (chip // ZC) % 2
    hub_z = 0
    is_hub = jnp.logical_and(chip % ZC == hub_z, (chip // ZC) // 2 == c)

    def hub_chip(i):
        return ZC * (2 * c + i)

    def rc(src, dst, i, j, dev):
        return pltpu.make_async_remote_copy(
            src_ref=src, dst_ref=dst, send_sem=ss.at[i], recv_sem=rs.at[j],
            device_id=dev, device_id_type=MESH,
        )

    loads = [
        pltpu.make_async_copy(a, b, ls.at[n])
        for n, (a, b) in enumerate(((k_in, k), (v_in, v), (q_in, q), (go_in, go), (w_in, w)))
    ]
    for x in loads:
        x.start()

    bar = pltpu.get_barrier_semaphore()

    def sig(dev):
        pl.semaphore_signal(bar, inc=1, device_id=dev, device_id_type=MESH)

    def from_near(b, n):
        step = (n + 1) // 2
        return ZC * b + (hub_z + jnp.where(n % 2 == 1, ZC - step, step)) % ZC

    @pl.when(is_hub)
    def _():
        @pl.loop(0, nchip)
        def _(n):
            u = from_near(n // ZC, n % ZC)

            @pl.when(u != chip)
            def _():
                sig((2 * u + c, y))

    for d in range(1, 4):
        sig((t, (y + d) % 4))
    sig((mate, y))
    for s in range(2):
        sig((2 * near + s, y))
        for d in range(2):
            sig((2 * (other + d) + s, y))

    off_p = [po[4 * y + 2 * c + i] for i in range(2)]
    off_f = [fo[4 * y + 2 * c + i] for i in range(2)]
    lane = pl.ds(pl.multiple_of(256 * c, 256), 256)
    mine = pl.ds(pl.multiple_of(ROWS * c, ROWS), ROWS)
    theirs = pl.ds(pl.multiple_of(ROWS * (1 - c), ROWS), ROWS)
    mate_lane = pl.ds(pl.multiple_of(256 * (1 - c), 256), 256)

    def one_hot(off):
        return jnp.where(
            iota((64, ROWS), 1) == 2 * iota((64, ROWS), 0) + off, 1.0, 0.0
        ).astype(BF)

    def pair_rows(src, slot):
        for h in range(4):
            e = one_hot(po[4 * y + h])
            cols = slice(128 * h, 128 * h + 128)
            PSND[slot, :, cols] = nn(e, src[:, cols]).astype(BF)

    for x in loads[:3]:
        x.wait()
    own_rows = (iota((8, 128), 0) // 4) == c
    for h in range(4):
        for n, src in enumerate((q, k, v)):
            x = src[:, 128 * h : 128 * h + 128].astype(F32)
            x = jnp.where((iota((ROWS, 128), 0) & (FAR - 1)) == fo[4 * y + h], x, 0.0)
            x = jnp.sum(x.reshape(4, FAR, 128), axis=1)
            x = jnp.where(own_rows, jnp.concatenate([x, x], axis=0), 0.0)
            FX[h // 2, h % 2, n] = x.astype(BF)

    @pl.when(upper == 0)
    def _():
        pair_rows(k, 0)
        pair_rows(v, 1)

    @pl.when(upper == 1)
    def _():
        pair_rows(q, 0)

    for src, dst in ((q, QC), (k, KC), (v, VC)):
        dst[mine, :] = jnp.where(c == 0, src[:, 0:256], src[:, 256:512])

    loads[3].wait()
    for d in range(4):
        to = (y + d) % 4
        r16 = iota((16, ROWS), 0)
        at = jnp.zeros((16, ROWS), jnp.int32)
        for h in range(4):
            at = jnp.where(r16 // 4 == h, fo[4 * to + h], at)
        e = jnp.where(iota((16, ROWS), 1) == FAR * (r16 & 3) + at, 1.0, 0.0).astype(BF)
        GFS[to] = nn(e, go[...]).astype(BF)

    count = 3 + 1 + 2 + 4
    for i in range(2):
        count = count + jnp.where(chip != hub_chip(i), 1, 0)
    pl.semaphore_wait(bar, count)

    def far_mate():
        return rc(FX.at[1 - c], FY, FMATE, FMATE, (mate, y))

    far_mate().start()

    def y_copy(d):
        return rc(go, GOA.at[y], YG + d - 1, YG + d - 1, (t, (y + d) % 4))

    def y_far(d):
        return rc(GFS.at[(y + d) % 4], GFR.at[y], YF + d - 1, YF + d - 1, (t, (y + d) % 4))

    for d in (2, 1, 3):
        y_far(d).start()
    for d in (2, 1, 3):
        y_copy(d).start()

    def local_copy(src, n, s):
        return rc(
            src.at[:, 256 * s : 256 * s + 256], LB.at[n, mine, :],
            LOC + 2 * n + s, LOC + 2 * n + c, (2 * near + s, y),
        )

    def pair_copy(n, d, s):
        at = pl.ds(pl.multiple_of(128 * odd + 64 * c, 64), 64)
        return rc(
            PSND.at[n, :, 256 * s : 256 * s + 256], PB.at[n, at, :],
            PAIR + 4 * n + 2 * d + s, PAIR + 4 * n + 2 * odd + c, (2 * (other + d) + s, y),
        )

    far_at = pl.ds(pl.multiple_of(8 * chip, 8), 8)
    far_mate().wait_recv()
    for i in range(2):
        FS[i] = FX[c, i] + FY[i]

    def far_copy(i):
        return rc(FS.at[i], FG.at[:, far_at, :], FA + i, FA, (2 * hub_chip(i) + c, y))

    def far_copy2(i):
        return rc(FS2.at[i], FG2.at[:, far_at, :], FB + i, FB, (2 * hub_chip(i) + c, y))

    for i in range(2):
        @pl.when(chip != hub_chip(i))
        def _(i=i):
            far_copy(i).start()

        @pl.when(chip == hub_chip(i))
        def _(i=i):
            FG[:, far_at, :] = FS[i]

    def ask_near():
        return rc(FS.at[:, 0], FQNB, FQN, FQN, (2 * near + c, y))

    def ask_pair(d):
        return rc(FS.at[:, 0], FQPB.at[odd], FQP + d, FQP + odd, (2 * (other + d) + c, y))

    def tell_near():
        return rc(FOUT.at[2], FRNB, FRN, FRN, (2 * near + c, y))

    def tell_pair(d):
        return rc(FOUT.at[d], FRPB.at[odd], FRP + d, FRP + odd, (2 * (other + d) + c, y))

    @pl.when(odd == 1)
    def _():
        ask_near().start()

    @pl.when(upper == 1)
    def _():
        for d in range(2):
            ask_pair(d).start()

    mate_copies = [
        rc(src.at[:, mate_lane], dst.at[mine, :], PQKV + n, PQKV + n, (mate, y))
        for n, (src, dst) in enumerate(((q, QC), (k, KC), (v, VC)))
    ]
    for x in mate_copies:
        x.start()

    for s in range(2):
        @pl.when(odd == 0)
        def _(s=s):
            local_copy(k, 0, s).start()

        @pl.when(odd == 1)
        def _(s=s):
            local_copy(q, 0, s).start()

    for d in range(2):
        for s in range(2):
            @pl.when(jnp.logical_or(upper == 1, odd == 1))
            def _(d=d, s=s):
                pair_copy(0, d, s).start()

    for x in mate_copies:
        x.wait_recv()

    def answer(slot, i, qq, near_row):
        cols = slice(128 * i, 128 * i + 128)
        match = jnp.logical_and((iota((8, BOTH), 1) & 1) == off_p[i], ((off_f[i] - off_p[i]) & 1) == 0)
        cnt = jnp.where(match, 1.0, 0.0) + near_row
        s = nt(qq, KC[:, cols]) * FACTOR
        s = jnp.where(cnt > 0.0, s, NEG)
        m = jnp.max(s, axis=1, keepdims=True)
        p = cnt * jnp.exp(s - m)
        FOUT[slot, i, 0] = nn(p.astype(BF), VC[:, cols])
        total = jnp.sum(p, axis=1, keepdims=True)
        FOUT[slot, i, 1] = jnp.where(iota((8, 128), 1) == 0, m, total)

    @pl.when(upper == 0)
    def _():
        for d in range(2):
            rc(FS.at[:, 0], FQPB.at[d], FQP, FQP + d, (2 * (other + d) + c, y)).wait_recv()
            for i in range(2):
                answer(d, i, FQPB[d, i], 0.0)
            tell_pair(d).start()

    @pl.when(odd == 0)
    def _():
        ask_near().wait_recv()
        for i in range(2):
            answer(2, i, FQNB[i], 1.0)
        tell_near().start()
        for s in range(2):
            local_copy(v, 1, s).start()

    @pl.when(upper == 0)
    def _():
        for d in range(2):
            for s in range(2):
                @pl.when(jnp.logical_and(odd == 0, zz != 8))
                def _(d=d, s=s):
                    pair_copy(0, d, s).start()

                @pl.when(jnp.logical_or(odd == 1, zz != 8))
                def _(d=d, s=s):
                    pair_copy(1, d, s).start()

    for i in range(2):
        cols = slice(128 * i, 128 * i + 128)
        at, to = iota((8, BOTH), 1), FAR * iota((8, BOTH), 0) + off_f[i]
        match = jnp.logical_and((at & 1) == off_p[i], (to & 1) == off_p[i])
        cnt = jnp.where(at <= to, jnp.where(match, 2.0, 1.0), 0.0)
        s = jnp.where(cnt > 0.0, nt(FS[i, 0], KC[:, cols]) * FACTOR, NEG)
        m = jnp.max(s, axis=1, keepdims=True)
        p = cnt * jnp.exp(s - m)
        FACC[i] = nn(p.astype(BF), VC[:, cols])
        FL[i] = jnp.broadcast_to(jnp.sum(p, axis=1, keepdims=True), (8, 128))
        FM[i] = jnp.broadcast_to(m, (8, 128))

    loads[4].wait()
    part = nt(GFS[y], w[:, pl.ds(pl.multiple_of(512 * y, 512), 512)])
    for d in (1, 3, 2):
        src = (y + 4 - d) % 4
        rc(GFS.at[0], GFR.at[src], YF + d - 1, YF + d - 1, (t, src)).wait_recv()
        part = part + nt(GFR[src], w[:, pl.ds(pl.multiple_of(512 * src, 512), 512)])
    for h in range(4):
        x = part[4 * h : 4 * h + 4, 128 * h : 128 * h + 128]
        x = jnp.where(own_rows, jnp.concatenate([x, x], axis=0), 0.0)
        DX[h // 2, h % 2] = x.astype(BF)

    def far_grad_mate():
        return rc(DX.at[1 - c], DY, FGM, FGM, (mate, y))

    far_grad_mate().start()

    ri = iota((BOTH, BOTH), 0)
    ci = iota((BOTH, BOTH), 1)

    def own_count(i):
        both = jnp.logical_and((ri & 1) == off_p[i], (ci & 1) == off_p[i])
        return jnp.where(both, 2.0, 1.0)

    def fwd(i, kk, vv, cnt, first=False):
        cols = slice(128 * i, 128 * i + 128)
        s = nt(QC[:, cols], kk) * FACTOR
        s = jnp.where(cnt > 0.0, s, NEG)
        top = jnp.max(s, axis=1, keepdims=True)
        if first:
            m = top
        else:
            m_old = MR[i][:, 0:1]
            m = jnp.maximum(m_old, top)
        p = cnt * jnp.exp(s - m)
        total = jnp.sum(p, axis=1, keepdims=True)
        num = nn(p.astype(BF), vv)
        if not first:
            a = jnp.exp(m_old - m)
            total = total + a * LR[i][:, 0:1]
            num = num + a * ACC[i]
        MR[i] = jnp.broadcast_to(m, (BOTH, 128))
        LR[i] = jnp.broadcast_to(total, (BOTH, 128))
        ACC[i] = num

    for i in range(2):
        cols = slice(128 * i, 128 * i + 128)
        fwd(i, KC[:, cols], VC[:, cols], jnp.where(ri >= ci, own_count(i), 0.0), True)

    def join(i, got):
        m_o = FM[i][:, 0:1]
        m_g = got[1][:, 0:1]
        m = jnp.maximum(m_o, m_g)
        a = jnp.exp(m_o - m)
        e = jnp.exp(m_g - m)
        FACC[i] = a * FACC[i] + e * got[0]
        FL[i] = jnp.broadcast_to(a * FL[i][:, 0:1] + e * got[1][:, 1:2], (8, 128))
        FM[i] = jnp.broadcast_to(m, (8, 128))

    @pl.when(odd == 1)
    def _():
        tell_near().wait_recv()
        for i in range(2):
            join(i, FRNB[i])

    @pl.when(upper == 1)
    def _():
        for d in range(2):
            rc(FOUT.at[d], FRPB.at[d], FRP, FRP + d, (2 * (other + d) + c, y)).wait_recv()
            for i in range(2):
                join(i, FRPB[d, i])

    far_grad_mate().wait_recv()
    l8 = iota((8, 128), 1)
    for i in range(2):
        gf = DX[c, i].astype(F32) + DY[i].astype(F32)
        dn = jnp.sum(gf * FACC[i], axis=1, keepdims=True)
        FS2[i, 0] = gf
        FS2[i, 1] = jnp.where(l8 == 0, FM[i], jnp.where(l8 == 1, FL[i], dn))

    for i in range(2):
        @pl.when(chip != hub_chip(i))
        def _(i=i):
            far_copy2(i).start()

        @pl.when(chip == hub_chip(i))
        def _(i=i):
            FG2[:, far_at, :] = FS2[i]

    grad = nt(go[...], w[:, pl.ds(pl.multiple_of(512 * y, 512), 512)])
    for d in (1, 3, 2):
        src = (y + 4 - d) % 4
        rc(go, GOA.at[src], YG + d - 1, YG + d - 1, (t, src)).wait_recv()
        grad = grad + nt(GOA[src], w[:, pl.ds(pl.multiple_of(512 * src, 512), 512)])
    GOUT[...] = grad.astype(BF)
    GC[mine, :] = jnp.where(c == 0, GOUT[:, 0:256], GOUT[:, 256:512])

    @pl.when(upper == 1)
    def _():
        pair_rows(GOUT, 1)

    grad_mate = rc(GOUT.at[:, mate_lane], GC.at[mine, :], PGRAD, PGRAD, (mate, y))
    grad_mate.start()

    @pl.when(odd == 1)
    def _():
        for s in range(2):
            local_copy(GOUT, 1, s).start()

    @pl.when(zz == 8)
    def _():
        for d in range(2):
            for s in range(2):
                pair_copy(0, d, s).start()

    @pl.when(jnp.logical_or(upper == 1, zz == 8))
    def _():
        for d in range(2):
            for s in range(2):
                pair_copy(1, d, s).start()

    @pl.when(odd == 1)
    def _():
        for n in range(2):
            for s in range(2):
                rc(
                    k.at[:, 0:256], LB.at[n, pl.ds(128 * s, 128), :],
                    LOC + 2 * n, LOC + 2 * n + s, (2 * near + s, y),
                ).wait_recv()
        for i in range(2):
            cols = slice(128 * i, 128 * i + 128)
            fwd(i, LB[0, :, cols], LB[1, :, cols], own_count(i))

    def pair_wait(n, d, s):
        rc(
            PSND.at[n, :, 0:256], PB.at[n, pl.ds(128 * d + 64 * s, 64), :],
            PAIR, PAIR + 4 * n + 2 * d + s, (2 * (other + d) + s, y),
        ).wait_recv()

    def pair_key_count(i, x):
        return jnp.where((x & 1) == off_p[i], 1.0, 0.0)

    @pl.when(upper == 1)
    def _():
        for n in range(2):
            for d in range(2):
                for s in range(2):
                    pair_wait(n, d, s)
        for i in range(2):
            cols = slice(128 * i, 128 * i + 128)
            fwd(i, PB[0, :, cols], PB[1, :, cols], pair_key_count(i, ri))

    for i in range(2):
        OB[:, 128 * i : 128 * i + 128] = (ACC[i] / LR[i]).astype(BF)
    out_mate = rc(OB.at[theirs, :], ORC, POUT, POUT, (mate, y))
    out_mate.start()
    out_mate.wait_recv()
    attended = jnp.where(
        c == 0,
        jnp.concatenate([OB[mine, :], ORC[...]], axis=1),
        jnp.concatenate([ORC[...], OB[mine, :]], axis=1),
    )

    def rs_copy(d, half):
        to = (y + d) % 4
        at = slice(256 * half, 256 * half + 256)
        n = RS + 3 * half + d - 1
        return rc(RSS.at[to, :, at], RSR.at[d - 1, :, at], n, n, (t, to))

    def lanes_of(to, half):
        return pl.ds(pl.multiple_of(512 * to + 256 * half, 256), 256)

    own_parts = []
    for half in range(2):
        for d in (2, 1, 3):
            to = (y + d) % 4
            RSS[to, :, 256 * half : 256 * half + 256] = nn(attended, w[:, lanes_of(to, half)]).astype(BF)
            rs_copy(d, half).start()
        own_parts.append(nn(attended, w[:, lanes_of(y, half)]).astype(BF).astype(F32))

    @pl.when(is_hub)
    def _():
        rest = FG.at[:, pl.ds(0, 8 * (nchip - 1)), :]
        rc(rest, rest, FA, FA, (t, y)).wait_recv()
        lanes = iota((128, 128), 1)
        for b in range(nchip // ZC):
            at, size = slice(128 * b, 128 * b + 128), 128 * b + 128
            s = nt(FG[0, at, :], FG[1, 0:size, :]) * FACTOR
            s = jnp.where(iota((128, size), 0) + 128 * b >= iota((128, size), 1), s, NEG)
            m = jnp.max(s, axis=1, keepdims=True)
            p = jnp.exp(s - m)
            total = jnp.sum(p, axis=1, keepdims=True)
            R1S[0, at, :] = nn(p.astype(BF), FG[2, 0:size, :])
            R1S[1, at, :] = jnp.where(lanes == 0, m, total)

            @pl.loop(0, ZC)
            def _(n, b=b):
                u = from_near(b, n)
                at = pl.ds(pl.multiple_of(8 * u, 8), 8)

                @pl.when(u != chip)
                def _():
                    rc(
                        R1S.at[:, at, :], FR1.at[hub_turn], R1, R1 + hub_turn, (2 * u + c, y)
                    ).start()

        FR1[hub_turn] = R1S[:, far_at, :]

    grad_mate.wait_recv()
    l128 = iota((BOTH, 128), 1)
    stats = jnp.zeros((BOTH, 128), F32)
    for i in range(2):
        cols = slice(128 * i, 128 * i + 128)

        @pl.when(chip != hub_chip(i))
        def _(i=i):
            rc(R1S.at[:, 0:8, :], FR1.at[i], R1, R1 + i, (2 * hub_chip(i) + c, y)).wait_recv()

        is_far = (iota((BOTH, 1), 0) & (FAR - 1)) == off_f[i]
        num_f = repeat_far(FR1[i, 0])
        st_f = repeat_far(FR1[i, 1])
        m_f = jnp.where(is_far, st_f[:, 0:1], NEG)
        l_f = jnp.where(is_far, st_f[:, 1:2], 0.0)
        m_n = MR[i][:, 0:1]
        m = jnp.maximum(m_n, m_f)
        a = jnp.exp(m_n - m)
        b = jnp.where(is_far, jnp.exp(m_f - m), 0.0)
        total = a * LR[i][:, 0:1] + b * l_f
        out = (a * ACC[i] + b * num_f) / total
        FST[i] = pick_far(out - OB[:, cols].astype(F32), off_f[i])
        lse = m + jnp.log(total)
        delta = jnp.sum(GC[:, cols].astype(F32) * out, axis=1, keepdims=True)
        MR[i] = jnp.broadcast_to(lse, (BOTH, 128))
        LR[i] = jnp.broadcast_to(delta, (BOTH, 128))
        stats = jnp.where(l128 == 2 * i, lse, jnp.where(l128 == 2 * i + 1, delta, stats))

    STR[...] = jnp.transpose(stats)[0:8, :]

    @pl.when(upper == 1)
    def _():
        srow = iota((8, 128), 0)
        parts = []
        for i in range(2):
            e = jnp.where(iota((BOTH, 128), 0) == 2 * iota((BOTH, 128), 1) + off_p[i], 1.0, 0.0)
            parts.append(exact(STR[...], e))
        STPS[...] = jnp.where(srow < 2, parts[0], parts[1])

    def near_stats():
        return rc(STR, LSR, STL, STL, (2 * near + c, y))

    def pair_stats(d):
        at = pl.ds(pl.multiple_of(128 * odd, 128), 128)
        return rc(STPS, PSR.at[:, at], STP + d, STP + odd, (2 * (other + d) + c, y))

    @pl.when(odd == 1)
    def _():
        near_stats().start()

    @pl.when(upper == 1)
    def _():
        for d in range(2):
            pair_stats(d).start()

    fixes = [
        nn(FST[i].astype(BF), w[pl.ds(pl.multiple_of(256 * c + 128 * i, 128), 128), :]) for i in range(2)
    ]
    fix_at = pl.ds(pl.multiple_of(8 * (2 * y + c), 8), 8)
    for s in range(2):
        CS[s] = jnp.concatenate([x[4 * s : 4 * s + 4, :] for x in fixes], axis=0).astype(BF)

    def fix_copy(d, s):
        return rc(
            CS.at[s], CB.at[fix_at, :], FIX + 2 * d + s, FIX + 2 * y + c,
            (2 * chip + s, (y + d) % 4),
        )

    for d in (2, 1, 3):
        for s in range(2):
            fix_copy(d, s).start()
    for s in range(2):
        @pl.when(c == s)
        def _(s=s):
            fix_copy(0, 1 - s).start()
            CB[fix_at, :] = CS[s]

    def ag_copy(d, half):
        at = slice(256 * half, 256 * half + 256)
        n = AG + 3 * half + d - 1
        return rc(AGS.at[:, at], AGR.at[d - 1, :, at], n, n, (t, (y + d) % 4))

    for half in range(2):
        at = slice(256 * half, 256 * half + 256)
        acc = own_parts[half]
        for d in (1, 3, 2):
            rs_copy(d, half).wait_recv()
            acc = acc + RSR[d - 1, :, at].astype(F32)
        AGS[:, at] = acc.astype(BF)
        for d in (2, 1, 3):
            ag_copy(d, half).start()

    def row_side(i, kk, vv, cnt, masked):
        cols = slice(128 * i, 128 * i + 128)
        s = nt(QC[:, cols], kk) * FACTOR
        if masked:
            s = jnp.where(cnt > 0.0, s, NEG)
        p = cnt * jnp.exp(s - MR[i][:, 0:1])
        ds = (p * (nt(GC[:, cols], vv) - LR[i][:, 0:1])).astype(BF)
        return nn(ds, kk)

    def col_side(i, qq, gg, st, cnt, masked):
        cols = slice(128 * i, 128 * i + 128)
        s = nt(KC[:, cols], qq) * FACTOR
        if masked:
            s = jnp.where(cnt > 0.0, s, NEG)
        p = cnt * jnp.exp(s - st[2 * i : 2 * i + 1, :])
        ds = (p * (nt(VC[:, cols], gg) - st[2 * i + 1 : 2 * i + 2, :])).astype(BF)
        return nn(ds, qq), nn(p.astype(BF), gg)

    for i in range(2):
        cols = slice(128 * i, 128 * i + 128)
        DQ[i] = row_side(i, KC[:, cols], VC[:, cols], jnp.where(ri >= ci, own_count(i), 0.0), True)
        DK[i], DV[i] = col_side(
            i, QC[:, cols], GC[:, cols], STR[...], jnp.where(ci >= ri, own_count(i), 0.0), True
        )

    @pl.when(is_hub)
    def _():
        rest = FG2.at[:, pl.ds(0, 8 * (nchip - 1)), :]
        rc(rest, rest, FB, FB, (t, y)).wait_recv()
        rows = []
        lanes = iota((128, 128), 1)
        for b in range(nchip // ZC):
            at = slice(128 * b, 128 * b + 128)
            m_f = R1S[1, at, 0:1]
            l_f = R1S[1, at, 1:2]
            m_n = FG2[1, at, 0:1]
            l_n = FG2[1, at, 1:2]
            d_n = FG2[1, at, 2:3]
            m = jnp.maximum(m_f, m_n)
            a = jnp.exp(m_n - m)
            e = jnp.exp(m_f - m)
            total = a * l_n + e * l_f
            lse = m + jnp.log(total)
            d_f = jnp.sum(FG2[0, at, :] * R1S[0, at, :], axis=1, keepdims=True)
            delta = (a * d_n + e * d_f) / total
            both = jnp.where(lanes == 0, lse, delta)
            FG2[1, at, :] = both
            rows.append(jnp.transpose(both))
        rows = jnp.concatenate([x[0:8, :] for x in rows], axis=1)
        size = FG.shape[1]
        for b in range(nchip // ZC):
            at, end = slice(128 * b, 128 * b + 128), 128 * b + 128
            past, ahead = slice(0, end), slice(128 * b, size)
            lse = FG2[1, at, 0:1]
            delta = FG2[1, at, 1:2]
            lower = iota((128, end), 0) + 128 * b >= iota((128, end), 1)
            s = jnp.where(lower, nt(FG[0, at, :], FG[1, past, :]) * FACTOR, NEG)
            p = jnp.exp(s - lse)
            ds = (p * (nt(FG2[0, at, :].astype(BF), FG[2, past, :]) - delta)).astype(BF)
            R2S[0, at, :] = (nn(ds, FG[1, past, :]) * FACTOR).astype(BF)
            later = iota((128, size - 128 * b), 1) >= iota((128, size - 128 * b), 0)
            s = jnp.where(later, nt(FG[1, at, :], FG[0, ahead, :]) * FACTOR, NEG)
            p = jnp.exp(s - rows[0:1, ahead])
            gb = FG2[0, ahead, :].astype(BF)
            R2S[2, at, :] = nn(p.astype(BF), gb).astype(BF)
            ds = (p * (nt(FG[2, at, :], gb) - rows[1:2, ahead])).astype(BF)
            R2S[1, at, :] = (nn(ds, FG[0, ahead, :]) * FACTOR).astype(BF)

        @pl.loop(0, nchip)
        def _(n):
            u = from_near(n % 4, n // 4)
            at = pl.ds(pl.multiple_of(8 * u, 8), 8)

            @pl.when(u != chip)
            def _():
                rc(R2S.at[:, at, :], FR2.at[hub_turn], R2, R2 + hub_turn, (2 * u + c, y)).start()

        FR2[hub_turn] = R2S[:, far_at, :]

    @pl.when(odd == 1)
    def _():
        for i in range(2):
            cols = slice(128 * i, 128 * i + 128)
            DQ[i] += row_side(i, LB[0, :, cols], LB[1, :, cols], own_count(i), False)

    @pl.when(odd == 0)
    def _():
        for n in range(2):
            for s in range(2):
                rc(
                    k.at[:, 0:256], LB.at[n, pl.ds(128 * s, 128), :],
                    LOC + 2 * n, LOC + 2 * n + s, (2 * near + s, y),
                ).wait_recv()
        near_stats().wait_recv()
        for i in range(2):
            cols = slice(128 * i, 128 * i + 128)
            a, b = col_side(i, LB[0, :, cols], LB[1, :, cols], LSR[...], own_count(i), False)
            DK[i] += a
            DV[i] += b

    @pl.when(upper == 1)
    def _():
        for i in range(2):
            cols = slice(128 * i, 128 * i + 128)
            DQ[i] += row_side(i, PB[0, :, cols], PB[1, :, cols], pair_key_count(i, ri), True)

    @pl.when(upper == 0)
    def _():
        for n in range(2):
            for d in range(2):
                for s in range(2):
                    pair_wait(n, d, s)
        for d in range(2):
            rc(
                STPS, PSR.at[:, 128 * d : 128 * d + 128], STP, STP + d, (2 * (other + d) + c, y)
            ).wait_recv()
        for i in range(2):
            cols = slice(128 * i, 128 * i + 128)
            a, b = col_side(
                i, PB[0, :, cols], PB[1, :, cols], PSR[...], pair_key_count(i, ri), True
            )
            DK[i] += a
            DV[i] += b

    for n, (src, scale) in enumerate(((DQ, FACTOR), (DK, FACTOR), (DV, 1.0))):
        full = jnp.concatenate([src[i] * scale for i in range(2)], axis=1)
        DSND[n] = jnp.where(c == 0, full[ROWS:, :], full[:ROWS, :]).astype(BF)
        GR[n] = jnp.where(c == 0, full[:ROWS, :], full[ROWS:, :])
    back = rc(DSND, DRCV, PDQ, PDQ, (mate, y))
    back.start()

    for i in range(2):
        @pl.when(chip != hub_chip(i))
        def _(i=i):
            rc(R2S.at[:, 0:8, :], FR2.at[i], R2, R2 + i, (2 * hub_chip(i) + c, y)).wait_recv()

    back_far = rc(FR2, FRM, FBK, FBK, (mate, y))
    back_far.start()

    def far_rows(tiles, n, cc):
        parts = []
        for i in range(2):
            x = tiles[i, n].astype(F32)
            x = jnp.where(c == 0, x[0:4, :], x[4:8, :])
            x = jnp.broadcast_to(x[:, None, :], (4, FAR, 128)).reshape(ROWS, 128)
            hit = (iota((ROWS, 128), 0) & (FAR - 1)) == fo[4 * y + 2 * cc + i]
            parts.append(jnp.where(hit, x, 0.0))
        return jnp.concatenate(parts, axis=1)

    for n, dst in enumerate((dq, dk, dv)):
        dst[:, lane] = (GR[n] + far_rows(FR2, n, c)).astype(BF)
    for d in range(4):
        for s in range(2):
            @pl.when(jnp.logical_or(d > 0, s != c))
            def _(d=d, s=s):
                src = (y + 4 - d) % 4
                rc(
                    CS.at[0], CB.at[pl.ds(pl.multiple_of(8 * (2 * src + s), 8), 8), :],
                    FIX, FIX + 2 * src + s, (2 * chip + s, src),
                ).wait_recv()
    kk = iota((ROWS, 64), 1)
    place = jnp.zeros((ROWS, 64), jnp.int32)
    for h in range(16):
        place = jnp.where(kk // 4 == h, fo[h], place)
    place = jnp.where(iota((ROWS, 64), 0) == FAR * (kk & 3) + place, 1.0, 0.0).astype(BF)

    def whole(base, at):
        lo[:, at] = (base.astype(F32) + nn(place, CB[:, at])).astype(BF)

    whole(AGS[...], pl.ds(pl.multiple_of(512 * y, 512), 512))
    for d in (1, 3, 2):
        ag_copy(d, 0).wait_recv()
        ag_copy(d, 1).wait_recv()
        src = (y + 4 - d) % 4
        whole(AGR[d - 1], pl.ds(pl.multiple_of(512 * src, 512), 512))

    back.wait_recv()
    back_far.wait_recv()
    for n, dst in enumerate((dq, dk, dv)):
        dst[:, mate_lane] = (DRCV[n].astype(F32) + far_rows(FRM, n, 1 - c)).astype(BF)

    far_mate().wait_send()
    far_grad_mate().wait_send()
    for x in mate_copies:
        x.wait_send()
    for d in range(1, 4):
        y_copy(d).wait_send()
        y_far(d).wait_send()
        for half in range(2):
            rs_copy(d, half).wait_send()
            ag_copy(d, half).wait_send()
    for n in range(2):
        for s in range(2):
            local_copy(k, n, s).wait_send()
            for d in range(2):
                pair_copy(n, d, s).wait_send()
    grad_mate.wait_send()
    out_mate.wait_send()
    back.wait_send()
    back_far.wait_send()
    for i in range(2):
        @pl.when(chip != hub_chip(i))
        def _(i=i):
            far_copy(i).wait_send()
            far_copy2(i).wait_send()

    @pl.when(odd == 1)
    def _():
        near_stats().wait_send()
        ask_near().wait_send()

    @pl.when(odd == 0)
    def _():
        tell_near().wait_send()

    @pl.when(upper == 0)
    def _():
        for d in range(2):
            tell_pair(d).wait_send()

    @pl.when(upper == 1)
    def _():
        for d in range(2):
            pair_stats(d).wait_send()
            ask_pair(d).wait_send()

    for d in range(1, 4):
        for s in range(2):
            fix_copy(d, s).wait_send()
    for s in range(2):
        @pl.when(c == s)
        def _(s=s):
            fix_copy(0, 1 - s).wait_send()

    @pl.when(is_hub)
    def _():
        for sent, n in ((R1S, R1), (R2S, R2)):
            sent = sent.at[:, pl.ds(0, 8 * (nchip - 1)), :]
            rc(sent, sent, n, n, (t, y)).wait_send()


def store(*refs):
    copies = [
        pltpu.make_async_copy(a, b, refs[8].at[n]) for n, (a, b) in enumerate(zip(refs[:4], refs[4:8]))
    ]
    for x in copies:
        x.start()
    for x in copies:
        x.wait()


def local(queries, key_rows, value_rows, out_weight, grad_out, pair_offsets, far_head_offsets):
    vm = pl.BlockSpec(memory_space=pltpu.VMEM)
    sm = pl.BlockSpec(memory_space=pltpu.SMEM)
    rows = jax.ShapeDtypeStruct((ROWS, 512), BF)

    def b(*shape):
        return pltpu.VMEM(shape, BF)

    def f(*shape):
        return pltpu.VMEM(shape, F32)

    outs = pl.pallas_call(
        kernel,
        out_shape=(pltpu.VMEM((ROWS, 2048), BF),) + (pltpu.VMEM((ROWS, 512), BF),) * 3,
        in_specs=[pl.BlockSpec(memory_space=pl.ANY)] * 5 + [sm] * 2,
        out_specs=(vm,) * 4,
        scratch_shapes=[
            b(128, 512), b(128, 512), b(128, 512), b(512, 2048), b(128, 512),
            b(256, 256), b(256, 256), b(256, 256), b(256, 256),
            b(2, 256, 256), b(2, 256, 256), b(2, 64, 512), b(4, 128, 512), b(128, 512),
            f(2, 256, 128), f(2, 256, 128), f(2, 256, 128),
            f(2, 256, 128), f(2, 256, 128), f(2, 256, 128),
            f(8, 256), f(8, 128), f(8, 256), f(8, 256),
            b(2, 2, 3, 8, 128), b(2, 3, 8, 128),
            b(2, 3, 8, 128), f(2, 2, 8, 128), b(3, 512, 128), f(2, 512, 128),
            f(2, 512, 128), b(3, 512, 128), f(2, 2, 8, 128), b(2, 3, 8, 128),
            b(4, 16, 512), b(4, 16, 512), b(2, 2, 8, 128), b(2, 8, 128),
            b(2, 8, 128), b(2, 2, 8, 128), f(2, 2, 8, 128), f(2, 2, 2, 8, 128), f(3, 2, 2, 8, 128),
            f(2, 8, 128), f(2, 8, 128), f(2, 8, 128), f(2, 8, 128),
            b(2, 8, 2048), b(64, 2048),
            b(256, 256), b(128, 256), b(4, 128, 512), b(3, 128, 512),
            b(128, 512), b(3, 128, 512), b(3, 128, 256), b(3, 128, 256), f(3, 128, 256), b(2, 3, 8, 128),
            pltpu.SemaphoreType.DMA((NSEM,)),
            pltpu.SemaphoreType.DMA((NSEM,)),
            pltpu.SemaphoreType.DMA((5,)),
        ],
        compiler_params=pltpu.CompilerParams(collective_id=0, has_side_effects=True),
    )(queries, key_rows, value_rows, out_weight, grad_out, pair_offsets, far_head_offsets)
    return pl.pallas_call(
        store,
        out_shape=(jax.ShapeDtypeStruct((ROWS, 2048), BF), rows, rows, rows),
        in_specs=[vm] * 4,
        out_specs=(pl.BlockSpec(memory_space=pl.ANY),) * 4,
        scratch_shapes=[pltpu.SemaphoreType.DMA((4,))],
    )(*[pltpu.with_memory_space_constraint(x, pltpu.VMEM) for x in outs])


def solution(mesh):
    seq = P("seq", "head")
    return jax.shard_map(
        local,
        mesh=mesh,
        in_specs=(seq, seq, seq, P("head", None), seq, P(), P()),
        out_specs=(P("seq", None), seq, seq, seq),
        check_vma=False,
    )
```

```python
import jax
import jax.numpy as jnp
from jax import lax
from jax.experimental import pallas as pl
from jax.experimental.pallas import tpu as pltpu
from jax.sharding import PartitionSpec as P

MESH = pl.DeviceIdType.MESH
NEG = -1.0e30
F32 = jnp.float32
BF = jnp.bfloat16
FACTOR = 128 ** (-0.5)
ROWS = 128
BOTH = 256
ZC = 16
FAR = 32

PQKV, PGRAD, POUT, PDQ = 0, 3, 4, 5
LOC, PAIR, YG, RS, AG = 6, 10, 18, 21, 54
STL, STP = 27, 28
R1, R2 = 30, 32
FA, FB, FMATE = 34, 36, 38
FQN, FQP, FRN, FRP, FIX, FBK = 39, 40, 42, 43, 45, 53
YF, FGM = 60, 63
NSEM = 64


def nt(a, b):
    return lax.dot_general(a, b, (((1,), (1,)), ((), ())), preferred_element_type=F32)


def nn(a, b):
    return jnp.dot(a, b, preferred_element_type=F32)


def exact(a, b):
    return lax.dot_general(
        a, b, (((1,), (0,)), ((), ())), precision=lax.Precision.HIGHEST, preferred_element_type=F32
    )


def iota(shape, dim):
    return lax.broadcasted_iota(jnp.int32, shape, dim)


def pick_far(x, off):
    rows = iota(x.shape, 0)
    kept = jnp.where((rows & (FAR - 1)) == off, x, 0.0)
    return jnp.sum(kept.reshape(BOTH // FAR, FAR, 128), axis=1)


def repeat_far(x):
    return jnp.broadcast_to(x[:, None, :], (BOTH // FAR, FAR, 128)).reshape(BOTH, 128)


def kernel(
    q_in, k_in, v_in, w_in, go_in, po, fo,
    lo, dq, dk, dv,
    q, k, v, w, go,
    QC, KC, VC, GC, LB, PB, PSND, GOA, GOUT,
    MR, LR, ACC, DQ, DK, DV, STR, STPS, LSR, PSR,
    FX, FY, FS, FS2, FG, FG2, R1S, R2S, FR1, FR2,
    GFS, GFR, DX, DY, FQNB, FQPB, FRNB, FRPB, FOUT, FM, FL, FACC, FST, CS, CB,
    OB, ORC, RSS, RSR, AGS, AGR, DSND, DRCV, GR, FRM,
    ss, rs, ls,
):
    t = lax.axis_index("seq")
    y = lax.axis_index("head")
    c = t % 2
    chip = t // 2
    odd = chip % 2
    g = chip % 4
    zz = chip % ZC
    upper = g // 2
    mate = t + 1 - 2 * c
    near = chip + 1 - 2 * odd
    other = chip - g + 2 - 2 * upper
    nchip = lax.axis_size("seq") // 2
    hub_turn = (chip // ZC) % 2
    hub_z = 0
    is_hub = jnp.logical_and(chip % ZC == hub_z, (chip // ZC) // 2 == c)

    def hub_chip(i):
        return ZC * (2 * c + i)

    def rc(src, dst, i, j, dev):
        return pltpu.make_async_remote_copy(
            src_ref=src, dst_ref=dst, send_sem=ss.at[i], recv_sem=rs.at[j],
            device_id=dev, device_id_type=MESH,
        )

    loads = [
        pltpu.make_async_copy(a, b, ls.at[n])
        for n, (a, b) in enumerate(((k_in, k), (v_in, v), (q_in, q), (go_in, go), (w_in, w)))
    ]
    for x in loads:
        x.start()

    bar = pltpu.get_barrier_semaphore()

    def sig(dev):
        pl.semaphore_signal(bar, inc=1, device_id=dev, device_id_type=MESH)

    def from_near(b, n):
        step = (n + 1) // 2
        return ZC * b + (hub_z + jnp.where(n % 2 == 1, ZC - step, step)) % ZC

    @pl.when(is_hub)
    def _():
        @pl.loop(0, nchip)
        def _(n):
            u = from_near(n // ZC, n % ZC)

            @pl.when(u != chip)
            def _():
                sig((2 * u + c, y))

    for d in range(1, 4):
        sig((t, (y + d) % 4))
    sig((mate, y))
    for s in range(2):
        sig((2 * near + s, y))
        for d in range(2):
            sig((2 * (other + d) + s, y))

    off_p = [po[4 * y + 2 * c + i] for i in range(2)]
    off_f = [fo[4 * y + 2 * c + i] for i in range(2)]
    lane = pl.ds(pl.multiple_of(256 * c, 256), 256)
    mine = pl.ds(pl.multiple_of(ROWS * c, ROWS), ROWS)
    theirs = pl.ds(pl.multiple_of(ROWS * (1 - c), ROWS), ROWS)
    mate_lane = pl.ds(pl.multiple_of(256 * (1 - c), 256), 256)

    def one_hot(off):
        return jnp.where(
            iota((64, ROWS), 1) == 2 * iota((64, ROWS), 0) + off, 1.0, 0.0
        ).astype(BF)

    def pair_rows(src, slot):
        for h in range(4):
            e = one_hot(po[4 * y + h])
            cols = slice(128 * h, 128 * h + 128)
            PSND[slot, :, cols] = nn(e, src[:, cols]).astype(BF)

    for x in loads[:3]:
        x.wait()
    own_rows = (iota((8, 128), 0) // 4) == c
    for h in range(4):
        for n, src in enumerate((q, k, v)):
            x = src[:, 128 * h : 128 * h + 128].astype(F32)
            x = jnp.where((iota((ROWS, 128), 0) & (FAR - 1)) == fo[4 * y + h], x, 0.0)
            x = jnp.sum(x.reshape(4, FAR, 128), axis=1)
            x = jnp.where(own_rows, jnp.concatenate([x, x], axis=0), 0.0)
            FX[h // 2, h % 2, n] = x.astype(BF)

    @pl.when(upper == 0)
    def _():
        pair_rows(k, 0)
        pair_rows(v, 1)

    @pl.when(upper == 1)
    def _():
        pair_rows(q, 0)

    for src, dst in ((q, QC), (k, KC), (v, VC)):
        dst[mine, :] = jnp.where(c == 0, src[:, 0:256], src[:, 256:512])

    loads[3].wait()
    for d in range(4):
        to = (y + d) % 4
        r16 = iota((16, ROWS), 0)
        at = jnp.zeros((16, ROWS), jnp.int32)
        for h in range(4):
            at = jnp.where(r16 // 4 == h, fo[4 * to + h], at)
        e = jnp.where(iota((16, ROWS), 1) == FAR * (r16 & 3) + at, 1.0, 0.0).astype(BF)
        GFS[to] = nn(e, go[...]).astype(BF)

    count = 3 + 1 + 2 + 4
    for i in range(2):
        count = count + jnp.where(chip != hub_chip(i), 1, 0)
    pl.semaphore_wait(bar, count)

    def far_mate():
        return rc(FX.at[1 - c], FY, FMATE, FMATE, (mate, y))

    far_mate().start()

    def y_copy(d):
        return rc(go, GOA.at[y], YG + d - 1, YG + d - 1, (t, (y + d) % 4))

    def y_far(d):
        return rc(GFS.at[(y + d) % 4], GFR.at[y], YF + d - 1, YF + d - 1, (t, (y + d) % 4))

    for d in (2, 1, 3):
        y_far(d).start()
    for d in (2, 1, 3):
        y_copy(d).start()

    def local_copy(src, n, s):
        return rc(
            src.at[:, 256 * s : 256 * s + 256], LB.at[n, mine, :],
            LOC + 2 * n + s, LOC + 2 * n + c, (2 * near + s, y),
        )

    def pair_copy(n, d, s):
        at = pl.ds(pl.multiple_of(128 * odd + 64 * c, 64), 64)
        return rc(
            PSND.at[n, :, 256 * s : 256 * s + 256], PB.at[n, at, :],
            PAIR + 4 * n + 2 * d + s, PAIR + 4 * n + 2 * odd + c, (2 * (other + d) + s, y),
        )

    far_at = pl.ds(pl.multiple_of(8 * chip, 8), 8)
    far_mate().wait_recv()
    for i in range(2):
        FS[i] = FX[c, i] + FY[i]

    def far_copy(i):
        return rc(FS.at[i], FG.at[:, far_at, :], FA + i, FA, (2 * hub_chip(i) + c, y))

    def far_copy2(i):
        return rc(FS2.at[i], FG2.at[:, far_at, :], FB + i, FB, (2 * hub_chip(i) + c, y))

    for i in range(2):
        @pl.when(chip != hub_chip(i))
        def _(i=i):
            far_copy(i).start()

        @pl.when(chip == hub_chip(i))
        def _(i=i):
            FG[:, far_at, :] = FS[i]

    def ask_near():
        return rc(FS.at[:, 0], FQNB, FQN, FQN, (2 * near + c, y))

    def ask_pair(d):
        return rc(FS.at[:, 0], FQPB.at[odd], FQP + d, FQP + odd, (2 * (other + d) + c, y))

    def tell_near():
        return rc(FOUT.at[2], FRNB, FRN, FRN, (2 * near + c, y))

    def tell_pair(d):
        return rc(FOUT.at[d], FRPB.at[odd], FRP + d, FRP + odd, (2 * (other + d) + c, y))

    @pl.when(odd == 1)
    def _():
        ask_near().start()

    @pl.when(upper == 1)
    def _():
        for d in range(2):
            ask_pair(d).start()

    mate_copies = [
        rc(src.at[:, mate_lane], dst.at[mine, :], PQKV + n, PQKV + n, (mate, y))
        for n, (src, dst) in enumerate(((q, QC), (k, KC), (v, VC)))
    ]
    for x in mate_copies:
        x.start()

    for s in range(2):
        @pl.when(odd == 0)
        def _(s=s):
            local_copy(k, 0, s).start()

        @pl.when(odd == 1)
        def _(s=s):
            local_copy(q, 0, s).start()

    for d in range(2):
        for s in range(2):
            @pl.when(jnp.logical_or(upper == 1, odd == 1))
            def _(d=d, s=s):
                pair_copy(0, d, s).start()

    for x in mate_copies:
        x.wait_recv()

    def answer(slot, i, qq, near_row):
        cols = slice(128 * i, 128 * i + 128)
        match = jnp.logical_and((iota((8, BOTH), 1) & 1) == off_p[i], ((off_f[i] - off_p[i]) & 1) == 0)
        cnt = jnp.where(match, 1.0, 0.0) + near_row
        s = nt(qq, KC[:, cols]) * FACTOR
        s = jnp.where(cnt > 0.0, s, NEG)
        m = jnp.max(s, axis=1, keepdims=True)
        p = cnt * jnp.exp(s - m)
        FOUT[slot, i, 0] = nn(p.astype(BF), VC[:, cols])
        total = jnp.sum(p, axis=1, keepdims=True)
        FOUT[slot, i, 1] = jnp.where(iota((8, 128), 1) == 0, m, total)

    @pl.when(upper == 0)
    def _():
        for d in range(2):
            rc(FS.at[:, 0], FQPB.at[d], FQP, FQP + d, (2 * (other + d) + c, y)).wait_recv()
            for i in range(2):
                answer(d, i, FQPB[d, i], 0.0)
            tell_pair(d).start()

    @pl.when(odd == 0)
    def _():
        ask_near().wait_recv()
        for i in range(2):
            answer(2, i, FQNB[i], 1.0)
        tell_near().start()
        for s in range(2):
            local_copy(v, 1, s).start()

    @pl.when(upper == 0)
    def _():
        for d in range(2):
            for s in range(2):
                @pl.when(jnp.logical_and(odd == 0, zz != 8))
                def _(d=d, s=s):
                    pair_copy(0, d, s).start()

                @pl.when(jnp.logical_or(odd == 1, zz != 8))
                def _(d=d, s=s):
                    pair_copy(1, d, s).start()

    for i in range(2):
        cols = slice(128 * i, 128 * i + 128)
        at, to = iota((8, BOTH), 1), FAR * iota((8, BOTH), 0) + off_f[i]
        match = jnp.logical_and((at & 1) == off_p[i], (to & 1) == off_p[i])
        cnt = jnp.where(at <= to, jnp.where(match, 2.0, 1.0), 0.0)
        s = jnp.where(cnt > 0.0, nt(FS[i, 0], KC[:, cols]) * FACTOR, NEG)
        m = jnp.max(s, axis=1, keepdims=True)
        p = cnt * jnp.exp(s - m)
        FACC[i] = nn(p.astype(BF), VC[:, cols])
        FL[i] = jnp.broadcast_to(jnp.sum(p, axis=1, keepdims=True), (8, 128))
        FM[i] = jnp.broadcast_to(m, (8, 128))

    loads[4].wait()
    part = nt(GFS[y], w[:, pl.ds(pl.multiple_of(512 * y, 512), 512)])
    for d in (1, 3, 2):
        src = (y + 4 - d) % 4
        rc(GFS.at[0], GFR.at[src], YF + d - 1, YF + d - 1, (t, src)).wait_recv()
        part = part + nt(GFR[src], w[:, pl.ds(pl.multiple_of(512 * src, 512), 512)])
    for h in range(4):
        x = part[4 * h : 4 * h + 4, 128 * h : 128 * h + 128]
        x = jnp.where(own_rows, jnp.concatenate([x, x], axis=0), 0.0)
        DX[h // 2, h % 2] = x.astype(BF)

    def far_grad_mate():
        return rc(DX.at[1 - c], DY, FGM, FGM, (mate, y))

    far_grad_mate().start()

    ri = iota((BOTH, BOTH), 0)
    ci = iota((BOTH, BOTH), 1)

    def own_count(i):
        both = jnp.logical_and((ri & 1) == off_p[i], (ci & 1) == off_p[i])
        return jnp.where(both, 2.0, 1.0)

    def fwd(i, kk, vv, cnt, first=False):
        cols = slice(128 * i, 128 * i + 128)
        s = nt(QC[:, cols], kk) * FACTOR
        s = jnp.where(cnt > 0.0, s, NEG)
        top = jnp.max(s, axis=1, keepdims=True)
        if first:
            m = top
        else:
            m_old = MR[i][:, 0:1]
            m = jnp.maximum(m_old, top)
        p = cnt * jnp.exp(s - m)
        total = jnp.sum(p, axis=1, keepdims=True)
        num = nn(p.astype(BF), vv)
        if not first:
            a = jnp.exp(m_old - m)
            total = total + a * LR[i][:, 0:1]
            num = num + a * ACC[i]
        MR[i] = jnp.broadcast_to(m, (BOTH, 128))
        LR[i] = jnp.broadcast_to(total, (BOTH, 128))
        ACC[i] = num

    for i in range(2):
        cols = slice(128 * i, 128 * i + 128)
        fwd(i, KC[:, cols], VC[:, cols], jnp.where(ri >= ci, own_count(i), 0.0), True)

    def join(i, got):
        m_o = FM[i][:, 0:1]
        m_g = got[1][:, 0:1]
        m = jnp.maximum(m_o, m_g)
        a = jnp.exp(m_o - m)
        e = jnp.exp(m_g - m)
        FACC[i] = a * FACC[i] + e * got[0]
        FL[i] = jnp.broadcast_to(a * FL[i][:, 0:1] + e * got[1][:, 1:2], (8, 128))
        FM[i] = jnp.broadcast_to(m, (8, 128))

    @pl.when(odd == 1)
    def _():
        tell_near().wait_recv()
        for i in range(2):
            join(i, FRNB[i])

    @pl.when(upper == 1)
    def _():
        for d in range(2):
            rc(FOUT.at[d], FRPB.at[d], FRP, FRP + d, (2 * (other + d) + c, y)).wait_recv()
            for i in range(2):
                join(i, FRPB[d, i])

    far_grad_mate().wait_recv()
    l8 = iota((8, 128), 1)
    for i in range(2):
        gf = DX[c, i].astype(F32) + DY[i].astype(F32)
        dn = jnp.sum(gf * FACC[i], axis=1, keepdims=True)
        FS2[i, 0] = gf
        FS2[i, 1] = jnp.where(l8 == 0, FM[i], jnp.where(l8 == 1, FL[i], dn))

    for i in range(2):
        @pl.when(chip != hub_chip(i))
        def _(i=i):
            far_copy2(i).start()

        @pl.when(chip == hub_chip(i))
        def _(i=i):
            FG2[:, far_at, :] = FS2[i]

    grad = nt(go[...], w[:, pl.ds(pl.multiple_of(512 * y, 512), 512)])
    for d in (1, 3, 2):
        src = (y + 4 - d) % 4
        rc(go, GOA.at[src], YG + d - 1, YG + d - 1, (t, src)).wait_recv()
        grad = grad + nt(GOA[src], w[:, pl.ds(pl.multiple_of(512 * src, 512), 512)])
    GOUT[...] = grad.astype(BF)
    GC[mine, :] = jnp.where(c == 0, GOUT[:, 0:256], GOUT[:, 256:512])

    @pl.when(upper == 1)
    def _():
        pair_rows(GOUT, 1)

    grad_mate = rc(GOUT.at[:, mate_lane], GC.at[mine, :], PGRAD, PGRAD, (mate, y))
    grad_mate.start()

    @pl.when(odd == 1)
    def _():
        for s in range(2):
            local_copy(GOUT, 1, s).start()

    @pl.when(zz == 8)
    def _():
        for d in range(2):
            for s in range(2):
                pair_copy(0, d, s).start()

    @pl.when(jnp.logical_or(upper == 1, zz == 8))
    def _():
        for d in range(2):
            for s in range(2):
                pair_copy(1, d, s).start()

    @pl.when(odd == 1)
    def _():
        for n in range(2):
            for s in range(2):
                rc(
                    k.at[:, 0:256], LB.at[n, pl.ds(128 * s, 128), :],
                    LOC + 2 * n, LOC + 2 * n + s, (2 * near + s, y),
                ).wait_recv()
        for i in range(2):
            cols = slice(128 * i, 128 * i + 128)
            fwd(i, LB[0, :, cols], LB[1, :, cols], own_count(i))

    def pair_wait(n, d, s):
        rc(
            PSND.at[n, :, 0:256], PB.at[n, pl.ds(128 * d + 64 * s, 64), :],
            PAIR, PAIR + 4 * n + 2 * d + s, (2 * (other + d) + s, y),
        ).wait_recv()

    def pair_key_count(i, x):
        return jnp.where((x & 1) == off_p[i], 1.0, 0.0)

    @pl.when(upper == 1)
    def _():
        for n in range(2):
            for d in range(2):
                for s in range(2):
                    pair_wait(n, d, s)
        for i in range(2):
            cols = slice(128 * i, 128 * i + 128)
            fwd(i, PB[0, :, cols], PB[1, :, cols], pair_key_count(i, ri))

    for i in range(2):
        OB[:, 128 * i : 128 * i + 128] = (ACC[i] / LR[i]).astype(BF)
    out_mate = rc(OB.at[theirs, :], ORC, POUT, POUT, (mate, y))
    out_mate.start()
    out_mate.wait_recv()
    attended = jnp.where(
        c == 0,
        jnp.concatenate([OB[mine, :], ORC[...]], axis=1),
        jnp.concatenate([ORC[...], OB[mine, :]], axis=1),
    )

    def rs_copy(d, half):
        to = (y + d) % 4
        at = slice(256 * half, 256 * half + 256)
        n = RS + 3 * half + d - 1
        return rc(RSS.at[to, :, at], RSR.at[d - 1, :, at], n, n, (t, to))

    def lanes_of(to, half):
        return pl.ds(pl.multiple_of(512 * to + 256 * half, 256), 256)

    own_parts = []
    for half in range(2):
        for d in (2, 1, 3):
            to = (y + d) % 4
            RSS[to, :, 256 * half : 256 * half + 256] = nn(attended, w[:, lanes_of(to, half)]).astype(BF)
            rs_copy(d, half).start()
        own_parts.append(nn(attended, w[:, lanes_of(y, half)]).astype(BF).astype(F32))

    @pl.when(is_hub)
    def _():
        rest = FG.at[:, pl.ds(0, 8 * (nchip - 1)), :]
        rc(rest, rest, FA, FA, (t, y)).wait_recv()
        lanes = iota((128, 128), 1)
        for b in range(nchip // ZC):
            at, size = slice(128 * b, 128 * b + 128), 128 * b + 128
            s = nt(FG[0, at, :], FG[1, 0:size, :]) * FACTOR
            s = jnp.where(iota((128, size), 0) + 128 * b >= iota((128, size), 1), s, NEG)
            m = jnp.max(s, axis=1, keepdims=True)
            p = jnp.exp(s - m)
            total = jnp.sum(p, axis=1, keepdims=True)
            R1S[0, at, :] = nn(p.astype(BF), FG[2, 0:size, :])
            R1S[1, at, :] = jnp.where(lanes == 0, m, total)

            def send(u):
                at = pl.ds(pl.multiple_of(8 * u, 8), 8)
                rc(R1S.at[:, at, :], FR1.at[hub_turn], R1, R1 + hub_turn, (2 * u + c, y)).start()

            @pl.when(ZC * b != chip)
            def _(b=b, send=send):
                send(ZC * b)

            @pl.loop(0, 5)
            def _(k, b=b, send=send):
                for j in range(3):
                    send(from_near(b, 3 * k + j + 1))

        FR1[hub_turn] = R1S[:, far_at, :]

    grad_mate.wait_recv()
    l128 = iota((BOTH, 128), 1)
    stats = jnp.zeros((BOTH, 128), F32)
    for i in range(2):
        cols = slice(128 * i, 128 * i + 128)

        @pl.when(chip != hub_chip(i))
        def _(i=i):
            rc(R1S.at[:, 0:8, :], FR1.at[i], R1, R1 + i, (2 * hub_chip(i) + c, y)).wait_recv()

        is_far = (iota((BOTH, 1), 0) & (FAR - 1)) == off_f[i]
        num_f = repeat_far(FR1[i, 0])
        st_f = repeat_far(FR1[i, 1])
        m_f = jnp.where(is_far, st_f[:, 0:1], NEG)
        l_f = jnp.where(is_far, st_f[:, 1:2], 0.0)
        m_n = MR[i][:, 0:1]
        m = jnp.maximum(m_n, m_f)
        a = jnp.exp(m_n - m)
        b = jnp.where(is_far, jnp.exp(m_f - m), 0.0)
        total = a * LR[i][:, 0:1] + b * l_f
        out = (a * ACC[i] + b * num_f) / total
        FST[i] = pick_far(out - OB[:, cols].astype(F32), off_f[i])
        lse = m + jnp.log(total)
        delta = jnp.sum(GC[:, cols].astype(F32) * out, axis=1, keepdims=True)
        MR[i] = jnp.broadcast_to(lse, (BOTH, 128))
        LR[i] = jnp.broadcast_to(delta, (BOTH, 128))
        stats = jnp.where(l128 == 2 * i, lse, jnp.where(l128 == 2 * i + 1, delta, stats))

    STR[...] = jnp.transpose(stats)[0:8, :]

    @pl.when(upper == 1)
    def _():
        srow = iota((8, 128), 0)
        parts = []
        for i in range(2):
            e = jnp.where(iota((BOTH, 128), 0) == 2 * iota((BOTH, 128), 1) + off_p[i], 1.0, 0.0)
            parts.append(exact(STR[...], e))
        STPS[...] = jnp.where(srow < 2, parts[0], parts[1])

    def near_stats():
        return rc(STR, LSR, STL, STL, (2 * near + c, y))

    def pair_stats(d):
        at = pl.ds(pl.multiple_of(128 * odd, 128), 128)
        return rc(STPS, PSR.at[:, at], STP + d, STP + odd, (2 * (other + d) + c, y))

    @pl.when(odd == 1)
    def _():
        near_stats().start()

    @pl.when(upper == 1)
    def _():
        for d in range(2):
            pair_stats(d).start()

    fixes = [
        nn(FST[i].astype(BF), w[pl.ds(pl.multiple_of(256 * c + 128 * i, 128), 128), :]) for i in range(2)
    ]
    fix_at = pl.ds(pl.multiple_of(8 * (2 * y + c), 8), 8)
    for s in range(2):
        CS[s] = jnp.concatenate([x[4 * s : 4 * s + 4, :] for x in fixes], axis=0).astype(BF)

    def fix_copy(d, s):
        return rc(
            CS.at[s], CB.at[fix_at, :], FIX + 2 * d + s, FIX + 2 * y + c,
            (2 * chip + s, (y + d) % 4),
        )

    for d in (2, 1, 3):
        for s in range(2):
            fix_copy(d, s).start()
    for s in range(2):
        @pl.when(c == s)
        def _(s=s):
            fix_copy(0, 1 - s).start()
            CB[fix_at, :] = CS[s]

    def ag_copy(d, half):
        at = slice(256 * half, 256 * half + 256)
        n = AG + 3 * half + d - 1
        return rc(AGS.at[:, at], AGR.at[d - 1, :, at], n, n, (t, (y + d) % 4))

    for half in range(2):
        at = slice(256 * half, 256 * half + 256)
        acc = own_parts[half]
        for d in (1, 3, 2):
            rs_copy(d, half).wait_recv()
            acc = acc + RSR[d - 1, :, at].astype(F32)
        AGS[:, at] = acc.astype(BF)
        for d in (2, 1, 3):
            ag_copy(d, half).start()

    def row_side(i, kk, vv, cnt, masked):
        cols = slice(128 * i, 128 * i + 128)
        s = nt(QC[:, cols], kk) * FACTOR
        if masked:
            s = jnp.where(cnt > 0.0, s, NEG)
        p = cnt * jnp.exp(s - MR[i][:, 0:1])
        ds = (p * (nt(GC[:, cols], vv) - LR[i][:, 0:1])).astype(BF)
        return nn(ds, kk)

    def col_side(i, qq, gg, st, cnt, masked):
        cols = slice(128 * i, 128 * i + 128)
        s = nt(KC[:, cols], qq) * FACTOR
        if masked:
            s = jnp.where(cnt > 0.0, s, NEG)
        p = cnt * jnp.exp(s - st[2 * i : 2 * i + 1, :])
        ds = (p * (nt(VC[:, cols], gg) - st[2 * i + 1 : 2 * i + 2, :])).astype(BF)
        return nn(ds, qq), nn(p.astype(BF), gg)

    for i in range(2):
        cols = slice(128 * i, 128 * i + 128)
        DQ[i] = row_side(i, KC[:, cols], VC[:, cols], jnp.where(ri >= ci, own_count(i), 0.0), True)
        DK[i], DV[i] = col_side(
            i, QC[:, cols], GC[:, cols], STR[...], jnp.where(ci >= ri, own_count(i), 0.0), True
        )

    def hub_backward():
        rest = FG2.at[:, pl.ds(0, 8 * (nchip - 1)), :]
        rc(rest, rest, FB, FB, (t, y)).wait_recv()
        rows = []
        lanes = iota((128, 128), 1)
        for b in range(nchip // ZC):
            at = slice(128 * b, 128 * b + 128)
            m_f = R1S[1, at, 0:1]
            l_f = R1S[1, at, 1:2]
            m_n = FG2[1, at, 0:1]
            l_n = FG2[1, at, 1:2]
            d_n = FG2[1, at, 2:3]
            m = jnp.maximum(m_f, m_n)
            a = jnp.exp(m_n - m)
            e = jnp.exp(m_f - m)
            total = a * l_n + e * l_f
            lse = m + jnp.log(total)
            d_f = jnp.sum(FG2[0, at, :] * R1S[0, at, :], axis=1, keepdims=True)
            delta = (a * d_n + e * d_f) / total
            both = jnp.where(lanes == 0, lse, delta)
            FG2[1, at, :] = both
            rows.append(jnp.transpose(both))
        rows = jnp.concatenate([x[0:8, :] for x in rows], axis=1)
        size = FG.shape[1]
        for b in range(nchip // ZC):
            at, end = slice(128 * b, 128 * b + 128), 128 * b + 128
            past, ahead = slice(0, end), slice(128 * b, size)
            lse = FG2[1, at, 0:1]
            delta = FG2[1, at, 1:2]
            lower = iota((128, end), 0) + 128 * b >= iota((128, end), 1)
            s = jnp.where(lower, nt(FG[0, at, :], FG[1, past, :]) * FACTOR, NEG)
            p = jnp.exp(s - lse)
            ds = (p * (nt(FG2[0, at, :].astype(BF), FG[2, past, :]) - delta)).astype(BF)
            R2S[0, at, :] = (nn(ds, FG[1, past, :]) * FACTOR).astype(BF)
            later = iota((128, size - 128 * b), 1) >= iota((128, size - 128 * b), 0)
            s = jnp.where(later, nt(FG[1, at, :], FG[0, ahead, :]) * FACTOR, NEG)
            p = jnp.exp(s - rows[0:1, ahead])
            gb = FG2[0, ahead, :].astype(BF)
            R2S[2, at, :] = nn(p.astype(BF), gb).astype(BF)
            ds = (p * (nt(FG[2, at, :], gb) - rows[1:2, ahead])).astype(BF)
            R2S[1, at, :] = (nn(ds, FG[0, ahead, :]) * FACTOR).astype(BF)

        def send(u):
            at = pl.ds(pl.multiple_of(8 * u, 8), 8)
            rc(R2S.at[:, at, :], FR2.at[hub_turn], R2, R2 + hub_turn, (2 * u + c, y)).start()

        for b in range(4):
            @pl.when(ZC * b != chip)
            def _(b=b):
                send(ZC * b)

        @pl.loop(1, ZC)
        def _(n):
            for b in range(4):
                send(from_near(b, n))

        FR2[hub_turn] = R2S[:, far_at, :]

    pl.when(jnp.logical_and(is_hub, chip != 0))(hub_backward)

    @pl.when(odd == 1)
    def _():
        for i in range(2):
            cols = slice(128 * i, 128 * i + 128)
            DQ[i] += row_side(i, LB[0, :, cols], LB[1, :, cols], own_count(i), False)

    @pl.when(odd == 0)
    def _():
        for n in range(2):
            for s in range(2):
                rc(
                    k.at[:, 0:256], LB.at[n, pl.ds(128 * s, 128), :],
                    LOC + 2 * n, LOC + 2 * n + s, (2 * near + s, y),
                ).wait_recv()
        near_stats().wait_recv()
        for i in range(2):
            cols = slice(128 * i, 128 * i + 128)
            a, b = col_side(i, LB[0, :, cols], LB[1, :, cols], LSR[...], own_count(i), False)
            DK[i] += a
            DV[i] += b

    @pl.when(upper == 1)
    def _():
        for i in range(2):
            cols = slice(128 * i, 128 * i + 128)
            DQ[i] += row_side(i, PB[0, :, cols], PB[1, :, cols], pair_key_count(i, ri), True)

    @pl.when(upper == 0)
    def _():
        for n in range(2):
            for d in range(2):
                for s in range(2):
                    pair_wait(n, d, s)
        for d in range(2):
            rc(
                STPS, PSR.at[:, 128 * d : 128 * d + 128], STP, STP + d, (2 * (other + d) + c, y)
            ).wait_recv()
        for i in range(2):
            cols = slice(128 * i, 128 * i + 128)
            a, b = col_side(
                i, PB[0, :, cols], PB[1, :, cols], PSR[...], pair_key_count(i, ri), True
            )
            DK[i] += a
            DV[i] += b

    for n, (src, scale) in enumerate(((DQ, FACTOR), (DK, FACTOR), (DV, 1.0))):
        full = jnp.concatenate([src[i] * scale for i in range(2)], axis=1)
        DSND[n] = jnp.where(c == 0, full[ROWS:, :], full[:ROWS, :]).astype(BF)
        GR[n] = jnp.where(c == 0, full[:ROWS, :], full[ROWS:, :])
    back = rc(DSND, DRCV, PDQ, PDQ, (mate, y))
    back.start()

    pl.when(jnp.logical_and(is_hub, chip == 0))(hub_backward)

    for i in range(2):
        @pl.when(chip != hub_chip(i))
        def _(i=i):
            rc(R2S.at[:, 0:8, :], FR2.at[i], R2, R2 + i, (2 * hub_chip(i) + c, y)).wait_recv()

    back_far = rc(FR2, FRM, FBK, FBK, (mate, y))
    back_far.start()

    def far_rows(tiles, n, cc):
        parts = []
        for i in range(2):
            x = tiles[i, n].astype(F32)
            x = jnp.where(c == 0, x[0:4, :], x[4:8, :])
            x = jnp.broadcast_to(x[:, None, :], (4, FAR, 128)).reshape(ROWS, 128)
            hit = (iota((ROWS, 128), 0) & (FAR - 1)) == fo[4 * y + 2 * cc + i]
            parts.append(jnp.where(hit, x, 0.0))
        return jnp.concatenate(parts, axis=1)

    for n, dst in enumerate((dq, dk, dv)):
        dst[:, lane] = (GR[n] + far_rows(FR2, n, c)).astype(BF)
    for d in range(4):
        for s in range(2):
            @pl.when(jnp.logical_or(d > 0, s != c))
            def _(d=d, s=s):
                src = (y + 4 - d) % 4
                rc(
                    CS.at[0], CB.at[pl.ds(pl.multiple_of(8 * (2 * src + s), 8), 8), :],
                    FIX, FIX + 2 * src + s, (2 * chip + s, src),
                ).wait_recv()
    kk = iota((ROWS, 64), 1)
    place = jnp.zeros((ROWS, 64), jnp.int32)
    for h in range(16):
        place = jnp.where(kk // 4 == h, fo[h], place)
    place = jnp.where(iota((ROWS, 64), 0) == FAR * (kk & 3) + place, 1.0, 0.0).astype(BF)

    def whole(base, at):
        lo[:, at] = (base.astype(F32) + nn(place, CB[:, at])).astype(BF)

    whole(AGS[...], pl.ds(pl.multiple_of(512 * y, 512), 512))
    for d in (1, 3, 2):
        ag_copy(d, 0).wait_recv()
        ag_copy(d, 1).wait_recv()
        src = (y + 4 - d) % 4
        whole(AGR[d - 1], pl.ds(pl.multiple_of(512 * src, 512), 512))

    back.wait_recv()
    back_far.wait_recv()
    for n, dst in enumerate((dq, dk, dv)):
        dst[:, mate_lane] = (DRCV[n].astype(F32) + far_rows(FRM, n, 1 - c)).astype(BF)

    far_mate().wait_send()
    far_grad_mate().wait_send()
    for x in mate_copies:
        x.wait_send()
    for d in range(1, 4):
        y_copy(d).wait_send()
        y_far(d).wait_send()
        for half in range(2):
            rs_copy(d, half).wait_send()
            ag_copy(d, half).wait_send()
    for n in range(2):
        for s in range(2):
            local_copy(k, n, s).wait_send()
            for d in range(2):
                pair_copy(n, d, s).wait_send()
    grad_mate.wait_send()
    out_mate.wait_send()
    back.wait_send()
    back_far.wait_send()
    for i in range(2):
        @pl.when(chip != hub_chip(i))
        def _(i=i):
            far_copy(i).wait_send()
            far_copy2(i).wait_send()

    @pl.when(odd == 1)
    def _():
        near_stats().wait_send()
        ask_near().wait_send()

    @pl.when(odd == 0)
    def _():
        tell_near().wait_send()

    @pl.when(upper == 0)
    def _():
        for d in range(2):
            tell_pair(d).wait_send()

    @pl.when(upper == 1)
    def _():
        for d in range(2):
            pair_stats(d).wait_send()
            ask_pair(d).wait_send()

    for d in range(1, 4):
        for s in range(2):
            fix_copy(d, s).wait_send()
    for s in range(2):
        @pl.when(c == s)
        def _(s=s):
            fix_copy(0, 1 - s).wait_send()

    @pl.when(is_hub)
    def _():
        for sent, n in ((R1S, R1), (R2S, R2)):
            sent = sent.at[:, pl.ds(0, 8 * (nchip - 1)), :]
            rc(sent, sent, n, n, (t, y)).wait_send()


def store(*refs):
    copies = [
        pltpu.make_async_copy(a, b, refs[8].at[n]) for n, (a, b) in enumerate(zip(refs[:4], refs[4:8]))
    ]
    for x in copies:
        x.start()
    for x in copies:
        x.wait()


def local(queries, key_rows, value_rows, out_weight, grad_out, pair_offsets, far_head_offsets):
    vm = pl.BlockSpec(memory_space=pltpu.VMEM)
    sm = pl.BlockSpec(memory_space=pltpu.SMEM)
    rows = jax.ShapeDtypeStruct((ROWS, 512), BF)

    def b(*shape):
        return pltpu.VMEM(shape, BF)

    def f(*shape):
        return pltpu.VMEM(shape, F32)

    outs = pl.pallas_call(
        kernel,
        out_shape=(pltpu.VMEM((ROWS, 2048), BF),) + (pltpu.VMEM((ROWS, 512), BF),) * 3,
        in_specs=[pl.BlockSpec(memory_space=pl.ANY)] * 5 + [sm] * 2,
        out_specs=(vm,) * 4,
        scratch_shapes=[
            b(128, 512), b(128, 512), b(128, 512), b(512, 2048), b(128, 512),
            b(256, 256), b(256, 256), b(256, 256), b(256, 256),
            b(2, 256, 256), b(2, 256, 256), b(2, 64, 512), b(4, 128, 512), b(128, 512),
            f(2, 256, 128), f(2, 256, 128), f(2, 256, 128),
            f(2, 256, 128), f(2, 256, 128), f(2, 256, 128),
            f(8, 256), f(8, 128), f(8, 256), f(8, 256),
            b(2, 2, 3, 8, 128), b(2, 3, 8, 128),
            b(2, 3, 8, 128), f(2, 2, 8, 128), b(3, 512, 128), f(2, 512, 128),
            f(2, 512, 128), b(3, 512, 128), f(2, 2, 8, 128), b(2, 3, 8, 128),
            b(4, 16, 512), b(4, 16, 512), b(2, 2, 8, 128), b(2, 8, 128),
            b(2, 8, 128), b(2, 2, 8, 128), f(2, 2, 8, 128), f(2, 2, 2, 8, 128), f(3, 2, 2, 8, 128),
            f(2, 8, 128), f(2, 8, 128), f(2, 8, 128), f(2, 8, 128),
            b(2, 8, 2048), b(64, 2048),
            b(256, 256), b(128, 256), b(4, 128, 512), b(3, 128, 512),
            b(128, 512), b(3, 128, 512), b(3, 128, 256), b(3, 128, 256), f(3, 128, 256), b(2, 3, 8, 128),
            pltpu.SemaphoreType.DMA((NSEM,)),
            pltpu.SemaphoreType.DMA((NSEM,)),
            pltpu.SemaphoreType.DMA((5,)),
        ],
        compiler_params=pltpu.CompilerParams(collective_id=0, has_side_effects=True),
    )(queries, key_rows, value_rows, out_weight, grad_out, pair_offsets, far_head_offsets)
    return pl.pallas_call(
        store,
        out_shape=(jax.ShapeDtypeStruct((ROWS, 2048), BF), rows, rows, rows),
        in_specs=[vm] * 4,
        out_specs=(pl.BlockSpec(memory_space=pl.ANY),) * 4,
        scratch_shapes=[pltpu.SemaphoreType.DMA((4,))],
    )(*[pltpu.with_memory_space_constraint(x, pltpu.VMEM) for x in outs])


def solution(mesh):
    seq = P("seq", "head")
    return jax.shard_map(
        local,
        mesh=mesh,
        in_specs=(seq, seq, seq, P("head", None), seq, P(), P()),
        out_specs=(P("seq", None), seq, seq, seq),
        check_vma=False,
    )
```

```python
import jax
import jax.numpy as jnp
from jax import lax
from jax.experimental import pallas as pl
from jax.experimental.pallas import tpu as pltpu
from jax.sharding import PartitionSpec as P

MESH = pl.DeviceIdType.MESH
NEG = -1.0e30
F32 = jnp.float32
BF = jnp.bfloat16
FACTOR = 128 ** (-0.5)
ROWS = 128
BOTH = 256
ZC = 16
FAR = 32

PQKV, PGRAD, POUT, PDQ = 0, 3, 4, 5
LOC, PAIR, YG, RS, AG = 6, 10, 18, 21, 54
STL, STP = 27, 28
R1, R2 = 30, 32
FA, FB, FMATE = 34, 36, 38
FQN, FQP, FRN, FRP, FIX, FBK = 39, 40, 42, 43, 45, 53
YF, FGM = 60, 63
NSEM = 64


def nt(a, b):
    return lax.dot_general(a, b, (((1,), (1,)), ((), ())), preferred_element_type=F32)


def nn(a, b):
    return jnp.dot(a, b, preferred_element_type=F32)


def exact(a, b):
    return lax.dot_general(
        a, b, (((1,), (0,)), ((), ())), precision=lax.Precision.HIGHEST, preferred_element_type=F32
    )


def iota(shape, dim):
    return lax.broadcasted_iota(jnp.int32, shape, dim)


def pick_far(x, off):
    rows = iota(x.shape, 0)
    kept = jnp.where((rows & (FAR - 1)) == off, x, 0.0)
    return jnp.sum(kept.reshape(BOTH // FAR, FAR, 128), axis=1)


def repeat_far(x):
    return jnp.broadcast_to(x[:, None, :], (BOTH // FAR, FAR, 128)).reshape(BOTH, 128)


def kernel(
    q_in, k_in, v_in, w_in, go_in, po, fo,
    lo, dq, dk, dv,
    q, k, v, w, go,
    QC, KC, VC, GC, LB, PB, PSND, GOA, GOUT,
    MR, LR, ACC, DQ, DK, DV, STR, STPS, LSR, PSR,
    FX, FY, FS, FS2, FG, FG2, R1S, R2S, FR1, FR2,
    GFS, GFR, DX, DY, FQNB, FQPB, FRNB, FRPB, FOUT, FM, FL, FACC, FST, CS, CB,
    OB, ORC, RSS, RSR, AGS, AGR, DSND, DRCV, GR, FRM,
    ss, rs, ls,
):
    t = lax.axis_index("seq")
    y = lax.axis_index("head")
    c = t % 2
    chip = t // 2
    odd = chip % 2
    g = chip % 4
    zz = chip % ZC
    upper = g // 2
    mate = t + 1 - 2 * c
    near = chip + 1 - 2 * odd
    other = chip - g + 2 - 2 * upper
    nchip = lax.axis_size("seq") // 2
    hub_turn = (chip // ZC) % 2
    hub_z = 0
    is_hub = jnp.logical_and(chip % ZC == hub_z, (chip // ZC) // 2 == c)

    def hub_chip(i):
        return ZC * (2 * c + i)

    def rc(src, dst, i, j, dev):
        return pltpu.make_async_remote_copy(
            src_ref=src, dst_ref=dst, send_sem=ss.at[i], recv_sem=rs.at[j],
            device_id=dev, device_id_type=MESH,
        )

    loads = [
        pltpu.make_async_copy(a, b, ls.at[n])
        for n, (a, b) in enumerate(((k_in, k), (v_in, v), (q_in, q), (go_in, go), (w_in, w)))
    ]
    for x in loads[:4]:
        x.start()

    bar = pltpu.get_barrier_semaphore()

    def sig(dev):
        pl.semaphore_signal(bar, inc=1, device_id=dev, device_id_type=MESH)

    def from_near(b, n):
        step = (n + 1) // 2
        return ZC * b + (hub_z + jnp.where(n % 2 == 1, ZC - step, step)) % ZC

    @pl.when(is_hub)
    def _():
        @pl.loop(0, nchip)
        def _(n):
            u = from_near(n // ZC, n % ZC)

            @pl.when(u != chip)
            def _():
                sig((2 * u + c, y))

    for d in range(1, 4):
        sig((t, (y + d) % 4))
    sig((mate, y))
    for s in range(2):
        sig((2 * near + s, y))
        for d in range(2):
            sig((2 * (other + d) + s, y))

    off_p = [po[4 * y + 2 * c + i] for i in range(2)]
    off_f = [fo[4 * y + 2 * c + i] for i in range(2)]
    lane = pl.ds(pl.multiple_of(256 * c, 256), 256)
    mine = pl.ds(pl.multiple_of(ROWS * c, ROWS), ROWS)
    theirs = pl.ds(pl.multiple_of(ROWS * (1 - c), ROWS), ROWS)
    mate_lane = pl.ds(pl.multiple_of(256 * (1 - c), 256), 256)

    def one_hot(off):
        return jnp.where(
            iota((64, ROWS), 1) == 2 * iota((64, ROWS), 0) + off, 1.0, 0.0
        ).astype(BF)

    def pair_rows(src, slot):
        for h in range(4):
            e = one_hot(po[4 * y + h])
            cols = slice(128 * h, 128 * h + 128)
            PSND[slot, :, cols] = nn(e, src[:, cols]).astype(BF)

    for x in loads[:3]:
        x.wait()
    loads[4].start()
    own_rows = (iota((8, 128), 0) // 4) == c
    for h in range(4):
        for n, src in enumerate((q, k, v)):
            x = src[:, 128 * h : 128 * h + 128].astype(F32)
            x = jnp.where((iota((ROWS, 128), 0) & (FAR - 1)) == fo[4 * y + h], x, 0.0)
            x = jnp.sum(x.reshape(4, FAR, 128), axis=1)
            x = jnp.where(own_rows, jnp.concatenate([x, x], axis=0), 0.0)
            FX[h // 2, h % 2, n] = x.astype(BF)

    @pl.when(upper == 0)
    def _():
        pair_rows(k, 0)
        pair_rows(v, 1)

    @pl.when(upper == 1)
    def _():
        pair_rows(q, 0)

    for src, dst in ((q, QC), (k, KC), (v, VC)):
        dst[mine, :] = jnp.where(c == 0, src[:, 0:256], src[:, 256:512])

    loads[3].wait()
    for d in range(4):
        to = (y + d) % 4
        r16 = iota((16, ROWS), 0)
        at = jnp.zeros((16, ROWS), jnp.int32)
        for h in range(4):
            at = jnp.where(r16 // 4 == h, fo[4 * to + h], at)
        e = jnp.where(iota((16, ROWS), 1) == FAR * (r16 & 3) + at, 1.0, 0.0).astype(BF)
        GFS[to] = nn(e, go[...]).astype(BF)

    count = 3 + 1 + 2 + 4
    for i in range(2):
        count = count + jnp.where(chip != hub_chip(i), 1, 0)
    pl.semaphore_wait(bar, count)

    def far_mate():
        return rc(FX.at[1 - c], FY, FMATE, FMATE, (mate, y))

    far_mate().start()
    mate_copies = [
        rc(src.at[:, mate_lane], dst.at[mine, :], PQKV + n, PQKV + n, (mate, y))
        for n, (src, dst) in enumerate(((q, QC), (k, KC), (v, VC)))
    ]
    for x in mate_copies:
        x.start()

    def y_copy(d):
        return rc(go, GOA.at[y], YG + d - 1, YG + d - 1, (t, (y + d) % 4))

    def y_far(d):
        return rc(GFS.at[(y + d) % 4], GFR.at[y], YF + d - 1, YF + d - 1, (t, (y + d) % 4))

    for d in (2, 1, 3):
        y_far(d).start()
    for d in (2, 1, 3):
        y_copy(d).start()

    def local_copy(src, n, s):
        return rc(
            src.at[:, 256 * s : 256 * s + 256], LB.at[n, mine, :],
            LOC + 2 * n + s, LOC + 2 * n + c, (2 * near + s, y),
        )

    def pair_copy(n, d, s):
        at = pl.ds(pl.multiple_of(128 * odd + 64 * c, 64), 64)
        return rc(
            PSND.at[n, :, 256 * s : 256 * s + 256], PB.at[n, at, :],
            PAIR + 4 * n + 2 * d + s, PAIR + 4 * n + 2 * odd + c, (2 * (other + d) + s, y),
        )

    far_at = pl.ds(pl.multiple_of(8 * chip, 8), 8)
    far_mate().wait_recv()
    for i in range(2):
        FS[i] = FX[c, i] + FY[i]

    def far_copy(i):
        return rc(FS.at[i], FG.at[:, far_at, :], FA + i, FA, (2 * hub_chip(i) + c, y))

    def far_copy2(i):
        return rc(FS2.at[i], FG2.at[:, far_at, :], FB + i, FB, (2 * hub_chip(i) + c, y))

    for i in range(2):
        @pl.when(chip != hub_chip(i))
        def _(i=i):
            far_copy(i).start()

        @pl.when(chip == hub_chip(i))
        def _(i=i):
            FG[:, far_at, :] = FS[i]

    def ask_near():
        return rc(FS.at[:, 0], FQNB, FQN, FQN, (2 * near + c, y))

    def ask_pair(d):
        return rc(FS.at[:, 0], FQPB.at[odd], FQP + d, FQP + odd, (2 * (other + d) + c, y))

    def tell_near():
        return rc(FOUT.at[2], FRNB, FRN, FRN, (2 * near + c, y))

    def tell_pair(d):
        return rc(FOUT.at[d], FRPB.at[odd], FRP + d, FRP + odd, (2 * (other + d) + c, y))

    @pl.when(odd == 1)
    def _():
        ask_near().start()

    @pl.when(upper == 1)
    def _():
        for d in range(2):
            ask_pair(d).start()

    for s in range(2):
        @pl.when(odd == 0)
        def _(s=s):
            local_copy(k, 0, s).start()

        @pl.when(odd == 1)
        def _(s=s):
            local_copy(q, 0, s).start()

    for d in range(2):
        for s in range(2):
            @pl.when(jnp.logical_or(upper == 1, odd == 1))
            def _(d=d, s=s):
                pair_copy(0, d, s).start()

    for x in mate_copies:
        x.wait_recv()

    def answer(slot, i, qq, near_row):
        cols = slice(128 * i, 128 * i + 128)
        match = jnp.logical_and((iota((8, BOTH), 1) & 1) == off_p[i], ((off_f[i] - off_p[i]) & 1) == 0)
        cnt = jnp.where(match, 1.0, 0.0) + near_row
        s = nt(qq, KC[:, cols]) * FACTOR
        s = jnp.where(cnt > 0.0, s, NEG)
        m = jnp.max(s, axis=1, keepdims=True)
        p = cnt * jnp.exp(s - m)
        FOUT[slot, i, 0] = nn(p.astype(BF), VC[:, cols])
        total = jnp.sum(p, axis=1, keepdims=True)
        FOUT[slot, i, 1] = jnp.where(iota((8, 128), 1) == 0, m, total)

    @pl.when(upper == 0)
    def _():
        for d in range(2):
            rc(FS.at[:, 0], FQPB.at[d], FQP, FQP + d, (2 * (other + d) + c, y)).wait_recv()
            for i in range(2):
                answer(d, i, FQPB[d, i], 0.0)
            tell_pair(d).start()

    @pl.when(odd == 0)
    def _():
        ask_near().wait_recv()
        for i in range(2):
            answer(2, i, FQNB[i], 1.0)
        tell_near().start()
        for s in range(2):
            local_copy(v, 1, s).start()

    @pl.when(upper == 0)
    def _():
        for d in range(2):
            for s in range(2):
                @pl.when(jnp.logical_and(odd == 0, zz != 8))
                def _(d=d, s=s):
                    pair_copy(0, d, s).start()

                @pl.when(jnp.logical_or(odd == 1, zz != 8))
                def _(d=d, s=s):
                    pair_copy(1, d, s).start()

    for i in range(2):
        cols = slice(128 * i, 128 * i + 128)
        at, to = iota((8, BOTH), 1), FAR * iota((8, BOTH), 0) + off_f[i]
        match = jnp.logical_and((at & 1) == off_p[i], (to & 1) == off_p[i])
        cnt = jnp.where(at <= to, jnp.where(match, 2.0, 1.0), 0.0)
        s = jnp.where(cnt > 0.0, nt(FS[i, 0], KC[:, cols]) * FACTOR, NEG)
        m = jnp.max(s, axis=1, keepdims=True)
        p = cnt * jnp.exp(s - m)
        FACC[i] = nn(p.astype(BF), VC[:, cols])
        FL[i] = jnp.broadcast_to(jnp.sum(p, axis=1, keepdims=True), (8, 128))
        FM[i] = jnp.broadcast_to(m, (8, 128))

    loads[4].wait()
    part = nt(GFS[y], w[:, pl.ds(pl.multiple_of(512 * y, 512), 512)])
    for d in (1, 3, 2):
        src = (y + 4 - d) % 4
        rc(GFS.at[0], GFR.at[src], YF + d - 1, YF + d - 1, (t, src)).wait_recv()
        part = part + nt(GFR[src], w[:, pl.ds(pl.multiple_of(512 * src, 512), 512)])
    for h in range(4):
        x = part[4 * h : 4 * h + 4, 128 * h : 128 * h + 128]
        x = jnp.where(own_rows, jnp.concatenate([x, x], axis=0), 0.0)
        DX[h // 2, h % 2] = x.astype(BF)

    def far_grad_mate():
        return rc(DX.at[1 - c], DY, FGM, FGM, (mate, y))

    far_grad_mate().start()

    ri = iota((BOTH, BOTH), 0)
    ci = iota((BOTH, BOTH), 1)

    def own_count(i):
        both = jnp.logical_and((ri & 1) == off_p[i], (ci & 1) == off_p[i])
        return jnp.where(both, 2.0, 1.0)

    def fwd(i, kk, vv, cnt, first=False):
        cols = slice(128 * i, 128 * i + 128)
        s = nt(QC[:, cols], kk) * FACTOR
        s = jnp.where(cnt > 0.0, s, NEG)
        top = jnp.max(s, axis=1, keepdims=True)
        if first:
            m = top
        else:
            m_old = MR[i][:, 0:1]
            m = jnp.maximum(m_old, top)
        p = cnt * jnp.exp(s - m)
        total = jnp.sum(p, axis=1, keepdims=True)
        num = nn(p.astype(BF), vv)
        if not first:
            a = jnp.exp(m_old - m)
            total = total + a * LR[i][:, 0:1]
            num = num + a * ACC[i]
        MR[i] = jnp.broadcast_to(m, (BOTH, 128))
        LR[i] = jnp.broadcast_to(total, (BOTH, 128))
        ACC[i] = num

    for i in range(2):
        cols = slice(128 * i, 128 * i + 128)
        fwd(i, KC[:, cols], VC[:, cols], jnp.where(ri >= ci, own_count(i), 0.0), True)

    def join(i, got):
        m_o = FM[i][:, 0:1]
        m_g = got[1][:, 0:1]
        m = jnp.maximum(m_o, m_g)
        a = jnp.exp(m_o - m)
        e = jnp.exp(m_g - m)
        FACC[i] = a * FACC[i] + e * got[0]
        FL[i] = jnp.broadcast_to(a * FL[i][:, 0:1] + e * got[1][:, 1:2], (8, 128))
        FM[i] = jnp.broadcast_to(m, (8, 128))

    @pl.when(odd == 1)
    def _():
        tell_near().wait_recv()
        for i in range(2):
            join(i, FRNB[i])

    @pl.when(upper == 1)
    def _():
        for d in range(2):
            rc(FOUT.at[d], FRPB.at[d], FRP, FRP + d, (2 * (other + d) + c, y)).wait_recv()
            for i in range(2):
                join(i, FRPB[d, i])

    far_grad_mate().wait_recv()
    l8 = iota((8, 128), 1)
    for i in range(2):
        gf = DX[c, i].astype(F32) + DY[i].astype(F32)
        dn = jnp.sum(gf * FACC[i], axis=1, keepdims=True)
        FS2[i, 0] = gf
        FS2[i, 1] = jnp.where(l8 == 0, FM[i], jnp.where(l8 == 1, FL[i], dn))

    for i in range(2):
        @pl.when(chip != hub_chip(i))
        def _(i=i):
            far_copy2(i).start()

        @pl.when(chip == hub_chip(i))
        def _(i=i):
            FG2[:, far_at, :] = FS2[i]

    grad = nt(go[...], w[:, pl.ds(pl.multiple_of(512 * y, 512), 512)])
    for d in (1, 3, 2):
        src = (y + 4 - d) % 4
        rc(go, GOA.at[src], YG + d - 1, YG + d - 1, (t, src)).wait_recv()
        grad = grad + nt(GOA[src], w[:, pl.ds(pl.multiple_of(512 * src, 512), 512)])
    GOUT[...] = grad.astype(BF)
    GC[mine, :] = jnp.where(c == 0, GOUT[:, 0:256], GOUT[:, 256:512])

    @pl.when(upper == 1)
    def _():
        pair_rows(GOUT, 1)

    grad_mate = rc(GOUT.at[:, mate_lane], GC.at[mine, :], PGRAD, PGRAD, (mate, y))
    grad_mate.start()

    @pl.when(odd == 1)
    def _():
        for s in range(2):
            local_copy(GOUT, 1, s).start()

    @pl.when(zz == 8)
    def _():
        for d in range(2):
            for s in range(2):
                pair_copy(0, d, s).start()

    @pl.when(jnp.logical_or(upper == 1, zz == 8))
    def _():
        for d in range(2):
            for s in range(2):
                pair_copy(1, d, s).start()

    @pl.when(odd == 1)
    def _():
        for n in range(2):
            for s in range(2):
                rc(
                    k.at[:, 0:256], LB.at[n, pl.ds(128 * s, 128), :],
                    LOC + 2 * n, LOC + 2 * n + s, (2 * near + s, y),
                ).wait_recv()
        for i in range(2):
            cols = slice(128 * i, 128 * i + 128)
            fwd(i, LB[0, :, cols], LB[1, :, cols], own_count(i))

    def pair_wait(n, d, s):
        rc(
            PSND.at[n, :, 0:256], PB.at[n, pl.ds(128 * d + 64 * s, 64), :],
            PAIR, PAIR + 4 * n + 2 * d + s, (2 * (other + d) + s, y),
        ).wait_recv()

    def pair_key_count(i, x):
        return jnp.where((x & 1) == off_p[i], 1.0, 0.0)

    @pl.when(upper == 1)
    def _():
        for n in range(2):
            for d in range(2):
                for s in range(2):
                    pair_wait(n, d, s)
        for i in range(2):
            cols = slice(128 * i, 128 * i + 128)
            fwd(i, PB[0, :, cols], PB[1, :, cols], pair_key_count(i, ri))

    for i in range(2):
        OB[:, 128 * i : 128 * i + 128] = (ACC[i] / LR[i]).astype(BF)
    out_mate = rc(OB.at[theirs, :], ORC, POUT, POUT, (mate, y))
    out_mate.start()
    out_mate.wait_recv()
    attended = jnp.where(
        c == 0,
        jnp.concatenate([OB[mine, :], ORC[...]], axis=1),
        jnp.concatenate([ORC[...], OB[mine, :]], axis=1),
    )

    def rs_copy(d, half):
        to = (y + d) % 4
        at = slice(256 * half, 256 * half + 256)
        n = RS + 3 * half + d - 1
        return rc(RSS.at[to, :, at], RSR.at[d - 1, :, at], n, n, (t, to))

    def lanes_of(to, half):
        return pl.ds(pl.multiple_of(512 * to + 256 * half, 256), 256)

    own_parts = []
    for half in range(2):
        for d in (2, 1, 3):
            to = (y + d) % 4
            RSS[to, :, 256 * half : 256 * half + 256] = nn(attended, w[:, lanes_of(to, half)]).astype(BF)
            rs_copy(d, half).start()
        own_parts.append(nn(attended, w[:, lanes_of(y, half)]).astype(BF).astype(F32))

    @pl.when(is_hub)
    def _():
        rest = FG.at[:, pl.ds(0, 8 * (nchip - 1)), :]
        rc(rest, rest, FA, FA, (t, y)).wait_recv()
        lanes = iota((128, 128), 1)
        for b in range(nchip // ZC):
            at, size = slice(128 * b, 128 * b + 128), 128 * b + 128
            s = nt(FG[0, at, :], FG[1, 0:size, :]) * FACTOR
            s = jnp.where(iota((128, size), 0) + 128 * b >= iota((128, size), 1), s, NEG)
            m = jnp.max(s, axis=1, keepdims=True)
            p = jnp.exp(s - m)
            total = jnp.sum(p, axis=1, keepdims=True)
            R1S[0, at, :] = nn(p.astype(BF), FG[2, 0:size, :])
            R1S[1, at, :] = jnp.where(lanes == 0, m, total)

            def send(u):
                at = pl.ds(pl.multiple_of(8 * u, 8), 8)
                rc(R1S.at[:, at, :], FR1.at[hub_turn], R1, R1 + hub_turn, (2 * u + c, y)).start()

            @pl.when(ZC * b != chip)
            def _(b=b, send=send):
                send(ZC * b)

            @pl.loop(0, 5)
            def _(k, b=b, send=send):
                for j in range(3):
                    send(from_near(b, 3 * k + j + 1))

        FR1[hub_turn] = R1S[:, far_at, :]

    grad_mate.wait_recv()
    l128 = iota((BOTH, 128), 1)
    stats = jnp.zeros((BOTH, 128), F32)
    for i in range(2):
        cols = slice(128 * i, 128 * i + 128)

        @pl.when(chip != hub_chip(i))
        def _(i=i):
            rc(R1S.at[:, 0:8, :], FR1.at[i], R1, R1 + i, (2 * hub_chip(i) + c, y)).wait_recv()

        is_far = (iota((BOTH, 1), 0) & (FAR - 1)) == off_f[i]
        num_f = repeat_far(FR1[i, 0])
        st_f = repeat_far(FR1[i, 1])
        m_f = jnp.where(is_far, st_f[:, 0:1], NEG)
        l_f = jnp.where(is_far, st_f[:, 1:2], 0.0)
        m_n = MR[i][:, 0:1]
        m = jnp.maximum(m_n, m_f)
        a = jnp.exp(m_n - m)
        b = jnp.where(is_far, jnp.exp(m_f - m), 0.0)
        total = a * LR[i][:, 0:1] + b * l_f
        out = (a * ACC[i] + b * num_f) / total
        FST[i] = pick_far(out - OB[:, cols].astype(F32), off_f[i])
        lse = m + jnp.log(total)
        delta = jnp.sum(GC[:, cols].astype(F32) * out, axis=1, keepdims=True)
        MR[i] = jnp.broadcast_to(lse, (BOTH, 128))
        LR[i] = jnp.broadcast_to(delta, (BOTH, 128))
        stats = jnp.where(l128 == 2 * i, lse, jnp.where(l128 == 2 * i + 1, delta, stats))

    STR[...] = jnp.transpose(stats)[0:8, :]

    @pl.when(upper == 1)
    def _():
        srow = iota((8, 128), 0)
        parts = []
        for i in range(2):
            e = jnp.where(iota((BOTH, 128), 0) == 2 * iota((BOTH, 128), 1) + off_p[i], 1.0, 0.0)
            parts.append(exact(STR[...], e))
        STPS[...] = jnp.where(srow < 2, parts[0], parts[1])

    def near_stats():
        return rc(STR, LSR, STL, STL, (2 * near + c, y))

    def pair_stats(d):
        at = pl.ds(pl.multiple_of(128 * odd, 128), 128)
        return rc(STPS, PSR.at[:, at], STP + d, STP + odd, (2 * (other + d) + c, y))

    @pl.when(odd == 1)
    def _():
        near_stats().start()

    @pl.when(upper == 1)
    def _():
        for d in range(2):
            pair_stats(d).start()

    fixes = [
        nn(FST[i].astype(BF), w[pl.ds(pl.multiple_of(256 * c + 128 * i, 128), 128), :]) for i in range(2)
    ]
    fix_at = pl.ds(pl.multiple_of(8 * (2 * y + c), 8), 8)
    for s in range(2):
        CS[s] = jnp.concatenate([x[4 * s : 4 * s + 4, :] for x in fixes], axis=0).astype(BF)

    def fix_copy(d, s):
        return rc(
            CS.at[s], CB.at[fix_at, :], FIX + 2 * d + s, FIX + 2 * y + c,
            (2 * chip + s, (y + d) % 4),
        )

    for d in (2, 1, 3):
        for s in range(2):
            fix_copy(d, s).start()
    for s in range(2):
        @pl.when(c == s)
        def _(s=s):
            fix_copy(0, 1 - s).start()
            CB[fix_at, :] = CS[s]

    def ag_copy(d, half):
        at = slice(256 * half, 256 * half + 256)
        n = AG + 3 * half + d - 1
        return rc(AGS.at[:, at], AGR.at[d - 1, :, at], n, n, (t, (y + d) % 4))

    for half in range(2):
        at = slice(256 * half, 256 * half + 256)
        acc = own_parts[half]
        for d in (1, 3, 2):
            rs_copy(d, half).wait_recv()
            acc = acc + RSR[d - 1, :, at].astype(F32)
        AGS[:, at] = acc.astype(BF)
        for d in (2, 1, 3):
            ag_copy(d, half).start()

    def row_side(i, kk, vv, cnt, masked):
        cols = slice(128 * i, 128 * i + 128)
        s = nt(QC[:, cols], kk) * FACTOR
        if masked:
            s = jnp.where(cnt > 0.0, s, NEG)
        p = cnt * jnp.exp(s - MR[i][:, 0:1])
        ds = (p * (nt(GC[:, cols], vv) - LR[i][:, 0:1])).astype(BF)
        return nn(ds, kk)

    def col_side(i, qq, gg, st, cnt, masked):
        cols = slice(128 * i, 128 * i + 128)
        s = nt(KC[:, cols], qq) * FACTOR
        if masked:
            s = jnp.where(cnt > 0.0, s, NEG)
        p = cnt * jnp.exp(s - st[2 * i : 2 * i + 1, :])
        ds = (p * (nt(VC[:, cols], gg) - st[2 * i + 1 : 2 * i + 2, :])).astype(BF)
        return nn(ds, qq), nn(p.astype(BF), gg)

    for i in range(2):
        cols = slice(128 * i, 128 * i + 128)
        DQ[i] = row_side(i, KC[:, cols], VC[:, cols], jnp.where(ri >= ci, own_count(i), 0.0), True)
        DK[i], DV[i] = col_side(
            i, QC[:, cols], GC[:, cols], STR[...], jnp.where(ci >= ri, own_count(i), 0.0), True
        )

    def hub_backward():
        rest = FG2.at[:, pl.ds(0, 8 * (nchip - 1)), :]
        rc(rest, rest, FB, FB, (t, y)).wait_recv()
        rows = []
        lanes = iota((128, 128), 1)
        for b in range(nchip // ZC):
            at = slice(128 * b, 128 * b + 128)
            m_f = R1S[1, at, 0:1]
            l_f = R1S[1, at, 1:2]
            m_n = FG2[1, at, 0:1]
            l_n = FG2[1, at, 1:2]
            d_n = FG2[1, at, 2:3]
            m = jnp.maximum(m_f, m_n)
            a = jnp.exp(m_n - m)
            e = jnp.exp(m_f - m)
            total = a * l_n + e * l_f
            lse = m + jnp.log(total)
            d_f = jnp.sum(FG2[0, at, :] * R1S[0, at, :], axis=1, keepdims=True)
            delta = (a * d_n + e * d_f) / total
            both = jnp.where(lanes == 0, lse, delta)
            FG2[1, at, :] = both
            rows.append(jnp.transpose(both))
        rows = jnp.concatenate([x[0:8, :] for x in rows], axis=1)
        size = FG.shape[1]
        for b in range(nchip // ZC):
            at, end = slice(128 * b, 128 * b + 128), 128 * b + 128
            past, ahead = slice(0, end), slice(128 * b, size)
            lse = FG2[1, at, 0:1]
            delta = FG2[1, at, 1:2]
            lower = iota((128, end), 0) + 128 * b >= iota((128, end), 1)
            s = jnp.where(lower, nt(FG[0, at, :], FG[1, past, :]) * FACTOR, NEG)
            p = jnp.exp(s - lse)
            ds = (p * (nt(FG2[0, at, :].astype(BF), FG[2, past, :]) - delta)).astype(BF)
            R2S[0, at, :] = (nn(ds, FG[1, past, :]) * FACTOR).astype(BF)
            later = iota((128, size - 128 * b), 1) >= iota((128, size - 128 * b), 0)
            s = jnp.where(later, nt(FG[1, at, :], FG[0, ahead, :]) * FACTOR, NEG)
            p = jnp.exp(s - rows[0:1, ahead])
            gb = FG2[0, ahead, :].astype(BF)
            R2S[2, at, :] = nn(p.astype(BF), gb).astype(BF)
            ds = (p * (nt(FG[2, at, :], gb) - rows[1:2, ahead])).astype(BF)
            R2S[1, at, :] = (nn(ds, FG[0, ahead, :]) * FACTOR).astype(BF)

        def send(u):
            at = pl.ds(pl.multiple_of(8 * u, 8), 8)
            rc(R2S.at[:, at, :], FR2.at[hub_turn], R2, R2 + hub_turn, (2 * u + c, y)).start()

        for b in range(4):
            @pl.when(ZC * b != chip)
            def _(b=b):
                send(ZC * b)

        @pl.loop(1, ZC)
        def _(n):
            for b in range(4):
                send(from_near(b, n))

        FR2[hub_turn] = R2S[:, far_at, :]

    pl.when(jnp.logical_and(is_hub, chip != 0))(hub_backward)

    @pl.when(odd == 1)
    def _():
        for i in range(2):
            cols = slice(128 * i, 128 * i + 128)
            DQ[i] += row_side(i, LB[0, :, cols], LB[1, :, cols], own_count(i), False)

    @pl.when(odd == 0)
    def _():
        for n in range(2):
            for s in range(2):
                rc(
                    k.at[:, 0:256], LB.at[n, pl.ds(128 * s, 128), :],
                    LOC + 2 * n, LOC + 2 * n + s, (2 * near + s, y),
                ).wait_recv()
        near_stats().wait_recv()
        for i in range(2):
            cols = slice(128 * i, 128 * i + 128)
            a, b = col_side(i, LB[0, :, cols], LB[1, :, cols], LSR[...], own_count(i), False)
            DK[i] += a
            DV[i] += b

    @pl.when(upper == 1)
    def _():
        for i in range(2):
            cols = slice(128 * i, 128 * i + 128)
            DQ[i] += row_side(i, PB[0, :, cols], PB[1, :, cols], pair_key_count(i, ri), True)

    @pl.when(upper == 0)
    def _():
        for n in range(2):
            for d in range(2):
                for s in range(2):
                    pair_wait(n, d, s)
        for d in range(2):
            rc(
                STPS, PSR.at[:, 128 * d : 128 * d + 128], STP, STP + d, (2 * (other + d) + c, y)
            ).wait_recv()
        for i in range(2):
            cols = slice(128 * i, 128 * i + 128)
            a, b = col_side(
                i, PB[0, :, cols], PB[1, :, cols], PSR[...], pair_key_count(i, ri), True
            )
            DK[i] += a
            DV[i] += b

    for n, (src, scale) in enumerate(((DQ, FACTOR), (DK, FACTOR), (DV, 1.0))):
        full = jnp.concatenate([src[i] * scale for i in range(2)], axis=1)
        DSND[n] = jnp.where(c == 0, full[ROWS:, :], full[:ROWS, :]).astype(BF)
        GR[n] = jnp.where(c == 0, full[:ROWS, :], full[ROWS:, :])
    back = rc(DSND, DRCV, PDQ, PDQ, (mate, y))
    back.start()

    pl.when(jnp.logical_and(is_hub, chip == 0))(hub_backward)

    for i in range(2):
        @pl.when(chip != hub_chip(i))
        def _(i=i):
            rc(R2S.at[:, 0:8, :], FR2.at[i], R2, R2 + i, (2 * hub_chip(i) + c, y)).wait_recv()

    back_far = rc(FR2, FRM, FBK, FBK, (mate, y))
    back_far.start()

    def far_rows(tiles, n, cc):
        parts = []
        for i in range(2):
            x = tiles[i, n].astype(F32)
            x = jnp.where(c == 0, x[0:4, :], x[4:8, :])
            x = jnp.broadcast_to(x[:, None, :], (4, FAR, 128)).reshape(ROWS, 128)
            hit = (iota((ROWS, 128), 0) & (FAR - 1)) == fo[4 * y + 2 * cc + i]
            parts.append(jnp.where(hit, x, 0.0))
        return jnp.concatenate(parts, axis=1)

    for n, dst in enumerate((dq, dk, dv)):
        dst[:, lane] = (GR[n] + far_rows(FR2, n, c)).astype(BF)
    for d in range(4):
        for s in range(2):
            @pl.when(jnp.logical_or(d > 0, s != c))
            def _(d=d, s=s):
                src = (y + 4 - d) % 4
                rc(
                    CS.at[0], CB.at[pl.ds(pl.multiple_of(8 * (2 * src + s), 8), 8), :],
                    FIX, FIX + 2 * src + s, (2 * chip + s, src),
                ).wait_recv()
    kk = iota((ROWS, 64), 1)
    place = jnp.zeros((ROWS, 64), jnp.int32)
    for h in range(16):
        place = jnp.where(kk // 4 == h, fo[h], place)
    place = jnp.where(iota((ROWS, 64), 0) == FAR * (kk & 3) + place, 1.0, 0.0).astype(BF)

    def whole(base, at):
        lo[:, at] = (base.astype(F32) + nn(place, CB[:, at])).astype(BF)

    whole(AGS[...], pl.ds(pl.multiple_of(512 * y, 512), 512))
    for d in (1, 3, 2):
        ag_copy(d, 0).wait_recv()
        ag_copy(d, 1).wait_recv()
        src = (y + 4 - d) % 4
        whole(AGR[d - 1], pl.ds(pl.multiple_of(512 * src, 512), 512))

    back.wait_recv()
    back_far.wait_recv()
    for n, dst in enumerate((dq, dk, dv)):
        dst[:, mate_lane] = (DRCV[n].astype(F32) + far_rows(FRM, n, 1 - c)).astype(BF)

    far_mate().wait_send()
    far_grad_mate().wait_send()
    for x in mate_copies:
        x.wait_send()
    for d in range(1, 4):
        y_copy(d).wait_send()
        y_far(d).wait_send()
        for half in range(2):
            rs_copy(d, half).wait_send()
            ag_copy(d, half).wait_send()
    for n in range(2):
        for s in range(2):
            local_copy(k, n, s).wait_send()
            for d in range(2):
                pair_copy(n, d, s).wait_send()
    grad_mate.wait_send()
    out_mate.wait_send()
    back.wait_send()
    back_far.wait_send()
    for i in range(2):
        @pl.when(chip != hub_chip(i))
        def _(i=i):
            far_copy(i).wait_send()
            far_copy2(i).wait_send()

    @pl.when(odd == 1)
    def _():
        near_stats().wait_send()
        ask_near().wait_send()

    @pl.when(odd == 0)
    def _():
        tell_near().wait_send()

    @pl.when(upper == 0)
    def _():
        for d in range(2):
            tell_pair(d).wait_send()

    @pl.when(upper == 1)
    def _():
        for d in range(2):
            pair_stats(d).wait_send()
            ask_pair(d).wait_send()

    for d in range(1, 4):
        for s in range(2):
            fix_copy(d, s).wait_send()
    for s in range(2):
        @pl.when(c == s)
        def _(s=s):
            fix_copy(0, 1 - s).wait_send()

    @pl.when(is_hub)
    def _():
        for sent, n in ((R1S, R1), (R2S, R2)):
            sent = sent.at[:, pl.ds(0, 8 * (nchip - 1)), :]
            rc(sent, sent, n, n, (t, y)).wait_send()


def store(*refs):
    copies = [
        pltpu.make_async_copy(a, b, refs[8].at[n]) for n, (a, b) in enumerate(zip(refs[:4], refs[4:8]))
    ]
    for x in copies:
        x.start()
    for x in copies:
        x.wait()


def local(queries, key_rows, value_rows, out_weight, grad_out, pair_offsets, far_head_offsets):
    vm = pl.BlockSpec(memory_space=pltpu.VMEM)
    sm = pl.BlockSpec(memory_space=pltpu.SMEM)
    rows = jax.ShapeDtypeStruct((ROWS, 512), BF)

    def b(*shape):
        return pltpu.VMEM(shape, BF)

    def f(*shape):
        return pltpu.VMEM(shape, F32)

    outs = pl.pallas_call(
        kernel,
        out_shape=(pltpu.VMEM((ROWS, 2048), BF),) + (pltpu.VMEM((ROWS, 512), BF),) * 3,
        in_specs=[pl.BlockSpec(memory_space=pl.ANY)] * 5 + [sm] * 2,
        out_specs=(vm,) * 4,
        scratch_shapes=[
            b(128, 512), b(128, 512), b(128, 512), b(512, 2048), b(128, 512),
            b(256, 256), b(256, 256), b(256, 256), b(256, 256),
            b(2, 256, 256), b(2, 256, 256), b(2, 64, 512), b(4, 128, 512), b(128, 512),
            f(2, 256, 128), f(2, 256, 128), f(2, 256, 128),
            f(2, 256, 128), f(2, 256, 128), f(2, 256, 128),
            f(8, 256), f(8, 128), f(8, 256), f(8, 256),
            b(2, 2, 3, 8, 128), b(2, 3, 8, 128),
            b(2, 3, 8, 128), f(2, 2, 8, 128), b(3, 512, 128), f(2, 512, 128),
            f(2, 512, 128), b(3, 512, 128), f(2, 2, 8, 128), b(2, 3, 8, 128),
            b(4, 16, 512), b(4, 16, 512), b(2, 2, 8, 128), b(2, 8, 128),
            b(2, 8, 128), b(2, 2, 8, 128), f(2, 2, 8, 128), f(2, 2, 2, 8, 128), f(3, 2, 2, 8, 128),
            f(2, 8, 128), f(2, 8, 128), f(2, 8, 128), f(2, 8, 128),
            b(2, 8, 2048), b(64, 2048),
            b(256, 256), b(128, 256), b(4, 128, 512), b(3, 128, 512),
            b(128, 512), b(3, 128, 512), b(3, 128, 256), b(3, 128, 256), f(3, 128, 256), b(2, 3, 8, 128),
            pltpu.SemaphoreType.DMA((NSEM,)),
            pltpu.SemaphoreType.DMA((NSEM,)),
            pltpu.SemaphoreType.DMA((5,)),
        ],
        compiler_params=pltpu.CompilerParams(collective_id=0, has_side_effects=True),
    )(queries, key_rows, value_rows, out_weight, grad_out, pair_offsets, far_head_offsets)
    return pl.pallas_call(
        store,
        out_shape=(jax.ShapeDtypeStruct((ROWS, 2048), BF), rows, rows, rows),
        in_specs=[vm] * 4,
        out_specs=(pl.BlockSpec(memory_space=pl.ANY),) * 4,
        scratch_shapes=[pltpu.SemaphoreType.DMA((4,))],
    )(*[pltpu.with_memory_space_constraint(x, pltpu.VMEM) for x in outs])


def solution(mesh):
    seq = P("seq", "head")
    return jax.shard_map(
        local,
        mesh=mesh,
        in_specs=(seq, seq, seq, P("head", None), seq, P(), P()),
        out_specs=(P("seq", None), seq, seq, seq),
        check_vma=False,
    )
```
